256 devices in a mesh: gz: 64 (over x, z, core), gx: 4 (over y).
Axes of the slice: x: 4, y: 4, z: 8, core: 2. Of those that a mesh axis runs over, the one named last changes fastest.
Arguments:
- strength: float32 [3, 131072], P(None, ('gz', 'gx')), may hold values from -6 to 6
- offsets: float32 [3, 131072], P(None, ('gz', 'gx')), may hold values from -0.5 to 0.5
- cell_index: int32 [131072], P(('gz', 'gx')), may hold values from 0 to 131071
- migrate_count: int32 [64, 4, 2], P('gz', 'gx'), may hold values from 32 to 64, as said below
- ambient: float32 [3, 512, 256, 256], P(None, 'gz', 'gx'), may hold values from -2.5 to 2.5
Outputs:
- velocity: float32 [3, 512, 256, 256], P(None, 'gz', 'gx')
- vorticity: float32 [3, 512, 256, 256], P(None, 'gz', 'gx')
The draws below stay inside these ranges and needn't reach their ends.
Inputs may be any that keep to these rules, and one draw needn't show every extreme that they name: `migrate_count`: some device has 64 in the first entry and some device has 64 in the second.
All inputs are finite; a program needn't handle non-finite values.
Results may differ from the reference program's by a relative error of at most 0.0003.
Values sent between devices are 32-bit elements; how exact they have to be, the bound alone decides.
A program may use at most 128 MiB of HBM per device.

```python
import jax
import jax.numpy as jnp

NX = 256
NY = 256
CZ = 8
NZ = 512
CX = 64
PART = 512
MIG = 64
PTOTAL = 131072
N_GZ = 64
N_GX = 4


def draw_migrate_count(key, part):
    first, second = jax.random.split(key)
    owners = N_GZ * N_GX
    counts = jax.random.randint(first, (owners, 2), MIG // 2, MIG + 1)
    chosen = jax.random.randint(second, (2,), 0, owners)
    rows_at = jnp.arange(owners)[:, None]
    counts = jnp.where(rows_at == chosen[None, :], MIG, counts)
    return counts.reshape(N_GZ, N_GX, 2).astype(jnp.int32)


def draw_ambient(key, part):
    extent = (3, NZ, NX, NY)
    return jnp.clip(0.5 * jax.random.normal(key, extent, jnp.float32), -2.5, 2.5)


def touch_ends(array, own_key, least, high):
    longest = array.shape.index(max(array.shape))
    spots = []
    for shift in (0, 1):
        where = [jax.random.randint(jax.random.fold_in(own_key, axis), (), 0, length) for axis, length in enumerate(array.shape)]
        where[longest] = (where[longest] + shift) % array.shape[longest]
        spots.append(tuple(where))
    return array.at[spots[0]].set(least).at[spots[1]].set(high)


def levels(rng, dims, cuts, low, high):
    loudness, own = 1.0, jax.random.fold_in(rng, 6)
    for axis_at, blocks in cuts:
        heights = jnp.exp(jax.random.uniform(jax.random.fold_in(own, axis_at), (blocks,), jnp.float32, low / len(cuts), high / len(cuts)))
        loudness = loudness * jnp.repeat(heights, dims[axis_at] // blocks).reshape([-1 if axis == axis_at else 1 for axis in range(len(dims))])
    return loudness


def gaussian(key, shape, width, limit, cuts=(), kind=jnp.bfloat16):
    level = levels(key, shape, cuts, -0.22, 0.18) if cuts else 1.0
    entries = jax.random.normal(key, shape, jnp.float32) * width * level
    return jnp.minimum(jnp.maximum(entries, -limit), limit).astype(kind)


def setup_inputs(seed: int = 0) -> dict:
    streams_of = jax.random.split(jax.random.key(seed), 6)
    strength = gaussian(streams_of[0], (3, PTOTAL), 1.0, 6.0, ((1, 256),), jnp.float32)
    offsets = jnp.clip(jax.random.uniform(streams_of[1], (3, PTOTAL), jnp.float32, -0.5, 0.5) * levels(streams_of[1], (3, PTOTAL), ((1, 256),), -0.4, 0.0), -0.5, 0.5)
    cell_index = touch_ends(jax.random.randint(streams_of[2], (PTOTAL,), 0, CZ * CX * NY), jax.random.fold_in(streams_of[2], 1), 0, (CZ * CX * NY) - 1).astype(jnp.int32)
    migrate_count = draw_migrate_count(jax.random.fold_in(streams_of[5], 71), 0)
    ambient = draw_ambient(jax.random.fold_in(streams_of[5], 71), 0)
    return dict(strength=strength, offsets=offsets, cell_index=cell_index, migrate_count=migrate_count, ambient=ambient)


def kernel_weight(distance):
    radius = jnp.abs(distance)
    near_part = 1.0 - 2.5 * radius * radius + 1.5 * radius * radius * radius
    far_part = 0.5 * (2.0 - radius) * (2.0 - radius) * (1.0 - radius)
    return jnp.where(radius < 1.0, near_part, jnp.where(radius < 2.0, far_part, 0.0))


def wave_of(position, extent):
    signed = jnp.where(position < extent // 2, position, position - extent)
    return 2.0 * jnp.pi * signed.astype(jnp.float32) / extent


def central(values, axis_number):
    return (jnp.roll(values, -1, axis=axis_number) - jnp.roll(values, 1, axis=axis_number)) * 0.5


def reference(strength, offsets, cell_index, migrate_count, ambient):
    owners = N_GZ * N_GX
    slot_index = jnp.arange(PART, dtype=jnp.int32)[None, :]
    counts = migrate_count.reshape(owners, 2)
    up_count = counts[:, 0:1]
    down_count = counts[:, 1:2]
    moves = jnp.where(slot_index < up_count, 1, jnp.where(slot_index < up_count + down_count, -1, 0)).astype(jnp.int32)
    owner = jnp.arange(owners, dtype=jnp.int32)[:, None]
    slab = (owner // N_GX + moves) % N_GZ
    cell_ids = cell_index.reshape(owners, PART)
    z_cell = (slab * CZ + cell_ids // (CX * NY)).reshape(-1)
    x_cell = ((owner % N_GX) * CX + (cell_ids // NY) % CX).reshape(-1)
    y_cell = (cell_ids % NY).reshape(-1)
    taps = jnp.arange(5, dtype=jnp.int32) - 2
    tap_float = taps.astype(jnp.float32)
    weight_z = kernel_weight(tap_float[None, :] - offsets[0][:, None])
    weight_x = kernel_weight(tap_float[None, :] - offsets[1][:, None])
    weight_y = kernel_weight(tap_float[None, :] - offsets[2][:, None])
    values = (strength[:, :, None] * weight_z[None])[:, :, :, None] * weight_x[None, :, None, :]
    values = values[:, :, :, :, None] * weight_y[None, :, None, None, :]
    index_z = (z_cell[:, None] + taps[None, :]) % NZ
    index_x = (x_cell[:, None] + taps[None, :]) % NX
    index_y = (y_cell[:, None] + taps[None, :]) % NY
    flat = (index_z[:, :, None, None] * NX + index_x[:, None, :, None]) * NY + index_y[:, None, None, :]
    deposited = jnp.zeros((3, NZ * NX * NY), jnp.float32).at[:, flat.reshape(-1)].add(values.reshape(3, -1))
    vorticity_mesh = ambient + deposited.reshape(3, NZ, NX, NY)
    spectrum = jnp.fft.fftn(vorticity_mesh, axes=(1, 2, 3))
    z_index = jnp.arange(NZ, dtype=jnp.int32)[:, None, None]
    x_index = jnp.arange(NX, dtype=jnp.int32)[None, :, None]
    y_index = jnp.arange(NY, dtype=jnp.int32)[None, None, :]
    wave_z = wave_of(z_index, NZ)
    wave_x = wave_of(x_index, NX)
    wave_y = wave_of(y_index, NY)
    anchor = (z_index == 0) & (x_index == 0) & (y_index == 0)
    wave_sq = wave_z * wave_z + wave_x * wave_x + wave_y * wave_y
    inverse_sq = jnp.where(anchor, 0.0, 1.0 / jnp.where(anchor, 1.0, wave_sq))
    stream = spectrum * inverse_sq
    crossed = jnp.stack([wave_x * stream[2] - wave_y * stream[1],
                         wave_y * stream[0] - wave_z * stream[2],
                         wave_z * stream[1] - wave_x * stream[0]])
    velocity = jnp.real(jnp.fft.ifftn(1j * crossed, axes=(1, 2, 3))).astype(jnp.float32)
    stretch = vorticity_mesh[0] * central(velocity, 1) + vorticity_mesh[1] * central(velocity, 2) + vorticity_mesh[2] * central(velocity, 3)
    return velocity, vorticity_mesh + 0.25 * stretch
```

```python
import functools
import math

import jax
import jax.numpy as jnp
import ml_dtypes
import numpy as np
from jax import lax
from jax.experimental import pallas as pl
from jax.experimental.pallas import tpu as pltpu
from jax.sharding import PartitionSpec as P

MESH = pl.DeviceIdType.MESH
F32 = jnp.float32
BF16 = jnp.bfloat16
PENCILS = 4
MODES = 32
PLANES = 8
KXS = 4


def halves(table):
    high = table.astype(ml_dtypes.bfloat16)
    low = (table - high.astype(np.float64)).astype(ml_dtypes.bfloat16)
    return np.stack([high, low])


def real_form(angle):
    cosine, sine = np.cos(angle), np.sin(angle)
    return np.stack([np.stack([cosine, sine], -1), np.stack([-sine, cosine], -1)], -2)


def kx_of(slabs):
    base = 2 * np.arange(slabs)
    rows = np.stack([base, base + 1, -base, -base - 1], 1) % (4 * slabs)
    rows[0, 2] = 2 * slabs
    return rows


def tables(slabs):
    nx, nz, ny = 4 * slabs, 8 * slabs, 2 * MODES * PENCILS
    rows = 8 * slabs
    two_pi = 2.0 * np.pi
    y = np.arange(ny)
    ahead_y, back_y = [], []
    for r in range(4):
        block = (np.arange(4) - r) % 4
        ky = (block[:, None] * MODES + np.arange(MODES)[None, :]).reshape(-1)
        angle = two_pi * (y[:, None] * ky[None, :] % ny) / ny
        cosine, sine = np.cos(angle), -np.sin(angle)
        sine = np.where(ky[None, :] == 0, (1.0 - 2.0 * (y % 2))[:, None], sine)
        table = np.concatenate([cosine, sine], 1)
        weight = np.where(ky == 0, 1.0, 2.0) / ny
        ahead_y.append(halves(table))
        back_y.append(halves(table.T * np.concatenate([weight, weight])[:, None]))
    kx = kx_of(slabs).reshape(-1)
    x = np.arange(nx)
    form = real_form(two_pi * (kx[:, None] * x[None, :] % nx) / nx)
    form = form.reshape(nx, PENCILS, nx // PENCILS, 2, 2).transpose(0, 3, 1, 4, 2)
    table_x = form.reshape(rows, rows)
    k1 = np.arange(slabs)
    form = real_form(two_pi * (k1[:, None] * k1[None, :] % slabs) / slabs)
    same = np.eye(KXS)
    table_1 = np.einsum("ksoi,ab->okasbi", form, same).reshape(rows, rows)
    k2 = np.arange(PLANES)
    form = real_form(two_pi * (k2[:, None] * k2[None, :] % PLANES) / PLANES)
    table_2 = np.einsum("kpoi,ab->ipaokb", form, np.eye(MODES)).reshape(2 * PLANES * MODES, -1)
    angle = two_pi * (k1[:, None] * k2[None, :]) / nz
    angle = np.repeat(np.repeat(angle, KXS, 0), MODES, 1)
    twiddle = np.stack([np.cos(angle), np.sin(angle)]).astype(np.float32)
    return (
        np.stack(ahead_y), np.stack(back_y), halves(table_x), halves(table_x.T / nx),
        halves(table_1), halves(table_1.T / nz), halves(table_2), halves(table_2.T), twiddle,
    )


def split(values):
    high = values.astype(BF16)
    return high, (values - high.astype(F32)).astype(BF16)


def dot(a, b):
    return jnp.dot(a, b, preferred_element_type=F32)


def table_times(table, values):
    high, low = split(values)
    return dot(table[0], high) + (dot(table[0], low) + dot(table[1], high))


def times_table(values, table):
    high, low = split(values)
    return dot(high, table[0]) + (dot(low, table[0]) + dot(high, table[1]))


def spectral_kernel(
    slabs, vort, ahead_y, back_y, ahead_x, back_x, ahead_1, back_1, ahead_2, back_2, twiddle,
    vel, ys, xr, xo, zr, spec, zo, xr2, xo2, yr, send_sem, recv_sem, own_sem,
):
    me_z, me_x = lax.axis_index("gz"), lax.axis_index("gx")
    nx = 4 * slabs
    xl = nx // PENCILS
    rows = 8 * slabs
    half = 4 * slabs
    part = 2 * xl
    lanes = PLANES * MODES

    barrier = pltpu.get_barrier_semaphore()

    def greet(i, carry):
        pl.semaphore_signal(barrier, inc=1, device_id={"gz": lax.rem(me_z + i, slabs)}, device_id_type=MESH)
        return carry

    lax.fori_loop(1, slabs, greet, 0)
    for i in range(1, PENCILS):
        pl.semaphore_signal(barrier, inc=1, device_id={"gx": lax.rem(me_x + i, PENCILS)}, device_id_type=MESH)
    pl.semaphore_wait(barrier, slabs - 1 + PENCILS - 1)

    def own_copy(src, dst, c, stage, width, index):
        at = pl.ds(pl.multiple_of(index * width, 8), width)
        return pltpu.make_async_copy(src.at[c, at], dst.at[c, at], own_sem.at[stage, c])

    def send_gx(src, dst, c, stage):
        mine = pl.ds(pl.multiple_of(me_x * part, 8), part)
        for i in (2, 1, 3):
            other = lax.rem(me_x + i, PENCILS)
            pltpu.make_async_remote_copy(
                src_ref=src.at[c, pl.ds(pl.multiple_of(other * part, 8), part)],
                dst_ref=dst.at[c, mine],
                send_sem=send_sem.at[stage, c],
                recv_sem=recv_sem.at[stage, c],
                device_id={"gx": other},
                device_id_type=MESH,
            ).start()
        own_copy(src, dst, c, stage, part, me_x).start()

    def send_gz(src, dst, c, stage):
        mine = pl.ds(pl.multiple_of(me_z * 8, 8), 8)

        def one(i, carry):
            step = lax.div(i + 1, 2)
            step = step + lax.rem(i + 1, 2) * (slabs - 2 * step)
            other = lax.rem(me_z + step, slabs)
            pltpu.make_async_remote_copy(
                src_ref=src.at[c, pl.ds(pl.multiple_of(other * 8, 8), 8)],
                dst_ref=dst.at[c, mine],
                send_sem=send_sem.at[stage, c],
                recv_sem=recv_sem.at[stage, c],
                device_id={"gz": other},
                device_id_type=MESH,
            ).start()
            return carry

        lax.fori_loop(1, slabs, one, 0)
        own_copy(src, dst, c, stage, 8, me_z).start()

    def remote_rows(stage):
        return part * (PENCILS - 1) if stage in (0, 3) else 8 * (slabs - 1)

    def arrive(src, dst, c, stage):
        window = dst.at[c, pl.ds(0, remote_rows(stage))]
        pltpu.make_async_copy(window, window, recv_sem.at[stage, c]).wait()
        width, index = (part, me_x) if stage in (0, 3) else (8, me_z)
        own_copy(src, dst, c, stage, width, index).wait()

    def sent(src, c, stage):
        window = src.at[c, pl.ds(0, remote_rows(stage))]
        pltpu.make_async_copy(window, window, send_sem.at[stage, c]).wait()

    for c in range(3):
        spread = []
        for r in range(4):
            cells = jnp.concatenate([vort[c, r], vort[c, r + 4]], axis=0)
            spread.append(times_table(cells, ahead_y[r]))
        spot = lax.broadcasted_iota(jnp.int32, (part, 128), 1) // MODES
        for b in range(PENCILS):
            for p in range(2):
                picked = spread[0][:, p * 128:(p + 1) * 128]
                for r in range(1, 4):
                    picked = jnp.where(spot == (b + r) % 4, spread[r][:, p * 128:(p + 1) * 128], picked)
                if b:
                    picked = pltpu.roll(picked, 128 - MODES * b, 1)
                at = b * part + p * xl
                ys[c, at:at + xl, 0:128] = picked[:xl]
                ys[c, at:at + xl, 128:256] = picked[xl:]
        send_gx(ys, xr, c, 0)
    for c in range(3):
        arrive(ys, xr, c, 0)
        xo[c] = table_times(ahead_x, xr[c])
        send_gz(xo, zr, c, 1)
    cos_t, sin_t = twiddle[0], twiddle[1]
    for c in range(3):
        arrive(xo, zr, c, 1)
        mixed = table_times(ahead_1, zr[c])
        real, imag = mixed[:half], mixed[half:]
        turned = jnp.concatenate([real * cos_t + imag * sin_t, imag * cos_t - real * sin_t], axis=1)
        spec[c] = times_table(turned, ahead_2)
    row = lax.broadcasted_iota(jnp.int32, (half, lanes), 0)
    lane = lax.broadcasted_iota(jnp.int32, (half, lanes), 1)
    slot = row % KXS
    k1 = row // KXS
    kz = k1 + slabs * (lane // MODES)
    mode = lane % MODES
    base = 2 * me_z
    kx = base + slot % 2
    kx = jnp.where(slot >= 2, -kx, kx)
    kx = jnp.where((slot == 2) & (me_z == 0), nx // 2, kx)
    nz = 8 * slabs
    ky = me_x * MODES + mode
    wave_z = jnp.where(kz < nz // 2, kz, kz - nz).astype(F32) * (2.0 * math.pi / nz)
    wave_x = kx.astype(F32) * (2.0 * math.pi / nx)
    wave_y = ky.astype(F32) * (2.0 * math.pi / (2 * MODES * PENCILS))
    flat_sq = wave_z * wave_z + wave_x * wave_x
    packed = ky == 0
    anchor = (kz == 0) & (kx == 0) & packed
    wave_sq = flat_sq + wave_y * wave_y
    inverse = jnp.where(anchor, 0.0, 1.0 / jnp.where(anchor, 1.0, wave_sq))
    odd_inverse = 1.0 / (flat_sq + math.pi * math.pi)
    even = jnp.where(packed, 0.5 * (inverse + odd_inverse), inverse)
    cross = jnp.where(packed, 0.5 * (inverse - odd_inverse), 0.0)
    wave_z = jnp.where(kz == nz // 2, 0.0, wave_z)
    wave_x = jnp.where((kx == nx // 2), 0.0, wave_x)
    to = lax.broadcasted_iota(jnp.int32, (half, half), 0)
    fro = lax.broadcasted_iota(jnp.int32, (half, half), 1)
    to_slot = to % KXS
    mirror_slot = jnp.where(
        (me_z == 0), jnp.where(to_slot % 2 == 0, to_slot, 4 - to_slot), (to_slot + 2) % 4
    )
    mirror_row = ((slabs - to // KXS) % slabs) * KXS + mirror_slot
    row_swap = jnp.where(fro == mirror_row, 1.0, 0.0).astype(BF16)
    fro = lax.broadcasted_iota(jnp.int32, (2 * lanes, 2 * lanes), 0)
    to = lax.broadcasted_iota(jnp.int32, (2 * lanes, 2 * lanes), 1)
    mirror_lane = (to // lanes) * lanes + (PLANES - 1 - (to % lanes) // MODES) * MODES
    sign = jnp.where(to < lanes, 1.0, -1.0)
    lane_swap = jnp.where((fro == mirror_lane) & (to % MODES == 0), sign, 0.0).astype(BF16)
    stream = []
    for c in range(3):
        modes = spec[c]
        high, low = split(modes)
        swapped = dot(row_swap, high) + dot(row_swap, low)
        high, low = split(swapped)
        swapped = dot(high, lane_swap) + dot(low, lane_swap)
        pair = []
        for p in range(2):
            mirror = swapped[:, p * lanes:(p + 1) * lanes]
            mirror = jnp.where(k1 == 0, jnp.concatenate([mirror[:, lanes - MODES:], mirror[:, :lanes - MODES]], axis=1), mirror)
            pair.append(even * modes[:, p * lanes:(p + 1) * lanes] + cross * mirror)
        stream.append(pair)

    def curl(c, p):
        if c == 0:
            return wave_x * stream[2][p] - wave_y * stream[1][p]
        if c == 1:
            return wave_y * stream[0][p] - wave_z * stream[2][p]
        return wave_z * stream[1][p] - wave_x * stream[0][p]

    for c in range(3):
        turned = times_table(jnp.concatenate([-curl(c, 1), curl(c, 0)], axis=1), back_2)
        real, imag = turned[:, :lanes], turned[:, lanes:]
        mixed = jnp.concatenate([real * cos_t - imag * sin_t, imag * cos_t + real * sin_t], axis=0)
        zo[c] = table_times(back_1, mixed)
        send_gz(zo, xr2, c, 2)
    for c in range(3):
        arrive(zo, xr2, c, 2)
        xo2[c] = table_times(back_x, xr2[c])
        send_gx(xo2, yr, c, 3)
    spot = lax.broadcasted_iota(jnp.int32, (xl, 128), 1) // MODES
    for c in range(3):
        arrive(xo2, yr, c, 3)
        rolled = {}
        for zh in range(2):
            for b in range(PENCILS):
                for p in range(2):
                    at = b * part + p * xl
                    tile = yr[c, at:at + xl, zh * 128:(zh + 1) * 128]
                    rolled[zh, b, p] = pltpu.roll(tile, MODES * b, 1) if b else tile
        for r in range(4):
            sides = []
            for zh in range(2):
                both = []
                for p in range(2):
                    picked = rolled[zh, 0, p]
                    for b in range(1, 4):
                        picked = jnp.where(spot == (b + r) % 4, rolled[zh, b, p], picked)
                    both.append(picked)
                sides.append(jnp.concatenate(both, axis=1))
            cells = times_table(jnp.concatenate(sides, axis=0), back_y[r])
            vel[c, r] = cells[:xl]
            vel[c, r + 4] = cells[xl:]
    for c in range(3):
        sent(ys, c, 0)
        sent(xo, c, 1)
        sent(zo, c, 2)
        sent(xo2, c, 3)


def spectral(vort, slabs):
    consts = [jnp.asarray(t) for t in tables(slabs)]
    rows = 8 * slabs
    lanes = PLANES * MODES
    wide = pltpu.VMEM((3, rows, lanes), F32)
    return pl.pallas_call(
        functools.partial(spectral_kernel, slabs),
        out_shape=jax.ShapeDtypeStruct(vort.shape, F32),
        in_specs=[pl.BlockSpec(memory_space=pltpu.VMEM)] * (1 + len(consts)),
        out_specs=pl.BlockSpec(memory_space=pltpu.VMEM),
        scratch_shapes=[
            wide, wide, wide, wide,
            pltpu.VMEM((3, 4 * slabs, 2 * lanes), F32),
            wide, wide, wide, wide,
            pltpu.SemaphoreType.DMA((4, 3)),
            pltpu.SemaphoreType.DMA((4, 3)),
            pltpu.SemaphoreType.DMA((4, 3)),
        ],
        compiler_params=pltpu.CompilerParams(
            collective_id=0, has_side_effects=True, vmem_limit_bytes=56 * 1024 * 1024
        ),
    )(vort, *consts)


NY = 256
PART = 512
MIG = 64
time_step = 0.25


def padded_2(cells, sides, width):
    for axis, dim in sides:
        count = lax.axis_size(axis)
        head = lax.slice_in_dim(cells, 0, width, axis=dim)
        tail = lax.slice_in_dim(cells, cells.shape[dim] - width, cells.shape[dim], axis=dim)
        cells = jnp.concatenate(
            [
                lax.ppermute(tail, axis, [(i, (i + 1) % count) for i in range(count)]),
                cells,
                lax.ppermute(head, axis, [((i + 1) % count, i) for i in range(count)]),
            ],
            axis=dim,
        )
    return cells


def kernel_weight(distance):
    radius = jnp.abs(distance)
    near_part = 1.0 - 2.5 * radius * radius + 1.5 * radius * radius * radius
    far_part = 0.5 * (2.0 - radius) * (2.0 - radius) * (1.0 - radius)
    return jnp.where(radius < 1.0, near_part, jnp.where(radius < 2.0, far_part, 0.0))


def on_device(strength, offsets, cell_index, migrate_count, ambient):
    slab_planes = ambient.shape[1]
    pencil_cols = ambient.shape[2]
    slab_count = lax.axis_size("gz")
    up_count = migrate_count[0, 0, 0]
    down_count = migrate_count[0, 0, 1]
    slot_index = jnp.arange(PART, dtype=jnp.int32)
    packet = jnp.concatenate([strength, offsets, cell_index.astype(jnp.float32)[None, :]], axis=0)
    is_strength = (jnp.arange(7) < 3)[:, None]
    head_live = slot_index[:MIG] < up_count
    upward = jnp.where(is_strength & ~head_live[None, :], 0.0, packet[:, :MIG])
    downward = lax.dynamic_slice_in_dim(packet, up_count, MIG, axis=1)
    down_live = jnp.arange(MIG, dtype=jnp.int32) < down_count
    downward = jnp.where(is_strength & ~down_live[None, :], 0.0, downward)
    outgoing = jnp.concatenate([downward, upward], axis=1)
    extended = padded_2(outgoing, (("gz", 1),), MIG)
    arrived = jnp.concatenate([extended[:, :MIG], extended[:, 3 * MIG :]], axis=1)
    staying = slot_index >= up_count + down_count
    retained = jnp.where(is_strength & ~staying[None, :], 0.0, packet)
    particles = jnp.concatenate([retained, arrived], axis=1)
    particle_total = particles.shape[1]
    block_rows = math.gcd(particle_total, 256)
    row_blocks = particles.T.reshape(particle_total // block_rows, block_rows, 7)
    planes = jnp.arange(slab_planes + 4, dtype=jnp.int32) - 2
    columns = jnp.arange(pencil_cols + 4, dtype=jnp.int32) - 2
    lateral = jnp.arange(NY, dtype=jnp.int32)

    def deposit(deposited, row_group):
        cell_ids = row_group[:, 6].astype(jnp.int32)
        z_cell = cell_ids // (pencil_cols * NY)
        x_cell = cell_ids // NY % pencil_cols
        y_cell = cell_ids % NY
        weight_z = kernel_weight(
            (planes[None, :] - z_cell[:, None]).astype(jnp.float32) - row_group[:, 3:4]
        )
        weight_x = kernel_weight(
            (columns[None, :] - x_cell[:, None]).astype(jnp.float32) - row_group[:, 4:5]
        )
        y_offset = (lateral[None, :] - y_cell[:, None] + NY // 2) % NY - NY // 2
        weight_y = kernel_weight(y_offset.astype(jnp.float32) - row_group[:, 5:6])
        spread = (
            row_group[:, 0:3, None, None] * weight_z[:, None, :, None] * weight_x[:, None, None, :]
        )
        spread = spread.reshape(block_rows, -1)
        added = lax.dot_general(
            spread,
            weight_y,
            (((0,), (0,)), ((), ())),
            precision=lax.Precision.HIGHEST,
            preferred_element_type=jnp.float32,
        )
        return (deposited + added, None)

    start_mesh = jnp.zeros((3 * (slab_planes + 4) * (pencil_cols + 4), NY), jnp.float32)
    deposited, _ = lax.scan(deposit, start_mesh, row_blocks)
    deposited = deposited.reshape(3, slab_planes + 4, pencil_cols + 4, NY)
    plane_rim = jnp.concatenate([deposited[:, :2], deposited[:, slab_planes + 2 :]], axis=1)
    plane_rim = padded_2(plane_rim, (("gz", 1),), 2)
    interior = deposited[:, 2 : slab_planes + 2]
    interior = (
        interior.at[:, :2].add(plane_rim[:, :2]).at[:, slab_planes - 2 :].add(plane_rim[:, 6:])
    )
    column_rim = jnp.concatenate([interior[:, :, :2], interior[:, :, pencil_cols + 2 :]], axis=2)
    column_rim = padded_2(column_rim, (("gx", 2),), 2)
    interior = interior[:, :, 2 : pencil_cols + 2]
    interior = (
        interior.at[:, :, :2]
        .add(column_rim[:, :, :2])
        .at[:, :, pencil_cols - 2 :]
        .add(column_rim[:, :, 6:])
    )
    vorticity_mesh = ambient + interior
    velocity = spectral(vorticity_mesh, slab_count)
    padded = padded_2(velocity, (("gz", 1), ("gx", 2)), 1)
    along_z = (padded[:, 2:, 1:-1] - padded[:, :-2, 1:-1]) * 0.5
    along_x = (padded[:, 1:-1, 2:] - padded[:, 1:-1, :-2]) * 0.5
    along_y = (jnp.roll(velocity, -1, axis=3) - jnp.roll(velocity, 1, axis=3)) * 0.5
    stretch = (
        vorticity_mesh[0] * along_z + vorticity_mesh[1] * along_x + vorticity_mesh[2] * along_y
    )
    return (velocity, vorticity_mesh + time_step * stretch)


def solution(mesh):
    placed = (
        P(None, ("gz", "gx")),
        P(None, ("gz", "gx")),
        P(("gz", "gx")),
        P("gz", "gx", None),
        P(None, "gz", "gx", None),
    )
    return jax.shard_map(
        on_device,
        mesh=mesh,
        in_specs=placed,
        out_specs=(P(None, "gz", "gx", None), P(None, "gz", "gx", None)),
        check_vma=False,
    )
```

```python
import functools
import math

import jax
import jax.numpy as jnp
import ml_dtypes
import numpy as np
from jax import lax
from jax.experimental import pallas as pl
from jax.experimental.pallas import tpu as pltpu
from jax.sharding import PartitionSpec as P

MESH = pl.DeviceIdType.MESH
F32 = jnp.float32
BF16 = jnp.bfloat16
PENCILS = 4
MODES = 32
PLANES = 8
KXS = 4
NY = 256
PART = 512
OWN = 640
LANES = 1792
HOPS = ((1, 0, 128, 512), (1, 128, 384, 128), (-1, 0, 128, 1152), (-1, 128, 384, 1280), (2, 0, 128, 0), (-2, 0, 128, 1664))


def halves(table):
    high = table.astype(ml_dtypes.bfloat16)
    low = (table - high.astype(np.float64)).astype(ml_dtypes.bfloat16)
    return np.stack([high, low])


def real_form(angle):
    cosine, sine = np.cos(angle), np.sin(angle)
    return np.stack([np.stack([cosine, sine], -1), np.stack([-sine, cosine], -1)], -2)


def kx_of(slabs):
    base = 2 * np.arange(slabs)
    rows = np.stack([base, base + 1, -base, -base - 1], 1) % (4 * slabs)
    rows[0, 2] = 2 * slabs
    return rows


def tables(slabs):
    nx, nz, ny = 4 * slabs, 8 * slabs, 2 * MODES * PENCILS
    rows = 8 * slabs
    two_pi = 2.0 * np.pi
    y = np.arange(ny)
    ahead_y, back_y = [], []
    for r in range(4):
        block = (np.arange(4) - r) % 4
        ky = (block[:, None] * MODES + np.arange(MODES)[None, :]).reshape(-1)
        angle = two_pi * (y[:, None] * ky[None, :] % ny) / ny
        cosine, sine = np.cos(angle), -np.sin(angle)
        sine = np.where(ky[None, :] == 0, (1.0 - 2.0 * (y % 2))[:, None], sine)
        table = np.concatenate([cosine, sine], 1)
        weight = np.where(ky == 0, 1.0, 2.0) / ny
        ahead_y.append(halves(table))
        back_y.append(halves(table.T * np.concatenate([weight, weight])[:, None]))
    kx = kx_of(slabs).reshape(-1)
    x = np.arange(nx)
    form = real_form(two_pi * (kx[:, None] * x[None, :] % nx) / nx)
    form = form.reshape(nx, PENCILS, nx // PENCILS, 2, 2).transpose(0, 3, 1, 4, 2)
    table_x = form.reshape(rows, rows)
    k1 = np.arange(slabs)
    form = real_form(two_pi * (k1[:, None] * k1[None, :] % slabs) / slabs)
    same = np.eye(KXS)
    table_1 = np.einsum("ksoi,ab->okasbi", form, same).reshape(rows, rows)
    k2 = np.arange(PLANES)
    form = real_form(two_pi * (k2[:, None] * k2[None, :] % PLANES) / PLANES)
    table_2 = np.einsum("kpoi,ab->ipaokb", form, np.eye(MODES)).reshape(2 * PLANES * MODES, -1)
    angle = two_pi * (k1[:, None] * k2[None, :]) / nz
    angle = np.repeat(np.repeat(angle, KXS, 0), MODES, 1)
    twiddle = np.stack([np.cos(angle), np.sin(angle)]).astype(np.float32)
    return (
        np.stack(ahead_y), np.stack(back_y), halves(table_x), halves(table_x.T / nx),
        halves(table_1), halves(table_1.T / nz), halves(table_2), halves(table_2.T), twiddle,
    )


def kernel_weight(distance):
    radius = jnp.abs(distance)
    near_part = 1.0 - 2.5 * radius * radius + 1.5 * radius * radius * radius
    far_part = 0.5 * (2.0 - radius) * (2.0 - radius) * (1.0 - radius)
    return jnp.where(radius < 1.0, near_part, jnp.where(radius < 2.0, far_part, 0.0))


def split(values):
    high = values.astype(BF16)
    return high, (values - high.astype(F32)).astype(BF16)


def dot(a, b):
    return jnp.dot(a, b, preferred_element_type=F32)


def table_times(table, values):
    high, low = split(values)
    return dot(table[0], high) + (dot(table[0], low) + dot(table[1], high))


def times_table(values, table):
    high, low = split(values)
    return dot(high, table[0]) + (dot(low, table[0]) + dot(high, table[1]))


def step_kernel(
    slabs, counts, strength, offsets, cells, ambient,
    ahead_y, back_y, ahead_x, back_x, ahead_1, back_1, ahead_2, back_2, twiddle,
    vel, vorticity,
    packet, wide_x, high_y, low_y, high_l, low_l, rim, rim_in, vort, plane_in, side, side_in,
    ys, xr, xo, zr, spec, zo, xr2, xo2, yr,
    send_sem, recv_sem, own_sem, packet_send, packet_recv, rim_send, rim_recv,
    plane_send, plane_recv, side_send, side_recv,
):
    me_z, me_x = lax.axis_index("gz"), lax.axis_index("gx")
    nx = 4 * slabs
    xl = nx // PENCILS
    rows = 8 * slabs
    half = 4 * slabs
    part = 2 * xl
    lanes = PLANES * MODES

    barrier = pltpu.get_barrier_semaphore()

    def greet(i, carry):
        pl.semaphore_signal(barrier, inc=1, device_id={"gz": lax.rem(me_z + i, slabs)}, device_id_type=MESH)
        return carry

    lax.fori_loop(1, slabs, greet, 0)
    for i in range(1, PENCILS):
        pl.semaphore_signal(barrier, inc=1, device_id={"gx": lax.rem(me_x + i, PENCILS)}, device_id_type=MESH)
    lane_id = lax.broadcasted_iota(jnp.int32, (1, PART), 1)
    up, down = counts[0], counts[1]
    moves = jnp.where(lane_id < up, 1, jnp.where(lane_id < up + down, -1, 0))
    cell = cells[...]
    packet[:, OWN:OWN + PART] = jnp.concatenate(
        [
            strength[...],
            offsets[...],
            (cell // (xl * NY) + PLANES * moves).astype(F32),
            (cell % (xl * NY)).astype(F32),
        ],
        axis=0,
    )
    pl.semaphore_wait(barrier, slabs - 1 + PENCILS - 1)

    hops = []
    for n, (far, start, width, land) in enumerate(HOPS):
        hop = pltpu.make_async_remote_copy(
            src_ref=packet.at[:, OWN + start:OWN + start + width],
            dst_ref=packet.at[:, land:land + width],
            send_sem=packet_send.at[n],
            recv_sem=packet_recv.at[n],
            device_id={"gz": lax.rem(me_z + far + slabs, slabs)},
            device_id_type=MESH,
        )
        hop.start()
        hops.append(hop)
    for hop in hops:
        hop.wait_recv()
    fields = packet[...]
    lane = lax.broadcasted_iota(jnp.int32, (1, LANES), 1)
    shift = jnp.where(lane < 128, -16.0, jnp.where(lane < OWN, -8.0, jnp.where(lane < OWN + PART, 0.0, jnp.where(lane < LANES - 128, 8.0, 16.0))))
    z_cell = fields[6:7] + shift
    lateral = fields[7:8].astype(jnp.int32)
    x_cell = (lateral // NY).astype(F32)
    y_cell = lateral % NY
    plane = lax.broadcasted_iota(jnp.int32, (PLANES, LANES), 0).astype(F32)
    weight_z = kernel_weight((plane - z_cell) - fields[3:4])
    row = lax.broadcasted_iota(jnp.int32, (xl, LANES), 0).astype(F32)
    wide_x[...] = kernel_weight((row - x_cell) - fields[4:5])
    at_y = lax.broadcasted_iota(jnp.int32, (NY, LANES), 0)
    away = (at_y - y_cell + NY // 2) % NY - NY // 2
    weight_y = kernel_weight(away.astype(F32) - fields[5:6])
    high, low = split(weight_y)
    high_y[...] = high
    low_y[...] = low
    charge = [fields[c:c + 1] * weight_z for c in range(3)]

    def spread_over_y(high, low, lo, hi):
        def times(a, b):
            return lax.dot_general(a, b, (((1,), (1,)), ((), ())), preferred_element_type=F32)

        top = high_y[:, lo:hi]
        return times(high, top) + (times(low, top) + times(high, low_y[:, lo:hi]))

    rims = []
    for n, first in enumerate((xl, -2)):
        beyond = []
        for c in range(3):
            for r in range(2):
                beyond.append(charge[c] * kernel_weight((float(first + r) - x_cell) - fields[4:5]))
        high, low = split(jnp.concatenate(beyond, axis=0))
        rim[n] = spread_over_y(high, low, 0, LANES)
        far = 1 if n == 0 else PENCILS - 1
        copy = pltpu.make_async_remote_copy(
            src_ref=rim.at[n],
            dst_ref=rim_in.at[n],
            send_sem=rim_send.at[n],
            recv_sem=rim_recv.at[n],
            device_id={"gx": lax.rem(me_x + far, PENCILS)},
            device_id_type=MESH,
        )
        copy.start()
        rims.append(copy)

    def deposit(c):
        for planes, lo, hi in ((range(0, 2), 0, 1280), (range(2, 6), 512, 1280), (range(6, 8), 512, 1792)):
            columns = wide_x[:, lo:hi]
            for n, z in enumerate(planes):
                high, low = split(columns * charge[c][z:z + 1, lo:hi])
                high_l[n * xl:(n + 1) * xl, 0:hi - lo] = high
                low_l[n * xl:(n + 1) * xl, 0:hi - lo] = low
            size = len(planes) * xl
            added = spread_over_y(high_l[0:size, 0:hi - lo], low_l[0:size, 0:hi - lo], lo, hi)
            for n, z in enumerate(planes):
                vort[c, z] = ambient[c, z] + added[n * xl:(n + 1) * xl]
        if c == 0:
            for copy in rims:
                copy.wait_recv()
        for n, first in enumerate((0, xl - 2)):
            for r in range(2):
                for z in range(PLANES):
                    at = c * 16 + r * 8 + z
                    vort[c, z, first + r:first + r + 1, :] += rim_in[n, at:at + 1, :]

    def own_copy(src, dst, c, stage, width, index):
        at = pl.ds(pl.multiple_of(index * width, 8), width)
        return pltpu.make_async_copy(src.at[c, at], dst.at[c, at], own_sem.at[stage, c])

    def send_gx(src, dst, c, stage):
        mine = pl.ds(pl.multiple_of(me_x * part, 8), part)
        for i in (2, 1, 3):
            other = lax.rem(me_x + i, PENCILS)
            pltpu.make_async_remote_copy(
                src_ref=src.at[c, pl.ds(pl.multiple_of(other * part, 8), part)],
                dst_ref=dst.at[c, mine],
                send_sem=send_sem.at[stage, c],
                recv_sem=recv_sem.at[stage, c],
                device_id={"gx": other},
                device_id_type=MESH,
            ).start()
        own_copy(src, dst, c, stage, part, me_x).start()

    def send_gz(src, dst, c, stage):
        mine = pl.ds(pl.multiple_of(me_z * 8, 8), 8)

        def one(i, carry):
            step = lax.div(i + 1, 2)
            step = step + lax.rem(i + 1, 2) * (slabs - 2 * step)
            other = lax.rem(me_z + step, slabs)
            pltpu.make_async_remote_copy(
                src_ref=src.at[c, pl.ds(pl.multiple_of(other * 8, 8), 8)],
                dst_ref=dst.at[c, mine],
                send_sem=send_sem.at[stage, c],
                recv_sem=recv_sem.at[stage, c],
                device_id={"gz": other},
                device_id_type=MESH,
            ).start()
            return carry

        lax.fori_loop(1, slabs, one, 0)
        own_copy(src, dst, c, stage, 8, me_z).start()

    def remote_rows(stage):
        return part * (PENCILS - 1) if stage in (0, 3) else 8 * (slabs - 1)

    def arrive(src, dst, c, stage):
        window = dst.at[c, pl.ds(0, remote_rows(stage))]
        pltpu.make_async_copy(window, window, recv_sem.at[stage, c]).wait()
        width, index = (part, me_x) if stage in (0, 3) else (8, me_z)
        own_copy(src, dst, c, stage, width, index).wait()

    def sent(src, c, stage):
        window = src.at[c, pl.ds(0, remote_rows(stage))]
        pltpu.make_async_copy(window, window, send_sem.at[stage, c]).wait()

    for c in range(3):
        deposit(c)
        spread = []
        for r in range(4):
            both = jnp.concatenate([vort[c, r], vort[c, r + 4]], axis=0)
            spread.append(times_table(both, ahead_y[r]))
        spot = lax.broadcasted_iota(jnp.int32, (part, 128), 1) // MODES
        for b in range(PENCILS):
            for p in range(2):
                picked = spread[0][:, p * 128:(p + 1) * 128]
                for r in range(1, 4):
                    picked = jnp.where(spot == (b + r) % 4, spread[r][:, p * 128:(p + 1) * 128], picked)
                if b:
                    picked = pltpu.roll(picked, 128 - MODES * b, 1)
                at = b * part + p * xl
                ys[c, at:at + xl, 0:128] = picked[:xl]
                ys[c, at:at + xl, 128:256] = picked[xl:]
        send_gx(ys, xr, c, 0)
    for c in range(3):
        arrive(ys, xr, c, 0)
        xo[c] = table_times(ahead_x, xr[c])
        send_gz(xo, zr, c, 1)
    cos_t, sin_t = twiddle[0], twiddle[1]
    for c in range(3):
        arrive(xo, zr, c, 1)
        mixed = table_times(ahead_1, zr[c])
        real, imag = mixed[:half], mixed[half:]
        turned = jnp.concatenate([real * cos_t + imag * sin_t, imag * cos_t - real * sin_t], axis=1)
        spec[c] = times_table(turned, ahead_2)
    row = lax.broadcasted_iota(jnp.int32, (half, lanes), 0)
    lane = lax.broadcasted_iota(jnp.int32, (half, lanes), 1)
    slot = row % KXS
    k1 = row // KXS
    kz = k1 + slabs * (lane // MODES)
    mode = lane % MODES
    base = 2 * me_z
    kx = base + slot % 2
    kx = jnp.where(slot >= 2, -kx, kx)
    kx = jnp.where((slot == 2) & (me_z == 0), nx // 2, kx)
    nz = 8 * slabs
    ky = me_x * MODES + mode
    wave_z = jnp.where(kz < nz // 2, kz, kz - nz).astype(F32) * (2.0 * math.pi / nz)
    wave_x = kx.astype(F32) * (2.0 * math.pi / nx)
    wave_y = ky.astype(F32) * (2.0 * math.pi / (2 * MODES * PENCILS))
    flat_sq = wave_z * wave_z + wave_x * wave_x
    packed = ky == 0
    anchor = (kz == 0) & (kx == 0) & packed
    wave_sq = flat_sq + wave_y * wave_y
    inverse = jnp.where(anchor, 0.0, 1.0 / jnp.where(anchor, 1.0, wave_sq))
    odd_inverse = 1.0 / (flat_sq + math.pi * math.pi)
    even = jnp.where(packed, 0.5 * (inverse + odd_inverse), inverse)
    cross = jnp.where(packed, 0.5 * (inverse - odd_inverse), 0.0)
    wave_z = jnp.where(kz == nz // 2, 0.0, wave_z)
    wave_x = jnp.where((kx == nx // 2), 0.0, wave_x)
    to = lax.broadcasted_iota(jnp.int32, (half, half), 0)
    fro = lax.broadcasted_iota(jnp.int32, (half, half), 1)
    to_slot = to % KXS
    mirror_slot = jnp.where(
        (me_z == 0), jnp.where(to_slot % 2 == 0, to_slot, 4 - to_slot), (to_slot + 2) % 4
    )
    mirror_row = ((slabs - to // KXS) % slabs) * KXS + mirror_slot
    row_swap = jnp.where(fro == mirror_row, 1.0, 0.0).astype(BF16)
    fro = lax.broadcasted_iota(jnp.int32, (2 * lanes, 2 * lanes), 0)
    to = lax.broadcasted_iota(jnp.int32, (2 * lanes, 2 * lanes), 1)
    mirror_lane = (to // lanes) * lanes + (PLANES - 1 - (to % lanes) // MODES) * MODES
    sign = jnp.where(to < lanes, 1.0, -1.0)
    lane_swap = jnp.where((fro == mirror_lane) & (to % MODES == 0), sign, 0.0).astype(BF16)
    stream = []
    for c in range(3):
        modes = spec[c]
        high, low = split(modes)
        swapped = dot(row_swap, high) + dot(row_swap, low)
        high, low = split(swapped)
        swapped = dot(high, lane_swap) + dot(low, lane_swap)
        pair = []
        for p in range(2):
            mirror = swapped[:, p * lanes:(p + 1) * lanes]
            mirror = jnp.where(k1 == 0, jnp.concatenate([mirror[:, lanes - MODES:], mirror[:, :lanes - MODES]], axis=1), mirror)
            pair.append(even * modes[:, p * lanes:(p + 1) * lanes] + cross * mirror)
        stream.append(pair)

    def curl(c, p):
        if c == 0:
            return wave_x * stream[2][p] - wave_y * stream[1][p]
        if c == 1:
            return wave_y * stream[0][p] - wave_z * stream[2][p]
        return wave_z * stream[1][p] - wave_x * stream[0][p]

    for c in range(3):
        turned = times_table(jnp.concatenate([-curl(c, 1), curl(c, 0)], axis=1), back_2)
        real, imag = turned[:, :lanes], turned[:, lanes:]
        mixed = jnp.concatenate([real * cos_t - imag * sin_t, imag * cos_t + real * sin_t], axis=0)
        zo[c] = table_times(back_1, mixed)
        send_gz(zo, xr2, c, 2)
    for c in range(3):
        arrive(zo, xr2, c, 2)
        xo2[c] = table_times(back_x, xr2[c])
        send_gx(xo2, yr, c, 3)
    spot = lax.broadcasted_iota(jnp.int32, (xl, 128), 1) // MODES
    edges = [[], [], []]
    for c in range(3):
        arrive(xo2, yr, c, 3)
        rolled = {}
        for zh in range(2):
            for b in range(PENCILS):
                for p in range(2):
                    at = b * part + p * xl
                    tile = yr[c, at:at + xl, zh * 128:(zh + 1) * 128]
                    rolled[zh, b, p] = pltpu.roll(tile, MODES * b, 1) if b else tile
        for r in range(4):
            sides = []
            for zh in range(2):
                both = []
                for p in range(2):
                    picked = rolled[zh, 0, p]
                    for b in range(1, 4):
                        picked = jnp.where(spot == (b + r) % 4, rolled[zh, b, p], picked)
                    both.append(picked)
                sides.append(jnp.concatenate(both, axis=1))
            both = times_table(jnp.concatenate(sides, axis=0), back_y[r])
            vel[c, r] = both[:xl]
            vel[c, r + 4] = both[xl:]
        for n, (far, z) in enumerate(((1, PLANES - 1), (slabs - 1, 0))):
            copy = pltpu.make_async_remote_copy(
                src_ref=vel.at[c, z],
                dst_ref=plane_in.at[n, c],
                send_sem=plane_send.at[n, c],
                recv_sem=plane_recv.at[n, c],
                device_id={"gz": lax.rem(me_z + far, slabs)},
                device_id_type=MESH,
            )
            copy.start()
            edges[c].append(copy)
        for n, (far, x) in enumerate(((1, xl - 1), (PENCILS - 1, 0))):
            side[n, c] = jnp.concatenate([vel[c, z, x:x + 1, :] for z in range(PLANES)], axis=0)
            copy = pltpu.make_async_remote_copy(
                src_ref=side.at[n, c],
                dst_ref=side_in.at[n, c],
                send_sem=side_send.at[n, c],
                recv_sem=side_recv.at[n, c],
                device_id={"gx": lax.rem(me_x + far, PENCILS)},
                device_id_type=MESH,
            )
            copy.start()
            edges[c].append(copy)
    at_x = lax.broadcasted_iota(jnp.int32, (xl, NY), 0)
    for c in range(3):
        for copy in edges[c]:
            copy.wait_recv()
        for z in range(PLANES):
            here = vel[c, z]
            above = vel[c, z + 1] if z < PLANES - 1 else plane_in[1, c]
            below = vel[c, z - 1] if z > 0 else plane_in[0, c]
            right = jnp.where(at_x == xl - 1, side_in[1, c, z:z + 1, :], pltpu.roll(here, xl - 1, 0))
            left = jnp.where(at_x == 0, side_in[0, c, z:z + 1, :], pltpu.roll(here, 1, 0))
            turned = pltpu.roll(here, NY - 1, 1) - pltpu.roll(here, 1, 1)
            stretch = (
                vort[0, z] * ((above - below) * 0.5)
                + vort[1, z] * ((right - left) * 0.5)
                + vort[2, z] * (turned * 0.5)
            )
            vorticity[c, z] = vort[c, z] + 0.25 * stretch
    for copy in hops + rims + edges[0] + edges[1] + edges[2]:
        copy.wait_send()
    for c in range(3):
        sent(ys, c, 0)
        sent(xo, c, 1)
        sent(zo, c, 2)
        sent(xo2, c, 3)


def on_device(strength, offsets, cell_index, migrate_count, ambient):
    slabs = lax.axis_size("gz")
    xl = ambient.shape[2]
    consts = [jnp.asarray(t) for t in tables(slabs)]
    rows = 8 * slabs
    lanes = PLANES * MODES
    wide = pltpu.VMEM((3, rows, lanes), F32)
    dma = pltpu.SemaphoreType.DMA
    vmem = pl.BlockSpec(memory_space=pltpu.VMEM)
    mesh = jax.ShapeDtypeStruct(ambient.shape, F32)
    return pl.pallas_call(
        functools.partial(step_kernel, slabs),
        out_shape=(mesh, mesh),
        in_specs=[pl.BlockSpec(memory_space=pltpu.SMEM)] + [vmem] * (4 + len(consts)),
        out_specs=(vmem, vmem),
        scratch_shapes=[
            pltpu.VMEM((8, LANES), F32),
            pltpu.VMEM((xl, LANES), F32),
            pltpu.VMEM((NY, LANES), BF16),
            pltpu.VMEM((NY, LANES), BF16),
            pltpu.VMEM((4 * xl, 1280), BF16),
            pltpu.VMEM((4 * xl, 1280), BF16),
            pltpu.VMEM((2, 48, NY), F32),
            pltpu.VMEM((2, 48, NY), F32),
            pltpu.VMEM((3, PLANES, xl, NY), F32),
            pltpu.VMEM((2, 3, xl, NY), F32),
            pltpu.VMEM((2, 3, PLANES, NY), F32),
            pltpu.VMEM((2, 3, PLANES, NY), F32),
            wide, wide, wide, wide,
            pltpu.VMEM((3, 4 * slabs, 2 * lanes), F32),
            wide, wide, wide, wide,
            dma((4, 3)), dma((4, 3)), dma((4, 3)),
            dma((6,)), dma((6,)), dma((2,)), dma((2,)),
            dma((2, 3)), dma((2, 3)), dma((2, 3)), dma((2, 3)),
        ],
        compiler_params=pltpu.CompilerParams(
            collective_id=0, has_side_effects=True, vmem_limit_bytes=60 * 1024 * 1024
        ),
    )(migrate_count.reshape(2), strength, offsets, cell_index.reshape(1, PART), ambient, *consts)


def solution(mesh):
    placed = (
        P(None, ("gz", "gx")),
        P(None, ("gz", "gx")),
        P(("gz", "gx")),
        P("gz", "gx", None),
        P(None, "gz", "gx", None),
    )
    return jax.shard_map(
        on_device,
        mesh=mesh,
        in_specs=placed,
        out_specs=(P(None, "gz", "gx", None), P(None, "gz", "gx", None)),
        check_vma=False,
    )
```

```python
import functools
import math

import jax
import jax.numpy as jnp
import ml_dtypes
import numpy as np
from jax import lax
from jax.experimental import pallas as pl
from jax.experimental.pallas import tpu as pltpu
from jax.sharding import PartitionSpec as P

MESH = pl.DeviceIdType.MESH
F32 = jnp.float32
BF16 = jnp.bfloat16
PENCILS = 4
PLANES = 8
MODES = 16
KXS = 4
NY = 256
PART = 512
CHUNKS = 6
OWN = 640
LANES = 1792
HOPS = ((1, 0, 128, 512), (1, 128, 384, 128), (-1, 0, 128, 1152), (-1, 128, 384, 1280), (2, 0, 128, 0), (-2, 0, 128, 1664))


def halves(table):
    high = table.astype(ml_dtypes.bfloat16)
    low = (table - high.astype(np.float64)).astype(ml_dtypes.bfloat16)
    return np.stack([high, low])


def real_form(angle):
    cosine, sine = np.cos(angle), np.sin(angle)
    return np.stack([np.stack([cosine, sine], -1), np.stack([-sine, cosine], -1)], -2)


def kx_of(slabs):
    base = 2 * np.arange(slabs)
    rows = np.stack([base, base + 1, -base, -base - 1], 1) % (4 * slabs)
    rows[0, 2] = 2 * slabs
    return rows


def tables(slabs):
    nx, nz = 4 * slabs, 8 * slabs
    rows = 8 * slabs
    two_pi = 2.0 * np.pi
    y = np.arange(NY)
    half, pencil, mode = np.meshgrid(np.arange(2), np.arange(PENCILS), np.arange(MODES), indexing="ij")
    ky = (pencil * 2 * MODES + half * MODES + mode).reshape(-1)
    angle = two_pi * (y[:, None] * ky[None, :] % NY) / NY
    sine = np.where(ky[None, :] == 0, (1.0 - 2.0 * (y % 2))[:, None], -np.sin(angle))
    table_y = np.concatenate([np.cos(angle), sine], 1)
    weight = np.where(ky == 0, 1.0, 2.0) / NY
    back_y = table_y.T * np.concatenate([weight, weight])[:, None]
    kx = kx_of(slabs).reshape(-1)
    x = np.arange(nx)
    form = real_form(two_pi * (kx[:, None] * x[None, :] % nx) / nx)
    form = form.reshape(nx, PENCILS, nx // PENCILS, 2, 2).transpose(0, 3, 1, 4, 2)
    table_x = form.reshape(rows, rows)
    k1 = np.arange(slabs)
    form = real_form(two_pi * (k1[:, None] * k1[None, :] % slabs) / slabs)
    table_1 = np.einsum("ksoi,ab->okasbi", form, np.eye(KXS)).reshape(rows, rows)
    k2 = np.arange(PLANES)
    form = real_form(two_pi * (k2[:, None] * k2[None, :] % PLANES) / PLANES)
    table_2 = np.einsum("kpoi,ab->ipaokb", form, np.eye(MODES)).reshape(2 * PLANES * MODES, -1)
    angle = two_pi * (k1[:, None] * k2[None, :]) / nz
    angle = np.repeat(np.repeat(angle, KXS, 0), MODES, 1)
    twiddle = np.stack([np.cos(angle), np.sin(angle)]).astype(np.float32)
    return (
        halves(table_y), halves(back_y), halves(table_x), halves(table_x.T / nx),
        halves(table_1), halves(table_1.T / nz), halves(table_2), halves(table_2.T), twiddle,
    )


def kernel_weight(distance):
    radius = jnp.abs(distance)
    near_part = 1.0 + radius * radius * (1.5 * radius - 2.5)
    beyond = 2.0 - radius
    far_part = 0.5 * beyond * beyond * (1.0 - radius)
    return jnp.where(radius < 1.0, near_part, jnp.where(radius < 2.0, far_part, 0.0))


def split(values):
    high = values.astype(BF16)
    return high, (values - high.astype(F32)).astype(BF16)


def dot(a, b):
    return jnp.dot(a, b, preferred_element_type=F32)


def table_times(table, values):
    high, low = split(values)
    width = values.shape[1]
    both = dot(table[0], jnp.concatenate([high, low], axis=1))
    return both[:, :width] + (both[:, width:] + dot(table[1], high))


def times_table(values, table):
    high, low = split(values)
    return dot(high, table[0]) + (dot(low, table[0]) + dot(high, table[1]))


def step_kernel(
    slabs, counts, strength, offsets, cells, ambient, *refs,
):
    tables_in, (vel_out, vorticity_out) = refs[:9], refs[9:11]
    (
        packet, wide_x, high_y, low_y, charge, high_l, low_l, rim, rim_in, vort, vel, vorticity,
        plane_in, side, side_in, ys, xr, xo, zr, spec, zo, xr2, xo2, yr, fixed, row_swap, lane_swap,
    ) = refs[11:38]
    tables_here = refs[38:47]
    ahead_y, back_y, ahead_x, back_x, ahead_1, back_1, ahead_2, back_2, twiddle = tables_here
    (
        send_sem, recv_sem, own_sem, packet_send, packet_recv, rim_send, rim_recv,
        plane_send, plane_recv, side_send, side_recv, load_sem, store_sem,
    ) = refs[47:]
    me_z, me_x = lax.axis_index("gz"), lax.axis_index("gx")
    nx, nz = 4 * slabs, 8 * slabs
    xl = nx // PENCILS
    half = 4 * slabs
    part = 2 * xl
    wide = PLANES * MODES

    barrier = pltpu.get_barrier_semaphore()

    def greet(i, carry):
        pl.semaphore_signal(barrier, inc=1, device_id={"gz": lax.rem(me_z + i, slabs)}, device_id_type=MESH)
        return carry

    lax.fori_loop(1, slabs, greet, 0)
    for i in range(1, PENCILS):
        pl.semaphore_signal(barrier, inc=1, device_id={"gx": lax.rem(me_x + i, PENCILS)}, device_id_type=MESH)
    load_mesh = pltpu.make_async_copy(ambient, vort, load_sem.at[9])
    load_mesh.start()
    loads = [pltpu.make_async_copy(a, b, load_sem.at[n]) for n, (a, b) in enumerate(zip(tables_in, tables_here))]
    for copy in loads:
        copy.start()

    lane_id = lax.broadcasted_iota(jnp.int32, (1, PART), 1)
    up, down = counts[0], counts[1]
    moves = jnp.where(lane_id < up, 1, jnp.where(lane_id < up + down, -1, 0))
    cell = cells[...]
    packet[:, OWN:OWN + PART] = jnp.concatenate(
        [
            strength[...],
            offsets[...],
            (cell // (xl * NY) + PLANES * moves).astype(F32),
            (cell % (xl * NY)).astype(F32),
        ],
        axis=0,
    )

    def weigh(lo, hi):
        size = hi - lo
        fields = packet[:, lo:hi]
        lane = lax.broadcasted_iota(jnp.int32, (1, size), 1) + lo
        shift = jnp.where(lane < 128, -16.0, jnp.where(lane < OWN, -8.0, jnp.where(lane < OWN + PART, 0.0, jnp.where(lane < LANES - 128, 8.0, 16.0))))
        lateral = fields[7:8].astype(jnp.int32)
        plane = lax.broadcasted_iota(jnp.int32, (PLANES, size), 0).astype(F32)
        weight_z = kernel_weight((plane - (fields[6:7] + shift)) - fields[3:4])
        row = lax.broadcasted_iota(jnp.int32, (xl, size), 0).astype(F32)
        wide_x[:, lo:hi] = kernel_weight((row - (lateral >> 8).astype(F32)) - fields[4:5])
        at_y = lax.broadcasted_iota(jnp.int32, (NY, size), 0)
        away = ((at_y + (NY // 2 - (lateral & 255))) & 255) - NY // 2
        high, low = split(kernel_weight(away.astype(F32) - fields[5:6]))
        high_y[:, lo:hi] = high
        low_y[:, lo:hi] = low
        for c in range(3):
            charge[8 * c:8 * c + 8, lo:hi] = fields[c:c + 1] * weight_z

    weigh(OWN, OWN + PART)
    pl.semaphore_wait(barrier, slabs - 1 + PENCILS - 1)

    hops = []
    for n, (far, start, width, land) in enumerate(HOPS):
        hop = pltpu.make_async_remote_copy(
            src_ref=packet.at[:, OWN + start:OWN + start + width],
            dst_ref=packet.at[:, land:land + width],
            send_sem=packet_send.at[n],
            recv_sem=packet_recv.at[n],
            device_id={"gz": lax.rem(me_z + far + slabs, slabs)},
            device_id_type=MESH,
        )
        hop.start()
        hops.append(hop)

    def send_gx(src, dst, k, stage):
        mine = pl.ds(pl.multiple_of(me_x * part, 8), part)
        for i in (2, 1, 3):
            other = lax.rem(me_x + i, PENCILS)
            pltpu.make_async_remote_copy(
                src_ref=src.at[k, pl.ds(pl.multiple_of(other * part, 8), part)],
                dst_ref=dst.at[k, mine],
                send_sem=send_sem.at[stage, k],
                recv_sem=recv_sem.at[stage, k],
                device_id={"gx": other},
                device_id_type=MESH,
            ).start()
        own_copy(src, dst, k, stage).start()

    def send_gz(src, dst, k, stage):
        mine = pl.ds(pl.multiple_of(me_z * 8, 8), 8)

        def one(i, carry):
            other = lax.rem(me_z + i, slabs)
            pltpu.make_async_remote_copy(
                src_ref=src.at[k, pl.ds(pl.multiple_of(other * 8, 8), 8)],
                dst_ref=dst.at[k, mine],
                send_sem=send_sem.at[stage, k],
                recv_sem=recv_sem.at[stage, k],
                device_id={"gz": other},
                device_id_type=MESH,
            ).start()
            return carry

        lax.fori_loop(1, slabs, one, 0)
        own_copy(src, dst, k, stage).start()

    def own_copy(src, dst, k, stage):
        width, index = (part, me_x) if stage in (0, 3) else (8, me_z)
        at = pl.ds(pl.multiple_of(index * width, 8), width)
        return pltpu.make_async_copy(src.at[k, at], dst.at[k, at], own_sem.at[stage, k])

    def remote_rows(stage):
        return part * (PENCILS - 1) if stage in (0, 3) else 8 * (slabs - 1)

    def arrive(src, dst, k, stage):
        window = dst.at[k, pl.ds(0, remote_rows(stage))]
        pltpu.make_async_copy(window, window, recv_sem.at[stage, k]).wait()
        own_copy(src, dst, k, stage).wait()

    def sent(src, k, stage):
        window = src.at[k, pl.ds(0, remote_rows(stage))]
        pltpu.make_async_copy(window, window, send_sem.at[stage, k]).wait()

    for hop in hops:
        hop.wait_recv()
    weigh(0, OWN)
    weigh(OWN + PART, LANES)

    def spread_over_y(high, low, lo, hi):
        def times(a, b):
            return lax.dot_general(a, b, (((1,), (1,)), ((), ())), preferred_element_type=F32)

        top = high_y[:, lo:hi]
        return times(high, top) + (times(low, top) + times(high, low_y[:, lo:hi]))

    rims = []
    x_cell = (packet[7:8, :].astype(jnp.int32) >> 8).astype(F32)
    for n, first in enumerate((xl, -2)):
        beyond = [kernel_weight((float(first + r) - x_cell) - packet[4:5, :]) for r in range(2)]
        high, low = split(jnp.concatenate([charge[8 * c:8 * c + 8, :] * beyond[r] for c in range(3) for r in range(2)], axis=0))
        rim[n] = spread_over_y(high, low, 0, LANES)
        far = 1 if n == 0 else PENCILS - 1
        copy = pltpu.make_async_remote_copy(
            src_ref=rim.at[n],
            dst_ref=rim_in.at[n],
            send_sem=rim_send.at[n],
            recv_sem=rim_recv.at[n],
            device_id={"gx": lax.rem(me_x + far, PENCILS)},
            device_id_type=MESH,
        )
        copy.start()
        rims.append(copy)
    load_mesh.wait()

    def deposit(c):
        for planes, lo, hi in ((range(0, 2), 0, 1280), (range(2, 6), 512, 1280), (range(6, 8), 512, 1792)):
            columns = wide_x[:, lo:hi]
            for n, z in enumerate(planes):
                high, low = split(columns * charge[8 * c + z:8 * c + z + 1, lo:hi])
                high_l[n * xl:(n + 1) * xl, 0:hi - lo] = high
                low_l[n * xl:(n + 1) * xl, 0:hi - lo] = low
            size = len(planes) * xl
            at = planes[0] * xl
            vort[c, at:at + size] += spread_over_y(high_l[0:size, 0:hi - lo], low_l[0:size, 0:hi - lo], lo, hi)
        if c == 0:
            for copy in rims:
                copy.wait_recv()
        for n, first in enumerate((0, xl - 2)):
            for r in range(2):
                for z in range(PLANES):
                    at = c * 16 + r * 8 + z
                    to = z * xl + first + r
                    vort[c, to:to + 1, :] += rim_in[n, at:at + 1, :]

    spot = lax.broadcasted_iota(jnp.int32, (xl, wide), 1) >> 4
    for c in range(3):
        deposit(c)
        if c == 0:
            loads[0].wait()
        modes = times_table(vort[c], ahead_y)
        for p in range(2):
            turned = []
            for z in range(PLANES):
                tile = modes[z * xl:(z + 1) * xl, p * wide:(p + 1) * wide]
                turned.append(pltpu.roll(tile, MODES * z, 1) if z else tile)
            for q in range(8):
                picked = turned[0]
                for z in range(1, PLANES):
                    picked = jnp.where(spot == (q + z) % 8, turned[z], picked)
                if q:
                    picked = pltpu.roll(picked, wide - MODES * q, 1)
                at = (q % PENCILS) * part + p * xl
                ys[3 * (q // PENCILS) + c, at:at + xl] = picked
        send_gx(ys, xr, c, 0)
    for c in range(3):
        send_gx(ys, xr, 3 + c, 0)
    loads[2].wait()
    for k in range(CHUNKS):
        arrive(ys, xr, k, 0)
        xo[k] = table_times(ahead_x, xr[k])
        send_gz(xo, zr, k, 1)
    row = lax.broadcasted_iota(jnp.int32, (half, wide), 0)
    lane = lax.broadcasted_iota(jnp.int32, (half, wide), 1)
    slot = row & 3
    k1 = row >> 2
    kz = k1 + slabs * (lane >> 4)
    kx = 2 * me_z + (slot & 1)
    kx = jnp.where(slot >= 2, -kx, kx)
    kx = jnp.where((slot == 2) & (me_z == 0), nx // 2, kx)
    wave_z = jnp.where(kz < nz // 2, kz, kz - nz).astype(F32) * (2.0 * math.pi / nz)
    wave_x = kx.astype(F32) * (2.0 * math.pi / nx)
    flat_sq = wave_z * wave_z + wave_x * wave_x
    fixed[0] = jnp.where(kz == nz // 2, 0.0, wave_z)
    fixed[1] = jnp.where(kx == nx // 2, 0.0, wave_x)
    for h in range(2):
        ky = me_x * (2 * MODES) + h * MODES + (lane & 15)
        wave_y = ky.astype(F32) * (2.0 * math.pi / NY)
        anchor = (kz == 0) & (kx == 0) & (ky == 0)
        inverse = jnp.where(anchor, 0.0, 1.0 / jnp.where(anchor, 1.0, flat_sq + wave_y * wave_y))
        fixed[2 + 2 * h] = wave_y
        if h == 0:
            packed = ky == 0
            other = 1.0 / (flat_sq + math.pi * math.pi)
            fixed[6] = jnp.where(packed, 0.5 * (inverse - other), 0.0)
            inverse = jnp.where(packed, 0.5 * (inverse + other), inverse)
        fixed[3 + 2 * h] = inverse
    fro = lax.broadcasted_iota(jnp.int32, (half, half), 1)
    to = lax.broadcasted_iota(jnp.int32, (half, half), 0)
    to_slot = to & 3
    paired_slot = jnp.where(me_z == 0, jnp.where((to_slot & 1) == 0, to_slot, 4 - to_slot), (to_slot + 2) & 3)
    mirror_row = ((slabs - (to >> 2)) & (slabs - 1)) * KXS + paired_slot
    row_swap[...] = jnp.where(fro == mirror_row, 1.0, 0.0).astype(BF16)
    fro = lax.broadcasted_iota(jnp.int32, (2 * wide, 2 * wide), 0)
    to = lax.broadcasted_iota(jnp.int32, (2 * wide, 2 * wide), 1)
    mirror_lane = (to & wide) + (PLANES - 1 - ((to & (wide - 1)) >> 4)) * MODES
    sign = jnp.where(to < wide, 1.0, -1.0)
    lane_swap[...] = jnp.where((fro == mirror_lane) & ((to & 15) == 0), sign, 0.0).astype(BF16)
    for n in (4, 6, 8, 7, 5):
        loads[n].wait()

    def to_modes(k):
        mixed = table_times(ahead_1, zr[k])
        real, imag = mixed[:half], mixed[half:]
        cos_t, sin_t = twiddle[0], twiddle[1]
        turned = jnp.concatenate([real * cos_t + imag * sin_t, imag * cos_t - real * sin_t], axis=1)
        spec[k] = times_table(turned, ahead_2)

    def from_modes(k, real, imag):
        turned = times_table(jnp.concatenate([real, imag], axis=1), back_2)
        cos_t, sin_t = twiddle[0], twiddle[1]
        real, imag = turned[:, :wide], turned[:, wide:]
        mixed = jnp.concatenate([real * cos_t - imag * sin_t, imag * cos_t + real * sin_t], axis=0)
        zo[k] = table_times(back_1, mixed)

    def mirrored(k):
        high, low = split(spec[k])
        swapped = dot(row_swap[...], high) + dot(row_swap[...], low)
        high, low = split(swapped)
        swapped = dot(high, lane_swap[...]) + dot(low, lane_swap[...])
        parts = []
        for p in range(2):
            tile = swapped[:, p * wide:(p + 1) * wide]
            parts.append(jnp.where(k1 == 0, pltpu.roll(tile, MODES, 1), tile))
        return parts

    for h in range(2):
        for c in range(3):
            k = 3 * h + c
            arrive(xo, zr, k, 1)
            to_modes(k)
            if h == 0:
                pair = mirrored(k)
                for p in range(2):
                    at = slice(p * wide, (p + 1) * wide)
                    spec[k, :, at] = fixed[3] * spec[k, :, at] + fixed[6] * pair[p]
            else:
                for p in range(2):
                    at = slice(p * wide, (p + 1) * wide)
                    spec[k, :, at] = fixed[5] * spec[k, :, at]

        def stream(c, p):
            return spec[3 * h + c, :, p * wide:(p + 1) * wide]

        def curl(c, p):
            if c == 0:
                return fixed[1] * stream(2, p) - fixed[2 + 2 * h] * stream(1, p)
            if c == 1:
                return fixed[2 + 2 * h] * stream(0, p) - fixed[0] * stream(2, p)
            return fixed[0] * stream(1, p) - fixed[1] * stream(0, p)

        for c in range(3):
            from_modes(3 * h + c, -curl(c, 1), curl(c, 0))
            send_gz(zo, xr2, 3 * h + c, 2)
    loads[3].wait()
    for k in range(CHUNKS):
        arrive(zo, xr2, k, 2)
        xo2[k] = table_times(back_x, xr2[k])
        send_gx(xo2, yr, k, 3)
    loads[1].wait()
    edges = [[], [], []]
    stores = []
    at_x = lax.broadcasted_iota(jnp.int32, (xl, NY), 0)

    def stretch(c):
        for copy in edges[c]:
            copy.wait_recv()
        for z in range(PLANES):
            rows = slice(z * xl, (z + 1) * xl)
            here = vel[c, rows]
            above = vel[c, (z + 1) * xl:(z + 2) * xl] if z < PLANES - 1 else plane_in[1, c]
            below = vel[c, (z - 1) * xl:z * xl] if z > 0 else plane_in[0, c]
            right = jnp.where(at_x == xl - 1, side_in[1, c, z:z + 1, :], pltpu.roll(here, xl - 1, 0))
            left = jnp.where(at_x == 0, side_in[0, c, z:z + 1, :], pltpu.roll(here, 1, 0))
            along_y = pltpu.roll(here, NY - 1, 1) - pltpu.roll(here, 1, 1)
            rate = (
                vort[0, rows] * ((above - below) * 0.5)
                + vort[1, rows] * ((right - left) * 0.5)
                + vort[2, rows] * (along_y * 0.5)
            )
            vorticity[c, rows] = vort[c, rows] + 0.25 * rate
        stores.append(pltpu.make_async_copy(vorticity.at[c], vorticity_out.at[c], store_sem.at[1, c]))
        stores[-1].start()

    for c in range(3):
        rolled = []
        for q in range(8):
            h, b = q // PENCILS, q % PENCILS
            if b == 0:
                arrive(xo2, yr, 3 * h + c, 3)
            both = []
            for p in range(2):
                at = b * part + p * xl
                tile = yr[3 * h + c, at:at + xl]
                both.append(pltpu.roll(tile, MODES * q, 1) if q else tile)
            rolled.append(both)
        planes = []
        for z in range(PLANES):
            both = []
            for p in range(2):
                picked = rolled[0][p]
                for q in range(1, 8):
                    picked = jnp.where(spot == (q + z) % 8, rolled[q][p], picked)
                both.append(pltpu.roll(picked, wide - MODES * z, 1) if z else picked)
            planes.append(jnp.concatenate(both, axis=1))
        vel[c] = times_table(jnp.concatenate(planes, axis=0), back_y)
        for n, (far, z) in enumerate(((1, PLANES - 1), (slabs - 1, 0))):
            copy = pltpu.make_async_remote_copy(
                src_ref=vel.at[c, pl.ds(z * xl, xl)],
                dst_ref=plane_in.at[n, c],
                send_sem=plane_send.at[n, c],
                recv_sem=plane_recv.at[n, c],
                device_id={"gz": lax.rem(me_z + far, slabs)},
                device_id_type=MESH,
            )
            copy.start()
            edges[c].append(copy)
        for n, (far, x) in enumerate(((1, xl - 1), (PENCILS - 1, 0))):
            side[n, c] = jnp.concatenate([vel[c, z * xl + x:z * xl + x + 1, :] for z in range(PLANES)], axis=0)
            copy = pltpu.make_async_remote_copy(
                src_ref=side.at[n, c],
                dst_ref=side_in.at[n, c],
                send_sem=side_send.at[n, c],
                recv_sem=side_recv.at[n, c],
                device_id={"gx": lax.rem(me_x + far, PENCILS)},
                device_id_type=MESH,
            )
            copy.start()
            edges[c].append(copy)
        stores.append(pltpu.make_async_copy(vel.at[c], vel_out.at[c], store_sem.at[0, c]))
        stores[-1].start()
        if c:
            stretch(c - 1)
    stretch(2)
    for copy in hops + rims + edges[0] + edges[1] + edges[2]:
        copy.wait_send()
    for k in range(CHUNKS):
        sent(ys, k, 0)
        sent(xo, k, 1)
        sent(zo, k, 2)
        sent(xo2, k, 3)
    for copy in stores:
        copy.wait()


def on_device(strength, offsets, cell_index, migrate_count, ambient):
    slabs = lax.axis_size("gz")
    xl = ambient.shape[2]
    consts = [jnp.asarray(t) for t in tables(slabs)]
    chunk = pltpu.VMEM((CHUNKS, 8 * slabs, PLANES * MODES), F32)
    mesh = pltpu.VMEM((3, PLANES * xl, NY), F32)
    dma = pltpu.SemaphoreType.DMA
    vmem = pl.BlockSpec(memory_space=pltpu.VMEM)
    whole = pl.BlockSpec(memory_space=pl.ANY)
    flat = jax.ShapeDtypeStruct((3, PLANES * xl, NY), F32)
    velocity, vorticity = pl.pallas_call(
        functools.partial(step_kernel, slabs),
        out_shape=(flat, flat),
        in_specs=[pl.BlockSpec(memory_space=pltpu.SMEM), vmem, vmem, vmem, whole] + [whole] * len(consts),
        out_specs=(whole, whole),
        scratch_shapes=[
            pltpu.VMEM((8, LANES), F32),
            pltpu.VMEM((xl, LANES), F32),
            pltpu.VMEM((NY, LANES), BF16),
            pltpu.VMEM((NY, LANES), BF16),
            pltpu.VMEM((24, LANES), F32),
            pltpu.VMEM((4 * xl, 1280), BF16),
            pltpu.VMEM((4 * xl, 1280), BF16),
            pltpu.VMEM((2, 48, NY), F32),
            pltpu.VMEM((2, 48, NY), F32),
            mesh, mesh, mesh,
            pltpu.VMEM((2, 3, xl, NY), F32),
            pltpu.VMEM((2, 3, PLANES, NY), F32),
            pltpu.VMEM((2, 3, PLANES, NY), F32),
            chunk, chunk, chunk, chunk,
            pltpu.VMEM((CHUNKS, 4 * slabs, 2 * PLANES * MODES), F32),
            chunk, chunk, chunk, chunk,
            pltpu.VMEM((7, 4 * slabs, PLANES * MODES), F32),
            pltpu.VMEM((4 * slabs, 4 * slabs), BF16),
            pltpu.VMEM((2 * PLANES * MODES, 2 * PLANES * MODES), BF16),
            *[pltpu.VMEM(t.shape, t.dtype) for t in consts],
            dma((4, CHUNKS)), dma((4, CHUNKS)), dma((4, CHUNKS)),
            dma((6,)), dma((6,)), dma((2,)), dma((2,)),
            dma((2, 3)), dma((2, 3)), dma((2, 3)), dma((2, 3)),
            dma((10,)), dma((2, 3)),
        ],
        compiler_params=pltpu.CompilerParams(
            collective_id=0, has_side_effects=True, vmem_limit_bytes=57 * 1024 * 1024
        ),
    )(migrate_count.reshape(2), strength, offsets, cell_index.reshape(1, PART), ambient.reshape(flat.shape), *consts)
    return velocity.reshape(ambient.shape), vorticity.reshape(ambient.shape)


def solution(mesh):
    placed = (
        P(None, ("gz", "gx")),
        P(None, ("gz", "gx")),
        P(("gz", "gx")),
        P("gz", "gx", None),
        P(None, "gz", "gx", None),
    )
    return jax.shard_map(
        on_device,
        mesh=mesh,
        in_specs=placed,
        out_specs=(P(None, "gz", "gx", None), P(None, "gz", "gx", None)),
        check_vma=False,
    )
```

```python
import functools
import math

import jax
import jax.numpy as jnp
import ml_dtypes
import numpy as np
from jax import lax
from jax.experimental import pallas as pl
from jax.experimental.pallas import tpu as pltpu
from jax.sharding import PartitionSpec as P

MESH = pl.DeviceIdType.MESH
F32 = jnp.float32
BF16 = jnp.bfloat16
PENCILS = 4
PLANES = 8
MODES = 16
KXS = 4
NY = 256
PART = 512
CHUNKS = 6
GROUP = 9
OWN = 640
LANES = 1792
HOPS = ((1, 0, 128, 512), (1, 128, 384, 128), (-1, 0, 128, 1152), (-1, 128, 384, 1280), (2, 0, 128, 0), (-2, 0, 128, 1664))


def halves(table):
    high = table.astype(ml_dtypes.bfloat16)
    low = (table - high.astype(np.float64)).astype(ml_dtypes.bfloat16)
    return np.stack([high, low])


def real_form(angle):
    cosine, sine = np.cos(angle), np.sin(angle)
    return np.stack([np.stack([cosine, sine], -1), np.stack([-sine, cosine], -1)], -2)


def kx_of(slabs):
    base = 2 * np.arange(slabs)
    rows = np.stack([base, base + 1, -base, -base - 1], 1) % (4 * slabs)
    rows[0, 2] = 2 * slabs
    return rows


def tables(slabs):
    nx, nz = 4 * slabs, 8 * slabs
    rows = 8 * slabs
    two_pi = 2.0 * np.pi
    y = np.arange(NY)
    half, pencil, mode = np.meshgrid(np.arange(2), np.arange(PENCILS), np.arange(MODES), indexing="ij")
    ky = (pencil * 2 * MODES + half * MODES + mode).reshape(-1)
    angle = two_pi * (y[:, None] * ky[None, :] % NY) / NY
    sine = np.where(ky[None, :] == 0, (1.0 - 2.0 * (y % 2))[:, None], -np.sin(angle))
    table_y = np.concatenate([np.cos(angle), sine], 1)
    weight = np.where(ky == 0, 1.0, 2.0) / NY
    back_y = table_y.T * np.concatenate([weight, weight])[:, None]
    kx = kx_of(slabs).reshape(-1)
    x = np.arange(nx)
    form = real_form(two_pi * (kx[:, None] * x[None, :] % nx) / nx)
    form = form.reshape(nx, PENCILS, nx // PENCILS, 2, 2).transpose(0, 3, 1, 4, 2)
    table_x = form.reshape(rows, rows)
    k1 = np.arange(slabs)
    form = real_form(two_pi * (k1[:, None] * k1[None, :] % slabs) / slabs)
    table_1 = np.einsum("ksoi,ab->okasbi", form, np.eye(KXS)).reshape(rows, rows)
    k2 = np.arange(PLANES)
    form = real_form(two_pi * (k2[:, None] * k2[None, :] % PLANES) / PLANES)
    table_2 = np.einsum("kpoi,ab->ipaokb", form, np.eye(MODES)).reshape(2 * PLANES * MODES, -1)
    angle = two_pi * (k1[:, None] * k2[None, :]) / nz
    angle = np.repeat(np.repeat(angle, KXS, 0), MODES, 1)
    twiddle = np.stack([np.cos(angle), np.sin(angle)]).astype(np.float32)
    return (
        halves(table_y), halves(back_y), halves(table_x), halves(table_x.T / nx),
        halves(table_1), halves(table_1.T / nz), halves(table_2), halves(table_2.T), twiddle,
    )


def kernel_weight(distance):
    radius = jnp.abs(distance)
    near_part = 1.0 + radius * radius * (1.5 * radius - 2.5)
    beyond = 2.0 - radius
    far_part = 0.5 * beyond * beyond * (1.0 - radius)
    return jnp.where(radius < 1.0, near_part, jnp.where(radius < 2.0, far_part, 0.0))


def split(values):
    high = values.astype(BF16)
    return high, (values - high.astype(F32)).astype(BF16)


def dot(a, b):
    return jnp.dot(a, b, preferred_element_type=F32)


def table_times(table, values):
    high, low = split(values)
    width = values.shape[1]
    both = dot(table[0], jnp.concatenate([high, low], axis=1))
    return both[:, :width] + (both[:, width:] + dot(table[1], high))


def times_table(values, table):
    high, low = split(values)
    return dot(high, table[0]) + (dot(low, table[0]) + dot(high, table[1]))


def step_kernel(
    slabs, counts, strength, offsets, cells, ambient, *refs,
):
    tables_in, (vel_out, vorticity_out) = refs[:9], refs[9:11]
    (
        packet, wide_x, high_y, low_y, charge, high_l, low_l, rim, rim_in, vort, vel, vorticity,
        plane_in, side, side_in, ys, xr, xo, zr, spec, zo, xr2, xo2, yr, fixed, row_swap, lane_swap,
    ) = refs[11:38]
    tables_here = refs[38:47]
    ahead_y, back_y, ahead_x, back_x, ahead_1, back_1, ahead_2, back_2, twiddle = tables_here
    (
        send_sem, recv_sem, own_sem, packet_send, packet_recv, rim_send, rim_recv,
        plane_send, plane_recv, side_send, side_recv, load_sem, store_sem,
    ) = refs[47:]
    me_z, me_x = lax.axis_index("gz"), lax.axis_index("gx")
    nx, nz = 4 * slabs, 8 * slabs
    xl = nx // PENCILS
    half = 4 * slabs
    part = 2 * xl
    wide = PLANES * MODES

    barrier = pltpu.get_barrier_semaphore()

    def each_other_slab(act):
        group = math.gcd(slabs - 1, GROUP)

        def some(i, carry):
            for j in range(group):
                act(lax.rem(me_z + 1 + j + i * group, slabs))
            return carry

        lax.fori_loop(0, (slabs - 1) // group, some, 0)

    def greet(other):
        pl.semaphore_signal(barrier, inc=1, device_id={"gz": other}, device_id_type=MESH)

    each_other_slab(greet)
    for i in range(1, PENCILS):
        pl.semaphore_signal(barrier, inc=1, device_id={"gx": lax.rem(me_x + i, PENCILS)}, device_id_type=MESH)
    load_mesh = pltpu.make_async_copy(ambient, vort, load_sem.at[9])
    load_mesh.start()
    loads = [pltpu.make_async_copy(a, b, load_sem.at[n]) for n, (a, b) in enumerate(zip(tables_in, tables_here))]
    for copy in loads:
        copy.start()

    lane_id = lax.broadcasted_iota(jnp.int32, (1, PART), 1)
    up, down = counts[0], counts[1]
    moves = jnp.where(lane_id < up, 1, jnp.where(lane_id < up + down, -1, 0))
    cell = cells[...]
    packet[:, OWN:OWN + PART] = jnp.concatenate(
        [
            strength[...],
            offsets[...],
            (cell // (xl * NY) + PLANES * moves).astype(F32),
            (cell % (xl * NY)).astype(F32),
        ],
        axis=0,
    )

    def weigh(lo, hi):
        size = hi - lo
        fields = packet[:, lo:hi]
        lane = lax.broadcasted_iota(jnp.int32, (1, size), 1) + lo
        shift = jnp.where(lane < 128, -16.0, jnp.where(lane < OWN, -8.0, jnp.where(lane < OWN + PART, 0.0, jnp.where(lane < LANES - 128, 8.0, 16.0))))
        lateral = fields[7:8].astype(jnp.int32)
        plane = lax.broadcasted_iota(jnp.int32, (PLANES, size), 0).astype(F32)
        weight_z = kernel_weight((plane - (fields[6:7] + shift)) - fields[3:4])
        row = lax.broadcasted_iota(jnp.int32, (xl, size), 0).astype(F32)
        wide_x[:, lo:hi] = kernel_weight((row - (lateral >> 8).astype(F32)) - fields[4:5])
        at_y = lax.broadcasted_iota(jnp.int32, (NY, size), 0)
        away = ((at_y + (NY // 2 - (lateral & 255))) & 255) - NY // 2
        high, low = split(kernel_weight(away.astype(F32) - fields[5:6]))
        high_y[:, lo:hi] = high
        low_y[:, lo:hi] = low
        for c in range(3):
            charge[8 * c:8 * c + 8, lo:hi] = fields[c:c + 1] * weight_z

    pl.semaphore_wait(barrier, slabs - 1 + PENCILS - 1)

    hops = []
    for n, (far, start, width, land) in enumerate(HOPS):
        hop = pltpu.make_async_remote_copy(
            src_ref=packet.at[:, OWN + start:OWN + start + width],
            dst_ref=packet.at[:, land:land + width],
            send_sem=packet_send.at[n],
            recv_sem=packet_recv.at[n],
            device_id={"gz": lax.rem(me_z + far + slabs, slabs)},
            device_id_type=MESH,
        )
        hop.start()
        hops.append(hop)

    def send_gx(src, dst, k, stage):
        mine = pl.ds(pl.multiple_of(me_x * part, 8), part)
        for i in (2, 1, 3):
            other = lax.rem(me_x + i, PENCILS)
            pltpu.make_async_remote_copy(
                src_ref=src.at[k, pl.ds(pl.multiple_of(other * part, 8), part)],
                dst_ref=dst.at[k, mine],
                send_sem=send_sem.at[stage, k],
                recv_sem=recv_sem.at[stage, k],
                device_id={"gx": other},
                device_id_type=MESH,
            ).start()
        own_copy(src, dst, k, stage).start()

    def send_gz(src, dst, k, stage):
        mine = pl.ds(pl.multiple_of(me_z * 8, 8), 8)

        def one(other):
            pltpu.make_async_remote_copy(
                src_ref=src.at[k, pl.ds(pl.multiple_of(other * 8, 8), 8)],
                dst_ref=dst.at[k, mine],
                send_sem=send_sem.at[stage, k],
                recv_sem=recv_sem.at[stage, k],
                device_id={"gz": other},
                device_id_type=MESH,
            ).start()

        each_other_slab(one)
        own_copy(src, dst, k, stage).start()

    def own_copy(src, dst, k, stage):
        width, index = (part, me_x) if stage in (0, 3) else (8, me_z)
        at = pl.ds(pl.multiple_of(index * width, 8), width)
        return pltpu.make_async_copy(src.at[k, at], dst.at[k, at], own_sem.at[stage, k])

    def remote_rows(stage):
        return part * (PENCILS - 1) if stage in (0, 3) else 8 * (slabs - 1)

    def arrive(src, dst, k, stage):
        window = dst.at[k, pl.ds(0, remote_rows(stage))]
        pltpu.make_async_copy(window, window, recv_sem.at[stage, k]).wait()
        own_copy(src, dst, k, stage).wait()

    def sent(src, k, stage):
        window = src.at[k, pl.ds(0, remote_rows(stage))]
        pltpu.make_async_copy(window, window, send_sem.at[stage, k]).wait()

    weigh(OWN, OWN + PART)
    for hop in hops:
        hop.wait_recv()
    weigh(0, OWN)
    weigh(OWN + PART, LANES)

    def spread_over_y(high, low, lo, hi):
        def times(a, b):
            return lax.dot_general(a, b, (((1,), (1,)), ((), ())), preferred_element_type=F32)

        top = high_y[:, lo:hi]
        return times(high, top) + (times(low, top) + times(high, low_y[:, lo:hi]))

    rims = []
    x_cell = (packet[7:8, :].astype(jnp.int32) >> 8).astype(F32)
    for n, first in enumerate((xl, -2)):
        beyond = [kernel_weight((float(first + r) - x_cell) - packet[4:5, :]) for r in range(2)]
        high, low = split(jnp.concatenate([charge[8 * c:8 * c + 8, :] * beyond[r] for c in range(3) for r in range(2)], axis=0))
        rim[n] = spread_over_y(high, low, 0, LANES)
        far = 1 if n == 0 else PENCILS - 1
        copy = pltpu.make_async_remote_copy(
            src_ref=rim.at[n],
            dst_ref=rim_in.at[n],
            send_sem=rim_send.at[n],
            recv_sem=rim_recv.at[n],
            device_id={"gx": lax.rem(me_x + far, PENCILS)},
            device_id_type=MESH,
        )
        copy.start()
        rims.append(copy)
    load_mesh.wait()

    def deposit(c):
        for planes, lo, hi in ((range(0, 2), 0, 1280), (range(2, 6), 512, 1280), (range(6, 8), 512, 1792)):
            columns = wide_x[:, lo:hi]
            for n, z in enumerate(planes):
                high, low = split(columns * charge[8 * c + z:8 * c + z + 1, lo:hi])
                high_l[n * xl:(n + 1) * xl, 0:hi - lo] = high
                low_l[n * xl:(n + 1) * xl, 0:hi - lo] = low
            size = len(planes) * xl
            at = planes[0] * xl
            vort[c, at:at + size] += spread_over_y(high_l[0:size, 0:hi - lo], low_l[0:size, 0:hi - lo], lo, hi)
        if c == 0:
            for copy in rims:
                copy.wait_recv()
        for n, first in enumerate((0, xl - 2)):
            for r in range(2):
                for z in range(PLANES):
                    at = c * 16 + r * 8 + z
                    to = z * xl + first + r
                    vort[c, to:to + 1, :] += rim_in[n, at:at + 1, :]

    spot = lax.broadcasted_iota(jnp.int32, (xl, wide), 1) >> 4
    for c in range(3):
        deposit(c)
        if c == 0:
            loads[0].wait()
        modes = times_table(vort[c], ahead_y)
        for p in range(2):
            turned = []
            for z in range(PLANES):
                tile = modes[z * xl:(z + 1) * xl, p * wide:(p + 1) * wide]
                turned.append(pltpu.roll(tile, MODES * z, 1) if z else tile)
            for q in range(8):
                picked = turned[0]
                for z in range(1, PLANES):
                    picked = jnp.where(spot == (q + z) % 8, turned[z], picked)
                if q:
                    picked = pltpu.roll(picked, wide - MODES * q, 1)
                at = (q % PENCILS) * part + p * xl
                ys[3 * (q // PENCILS) + c, at:at + xl] = picked
        send_gx(ys, xr, c, 0)
    for c in range(3):
        send_gx(ys, xr, 3 + c, 0)
    loads[2].wait()
    for k in range(CHUNKS):
        arrive(ys, xr, k, 0)
        xo[k] = table_times(ahead_x, xr[k])
        send_gz(xo, zr, k, 1)
    row = lax.broadcasted_iota(jnp.int32, (half, wide), 0)
    lane = lax.broadcasted_iota(jnp.int32, (half, wide), 1)
    slot = row & 3
    k1 = row >> 2
    kz = k1 + slabs * (lane >> 4)
    kx = 2 * me_z + (slot & 1)
    kx = jnp.where(slot >= 2, -kx, kx)
    kx = jnp.where((slot == 2) & (me_z == 0), nx // 2, kx)
    wave_z = jnp.where(kz < nz // 2, kz, kz - nz).astype(F32) * (2.0 * math.pi / nz)
    wave_x = kx.astype(F32) * (2.0 * math.pi / nx)
    flat_sq = wave_z * wave_z + wave_x * wave_x
    fixed[0] = jnp.where(kz == nz // 2, 0.0, wave_z)
    fixed[1] = jnp.where(kx == nx // 2, 0.0, wave_x)
    for h in range(2):
        ky = me_x * (2 * MODES) + h * MODES + (lane & 15)
        wave_y = ky.astype(F32) * (2.0 * math.pi / NY)
        anchor = (kz == 0) & (kx == 0) & (ky == 0)
        inverse = jnp.where(anchor, 0.0, 1.0 / jnp.where(anchor, 1.0, flat_sq + wave_y * wave_y))
        fixed[2 + 2 * h] = wave_y
        if h == 0:
            packed = ky == 0
            other = 1.0 / (flat_sq + math.pi * math.pi)
            fixed[6] = jnp.where(packed, 0.5 * (inverse - other), 0.0)
            inverse = jnp.where(packed, 0.5 * (inverse + other), inverse)
        fixed[3 + 2 * h] = inverse
    fro = lax.broadcasted_iota(jnp.int32, (half, half), 1)
    to = lax.broadcasted_iota(jnp.int32, (half, half), 0)
    to_slot = to & 3
    paired_slot = jnp.where(me_z == 0, jnp.where((to_slot & 1) == 0, to_slot, 4 - to_slot), (to_slot + 2) & 3)
    mirror_row = ((slabs - (to >> 2)) & (slabs - 1)) * KXS + paired_slot
    row_swap[...] = jnp.where(fro == mirror_row, 1.0, 0.0).astype(BF16)
    fro = lax.broadcasted_iota(jnp.int32, (2 * wide, 2 * wide), 0)
    to = lax.broadcasted_iota(jnp.int32, (2 * wide, 2 * wide), 1)
    mirror_lane = (to & wide) + (PLANES - 1 - ((to & (wide - 1)) >> 4)) * MODES
    sign = jnp.where(to < wide, 1.0, -1.0)
    lane_swap[...] = jnp.where((fro == mirror_lane) & ((to & 15) == 0), sign, 0.0).astype(BF16)
    for n in (4, 6, 8, 7, 5):
        loads[n].wait()

    def to_modes(k):
        mixed = table_times(ahead_1, zr[k])
        real, imag = mixed[:half], mixed[half:]
        cos_t, sin_t = twiddle[0], twiddle[1]
        turned = jnp.concatenate([real * cos_t + imag * sin_t, imag * cos_t - real * sin_t], axis=1)
        spec[k] = times_table(turned, ahead_2)

    def from_modes(k, real, imag):
        turned = times_table(jnp.concatenate([real, imag], axis=1), back_2)
        cos_t, sin_t = twiddle[0], twiddle[1]
        real, imag = turned[:, :wide], turned[:, wide:]
        mixed = jnp.concatenate([real * cos_t - imag * sin_t, imag * cos_t + real * sin_t], axis=0)
        zo[k] = table_times(back_1, mixed)

    def mirrored(k):
        high, low = split(spec[k])
        swapped = dot(row_swap[...], high) + dot(row_swap[...], low)
        high, low = split(swapped)
        swapped = dot(high, lane_swap[...]) + dot(low, lane_swap[...])
        parts = []
        for p in range(2):
            tile = swapped[:, p * wide:(p + 1) * wide]
            parts.append(jnp.where(k1 == 0, pltpu.roll(tile, MODES, 1), tile))
        return parts

    for h in range(2):
        for c in range(3):
            k = 3 * h + c
            arrive(xo, zr, k, 1)
            to_modes(k)
            if h == 0:
                pair = mirrored(k)
                for p in range(2):
                    at = slice(p * wide, (p + 1) * wide)
                    spec[k, :, at] = fixed[3] * spec[k, :, at] + fixed[6] * pair[p]
            else:
                for p in range(2):
                    at = slice(p * wide, (p + 1) * wide)
                    spec[k, :, at] = fixed[5] * spec[k, :, at]

        def stream(c, p):
            return spec[3 * h + c, :, p * wide:(p + 1) * wide]

        def curl(c, p):
            if c == 0:
                return fixed[1] * stream(2, p) - fixed[2 + 2 * h] * stream(1, p)
            if c == 1:
                return fixed[2 + 2 * h] * stream(0, p) - fixed[0] * stream(2, p)
            return fixed[0] * stream(1, p) - fixed[1] * stream(0, p)

        for c in range(3):
            from_modes(3 * h + c, -curl(c, 1), curl(c, 0))
            send_gz(zo, xr2, 3 * h + c, 2)
    loads[3].wait()
    loads[1].wait()
    edges = [[], [], []]
    stores = []

    def back_to_x(k):
        arrive(zo, xr2, k, 2)
        xo2[k] = table_times(back_x, xr2[k])
        send_gx(xo2, yr, k, 3)

    def back_to_y(c):
        rolled = []
        for q in range(8):
            h, b = q // PENCILS, q % PENCILS
            if b == 0:
                arrive(xo2, yr, 3 * h + c, 3)
            both = []
            for p in range(2):
                at = b * part + p * xl
                tile = yr[3 * h + c, at:at + xl]
                both.append(pltpu.roll(tile, MODES * q, 1) if q else tile)
            rolled.append(both)
        planes = []
        for z in range(PLANES):
            both = []
            for p in range(2):
                picked = rolled[0][p]
                for q in range(1, 8):
                    picked = jnp.where(spot == (q + z) % 8, rolled[q][p], picked)
                both.append(pltpu.roll(picked, wide - MODES * z, 1) if z else picked)
            planes.append(jnp.concatenate(both, axis=1))
        vel[c] = times_table(jnp.concatenate(planes, axis=0), back_y)
        for n, (far, z) in enumerate(((1, PLANES - 1), (slabs - 1, 0))):
            copy = pltpu.make_async_remote_copy(
                src_ref=vel.at[c, pl.ds(z * xl, xl)],
                dst_ref=plane_in.at[n, c],
                send_sem=plane_send.at[n, c],
                recv_sem=plane_recv.at[n, c],
                device_id={"gz": lax.rem(me_z + far, slabs)},
                device_id_type=MESH,
            )
            copy.start()
            edges[c].append(copy)
        for n, (far, x) in enumerate(((1, xl - 1), (PENCILS - 1, 0))):
            side[n, c] = jnp.concatenate([vel[c, z * xl + x:z * xl + x + 1, :] for z in range(PLANES)], axis=0)
            copy = pltpu.make_async_remote_copy(
                src_ref=side.at[n, c],
                dst_ref=side_in.at[n, c],
                send_sem=side_send.at[n, c],
                recv_sem=side_recv.at[n, c],
                device_id={"gx": lax.rem(me_x + far, PENCILS)},
                device_id_type=MESH,
            )
            copy.start()
            edges[c].append(copy)
        stores.append(pltpu.make_async_copy(vel.at[c], vel_out.at[c], store_sem.at[0, c]))
        stores[-1].start()

    at_x = lax.broadcasted_iota(jnp.int32, (xl, NY), 0)

    def stretch_inside(c):
        for z in range(PLANES):
            rows = slice(z * xl, (z + 1) * xl)
            here = vel[c, rows]
            along_z = -vel[c, (z - 1) * xl:z * xl] if z > 0 else None
            if z < PLANES - 1:
                above = vel[c, (z + 1) * xl:(z + 2) * xl]
                along_z = above + along_z if z > 0 else above
            right = jnp.where(at_x == xl - 1, 0.0, pltpu.roll(here, xl - 1, 0))
            left = jnp.where(at_x == 0, 0.0, pltpu.roll(here, 1, 0))
            along_y = pltpu.roll(here, NY - 1, 1) - pltpu.roll(here, 1, 1)
            rate = vort[0, rows] * along_z + vort[1, rows] * (right - left) + vort[2, rows] * along_y
            vorticity[c, rows] = vort[c, rows] + 0.125 * rate

    def stretch_edges(c):
        for copy in edges[c]:
            copy.wait_recv()
        for n, (first, sign) in enumerate(((0, -0.125), ((PLANES - 1) * xl, 0.125))):
            rows = slice(first, first + xl)
            vorticity[c, rows] += vort[0, rows] * (sign * plane_in[n, c])
        for n, (first, sign) in enumerate(((0, -0.125), (xl - 1, 0.125))):
            for z in range(PLANES):
                at = z * xl + first
                vorticity[c, at:at + 1, :] += vort[1, at:at + 1, :] * (sign * side_in[n, c, z:z + 1, :])
        stores.append(pltpu.make_async_copy(vorticity.at[c], vorticity_out.at[c], store_sem.at[1, c]))
        stores[-1].start()

    for k in range(CHUNKS - 1):
        back_to_x(k)
    back_to_y(0)
    back_to_x(CHUNKS - 1)
    stretch_inside(0)
    back_to_y(1)
    stretch_edges(0)
    stretch_inside(1)
    back_to_y(2)
    stretch_edges(1)
    stretch_inside(2)
    stretch_edges(2)
    for copy in hops + rims + edges[0] + edges[1] + edges[2]:
        copy.wait_send()
    for k in range(CHUNKS):
        sent(ys, k, 0)
        sent(xo, k, 1)
        sent(zo, k, 2)
        sent(xo2, k, 3)
    for copy in stores:
        copy.wait()


def put_kernel(velocity, vorticity, velocity_out, vorticity_out, sems):
    copies = [
        pltpu.make_async_copy(velocity, velocity_out, sems.at[0]),
        pltpu.make_async_copy(vorticity, vorticity_out, sems.at[1]),
    ]
    for copy in copies:
        copy.start()
    for copy in copies:
        copy.wait()


def on_device(strength, offsets, cell_index, migrate_count, ambient):
    slabs = lax.axis_size("gz")
    xl = ambient.shape[2]
    consts = [jnp.asarray(t) for t in tables(slabs)]
    chunk = pltpu.VMEM((CHUNKS, 8 * slabs, PLANES * MODES), F32)
    mesh = pltpu.VMEM((3, PLANES * xl, NY), F32)
    dma = pltpu.SemaphoreType.DMA
    vmem = pl.BlockSpec(memory_space=pltpu.VMEM)
    whole = pl.BlockSpec(memory_space=pl.ANY)
    flat = jax.ShapeDtypeStruct((3, PLANES * xl, NY), F32)
    velocity, vorticity = pl.pallas_call(
        functools.partial(step_kernel, slabs),
        out_shape=(pltpu.VMEM(flat.shape, F32), pltpu.VMEM(flat.shape, F32)),
        in_specs=[pl.BlockSpec(memory_space=pltpu.SMEM), vmem, vmem, vmem, whole] + [whole] * len(consts),
        out_specs=(whole, whole),
        scratch_shapes=[
            pltpu.VMEM((8, LANES), F32),
            pltpu.VMEM((xl, LANES), F32),
            pltpu.VMEM((NY, LANES), BF16),
            pltpu.VMEM((NY, LANES), BF16),
            pltpu.VMEM((24, LANES), F32),
            pltpu.VMEM((4 * xl, 1280), BF16),
            pltpu.VMEM((4 * xl, 1280), BF16),
            pltpu.VMEM((2, 48, NY), F32),
            pltpu.VMEM((2, 48, NY), F32),
            mesh, mesh, mesh,
            pltpu.VMEM((2, 3, xl, NY), F32),
            pltpu.VMEM((2, 3, PLANES, NY), F32),
            pltpu.VMEM((2, 3, PLANES, NY), F32),
            chunk, chunk, chunk, chunk,
            pltpu.VMEM((CHUNKS, 4 * slabs, 2 * PLANES * MODES), F32),
            chunk, chunk, chunk, chunk,
            pltpu.VMEM((7, 4 * slabs, PLANES * MODES), F32),
            pltpu.VMEM((4 * slabs, 4 * slabs), BF16),
            pltpu.VMEM((2 * PLANES * MODES, 2 * PLANES * MODES), BF16),
            *[pltpu.VMEM(t.shape, t.dtype) for t in consts],
            dma((4, CHUNKS)), dma((4, CHUNKS)), dma((4, CHUNKS)),
            dma((6,)), dma((6,)), dma((2,)), dma((2,)),
            dma((2, 3)), dma((2, 3)), dma((2, 3)), dma((2, 3)),
            dma((10,)), dma((2, 3)),
        ],
        compiler_params=pltpu.CompilerParams(
            collective_id=0, has_side_effects=True, vmem_limit_bytes=56 * 1024 * 1024
        ),
    )(migrate_count.reshape(2), strength, offsets, cell_index.reshape(1, PART), ambient.reshape(flat.shape), *consts)
    velocity, vorticity = pl.pallas_call(
        put_kernel,
        out_shape=(flat, flat),
        in_specs=[whole, whole],
        out_specs=(whole, whole),
        scratch_shapes=[dma((2,))],
    )(velocity, vorticity)
    return velocity.reshape(ambient.shape), vorticity.reshape(ambient.shape)


def solution(mesh):
    placed = (
        P(None, ("gz", "gx")),
        P(None, ("gz", "gx")),
        P(("gz", "gx")),
        P("gz", "gx", None),
        P(None, "gz", "gx", None),
    )
    return jax.shard_map(
        on_device,
        mesh=mesh,
        in_specs=placed,
        out_specs=(P(None, "gz", "gx", None), P(None, "gz", "gx", None)),
        check_vma=False,
    )
```

```python
import functools
import math

import jax
import jax.numpy as jnp
import ml_dtypes
import numpy as np
from jax import lax
from jax.experimental import pallas as pl
from jax.experimental.pallas import tpu as pltpu
from jax.sharding import PartitionSpec as P

MESH = pl.DeviceIdType.MESH
F32 = jnp.float32
BF16 = jnp.bfloat16
PENCILS = 4
PLANES = 8
MODES = 16
KXS = 4
NY = 256
PART = 512
CHUNKS = 6
GROUP = 9
OWN = 640
LANES = 1792
HOPS = ((1, 0, 128, 512), (1, 128, 384, 128), (-1, 0, 128, 1152), (-1, 128, 384, 1280), (2, 0, 128, 0), (-2, 0, 128, 1664))


def halves(table):
    high = table.astype(ml_dtypes.bfloat16)
    low = (table - high.astype(np.float64)).astype(ml_dtypes.bfloat16)
    return np.stack([high, low])


def real_form(angle):
    cosine, sine = np.cos(angle), np.sin(angle)
    return np.stack([np.stack([cosine, sine], -1), np.stack([-sine, cosine], -1)], -2)


def kx_of(slabs):
    base = 2 * np.arange(slabs)
    rows = np.stack([base, base + 1, -base, -base - 1], 1) % (4 * slabs)
    rows[0, 2] = 2 * slabs
    return rows


def tables(slabs):
    nx, nz = 4 * slabs, 8 * slabs
    rows = 8 * slabs
    two_pi = 2.0 * np.pi
    y = np.arange(NY)
    half, pencil, mode = np.meshgrid(np.arange(2), np.arange(PENCILS), np.arange(MODES), indexing="ij")
    ky = (pencil * 2 * MODES + half * MODES + mode).reshape(-1)
    angle = two_pi * (y[:, None] * ky[None, :] % NY) / NY
    sine = np.where(ky[None, :] == 0, (1.0 - 2.0 * (y % 2))[:, None], -np.sin(angle))
    table_y = np.concatenate([np.cos(angle), sine], 1)
    weight = np.where(ky == 0, 1.0, 2.0) / NY
    back_y = table_y.T * np.concatenate([weight, weight])[:, None]
    kx = kx_of(slabs).reshape(-1)
    x = np.arange(nx)
    form = real_form(two_pi * (kx[:, None] * x[None, :] % nx) / nx)
    form = form.reshape(nx, PENCILS, nx // PENCILS, 2, 2).transpose(0, 3, 1, 4, 2)
    table_x = form.reshape(rows, rows)
    k1 = np.arange(slabs)
    form = real_form(two_pi * (k1[:, None] * k1[None, :] % slabs) / slabs)
    table_1 = np.einsum("ksoi,ab->okasbi", form, np.eye(KXS)).reshape(rows, rows)
    k2 = np.arange(PLANES)
    form = real_form(two_pi * (k2[:, None] * k2[None, :] % PLANES) / PLANES)
    table_2 = np.einsum("kpoi,ab->ipaokb", form, np.eye(MODES)).reshape(2 * PLANES * MODES, -1)
    angle = two_pi * (k1[:, None] * k2[None, :]) / nz
    angle = np.repeat(np.repeat(angle, KXS, 0), MODES, 1)
    twiddle = np.stack([np.cos(angle), np.sin(angle)]).astype(np.float32)
    return (
        halves(table_y), halves(back_y), halves(table_x), halves(table_x.T / nx),
        halves(table_1), halves(table_1.T / nz), halves(table_2), halves(table_2.T), twiddle,
    )


def kernel_weight(distance):
    radius = jnp.abs(distance)
    near_part = 1.0 + radius * radius * (1.5 * radius - 2.5)
    beyond = 2.0 - radius
    far_part = 0.5 * beyond * beyond * (1.0 - radius)
    return jnp.where(radius < 1.0, near_part, jnp.where(radius < 2.0, far_part, 0.0))


def split(values):
    high = values.astype(BF16)
    return high, (values - high.astype(F32)).astype(BF16)


def dot(a, b):
    return jnp.dot(a, b, preferred_element_type=F32)


def table_times(table, values):
    high, low = split(values)
    width = values.shape[1]
    both = dot(table[0], jnp.concatenate([high, low], axis=1))
    return both[:, :width] + (both[:, width:] + dot(table[1], high))


def times_table(values, table):
    high, low = split(values)
    return dot(high, table[0]) + (dot(low, table[0]) + dot(high, table[1]))


def step_kernel(
    slabs, counts, strength, offsets, cells, ambient, *refs,
):
    tables_in, (vel_out, vorticity_out) = refs[:9], refs[9:11]
    (
        packet, wide_x, high_y, low_y, charge, high_l, low_l, rim, rim_in, vort, vel, vorticity,
        plane_in, side, side_in, ys, xr, xo, zr, spec, zo, xr2, xo2, yr, fixed, row_swap, lane_swap,
    ) = refs[11:38]
    tables_here = refs[38:47]
    ahead_y, back_y, ahead_x, back_x, ahead_1, back_1, ahead_2, back_2, twiddle = tables_here
    (
        send_sem, recv_sem, own_sem, packet_send, packet_recv, rim_send, rim_recv,
        plane_send, plane_recv, side_send, side_recv, load_sem, store_sem,
    ) = refs[47:]
    me_z, me_x = lax.axis_index("gz"), lax.axis_index("gx")
    nx, nz = 4 * slabs, 8 * slabs
    xl = nx // PENCILS
    half = 4 * slabs
    part = 2 * xl
    wide = PLANES * MODES

    barrier = pltpu.get_barrier_semaphore()

    def each_other_slab(act):
        group = math.gcd(slabs - 1, GROUP)

        def some(i, carry):
            for j in range(group):
                act(lax.rem(me_z + 1 + j + i * group, slabs))
            return carry

        lax.fori_loop(0, (slabs - 1) // group, some, 0)

    def greet(other):
        pl.semaphore_signal(barrier, inc=1, device_id={"gz": other}, device_id_type=MESH)

    each_other_slab(greet)
    for i in range(1, PENCILS):
        pl.semaphore_signal(barrier, inc=1, device_id={"gx": lax.rem(me_x + i, PENCILS)}, device_id_type=MESH)
    load_mesh = pltpu.make_async_copy(ambient, vort, load_sem.at[9])
    load_mesh.start()
    loads = [pltpu.make_async_copy(a, b, load_sem.at[n]) for n, (a, b) in enumerate(zip(tables_in, tables_here))]
    for copy in loads:
        copy.start()

    lane_id = lax.broadcasted_iota(jnp.int32, (1, PART), 1)
    up, down = counts[0], counts[1]
    moves = jnp.where(lane_id < up, 1, jnp.where(lane_id < up + down, -1, 0))
    cell = cells[...]
    packet[:, OWN:OWN + PART] = jnp.concatenate(
        [
            strength[...],
            offsets[...],
            (cell // (xl * NY) + PLANES * moves).astype(F32),
            (cell % (xl * NY)).astype(F32),
        ],
        axis=0,
    )

    def weigh(lo, hi):
        size = hi - lo
        fields = packet[:, lo:hi]
        lane = lax.broadcasted_iota(jnp.int32, (1, size), 1) + lo
        shift = jnp.where(lane < 128, -16.0, jnp.where(lane < OWN, -8.0, jnp.where(lane < OWN + PART, 0.0, jnp.where(lane < LANES - 128, 8.0, 16.0))))
        lateral = fields[7:8].astype(jnp.int32)
        plane = lax.broadcasted_iota(jnp.int32, (PLANES, size), 0).astype(F32)
        weight_z = kernel_weight((plane - (fields[6:7] + shift)) - fields[3:4])
        row = lax.broadcasted_iota(jnp.int32, (xl, size), 0).astype(F32)
        wide_x[:, lo:hi] = kernel_weight((row - (lateral >> 8).astype(F32)) - fields[4:5])
        at_y = lax.broadcasted_iota(jnp.int32, (NY, size), 0)
        away = ((at_y + (NY // 2 - (lateral & 255))) & 255) - NY // 2
        high, low = split(kernel_weight(away.astype(F32) - fields[5:6]))
        high_y[:, lo:hi] = high
        low_y[:, lo:hi] = low
        for c in range(3):
            charge[8 * c:8 * c + 8, lo:hi] = fields[c:c + 1] * weight_z

    pl.semaphore_wait(barrier, slabs - 1 + PENCILS - 1)

    hops = []
    for n, (far, start, width, land) in enumerate(HOPS):
        hop = pltpu.make_async_remote_copy(
            src_ref=packet.at[:, OWN + start:OWN + start + width],
            dst_ref=packet.at[:, land:land + width],
            send_sem=packet_send.at[n],
            recv_sem=packet_recv.at[n],
            device_id={"gz": lax.rem(me_z + far + slabs, slabs)},
            device_id_type=MESH,
        )
        hop.start()
        hops.append(hop)

    def send_gx(src, dst, k, stage):
        mine = pl.ds(pl.multiple_of(me_x * part, 8), part)
        for i in (2, 1, 3):
            other = lax.rem(me_x + i, PENCILS)
            pltpu.make_async_remote_copy(
                src_ref=src.at[k, pl.ds(pl.multiple_of(other * part, 8), part)],
                dst_ref=dst.at[k, mine],
                send_sem=send_sem.at[stage, k],
                recv_sem=recv_sem.at[stage, k],
                device_id={"gx": other},
                device_id_type=MESH,
            ).start()
        own_copy(src, dst, k, stage).start()

    def send_gz(src, dst, k, stage):
        mine = pl.ds(pl.multiple_of(me_z * 8, 8), 8)

        def one(other):
            pltpu.make_async_remote_copy(
                src_ref=src.at[k, pl.ds(pl.multiple_of(other * 8, 8), 8)],
                dst_ref=dst.at[k, mine],
                send_sem=send_sem.at[stage, k],
                recv_sem=recv_sem.at[stage, k],
                device_id={"gz": other},
                device_id_type=MESH,
            ).start()

        each_other_slab(one)
        own_copy(src, dst, k, stage).start()

    def own_copy(src, dst, k, stage):
        width, index = (part, me_x) if stage in (0, 3) else (8, me_z)
        at = pl.ds(pl.multiple_of(index * width, 8), width)
        return pltpu.make_async_copy(src.at[k, at], dst.at[k, at], own_sem.at[stage, k])

    def remote_rows(stage):
        return part * (PENCILS - 1) if stage in (0, 3) else 8 * (slabs - 1)

    def arrive(src, dst, k, stage):
        window = dst.at[k, pl.ds(0, remote_rows(stage))]
        pltpu.make_async_copy(window, window, recv_sem.at[stage, k]).wait()
        own_copy(src, dst, k, stage).wait()

    def sent(src, k, stage):
        window = src.at[k, pl.ds(0, remote_rows(stage))]
        pltpu.make_async_copy(window, window, send_sem.at[stage, k]).wait()

    weigh(OWN, OWN + PART)
    for hop in hops:
        hop.wait_recv()
    weigh(0, OWN)
    weigh(OWN + PART, LANES)

    def spread_over_y(high, low, lo, hi):
        def times(a, b):
            return lax.dot_general(a, b, (((1,), (1,)), ((), ())), preferred_element_type=F32)

        top = high_y[:, lo:hi]
        return times(high, top) + (times(low, top) + times(high, low_y[:, lo:hi]))

    rims = []
    x_cell = (packet[7:8, :].astype(jnp.int32) >> 8).astype(F32)
    for n, first in enumerate((xl, -2)):
        beyond = [kernel_weight((float(first + r) - x_cell) - packet[4:5, :]) for r in range(2)]
        high, low = split(jnp.concatenate([charge[8 * c:8 * c + 8, :] * beyond[r] for c in range(3) for r in range(2)], axis=0))
        rim[n] = spread_over_y(high, low, 0, LANES)
        far = 1 if n == 0 else PENCILS - 1
        copy = pltpu.make_async_remote_copy(
            src_ref=rim.at[n],
            dst_ref=rim_in.at[n],
            send_sem=rim_send.at[n],
            recv_sem=rim_recv.at[n],
            device_id={"gx": lax.rem(me_x + far, PENCILS)},
            device_id_type=MESH,
        )
        copy.start()
        rims.append(copy)
    load_mesh.wait()

    def deposit(c):
        for planes, lo, hi in ((range(0, 2), 0, 1280), (range(2, 6), 512, 1280), (range(6, 8), 512, 1792)):
            columns = wide_x[:, lo:hi]
            for n, z in enumerate(planes):
                high, low = split(columns * charge[8 * c + z:8 * c + z + 1, lo:hi])
                high_l[n * xl:(n + 1) * xl, 0:hi - lo] = high
                low_l[n * xl:(n + 1) * xl, 0:hi - lo] = low
            size = len(planes) * xl
            at = planes[0] * xl
            vort[c, at:at + size] += spread_over_y(high_l[0:size, 0:hi - lo], low_l[0:size, 0:hi - lo], lo, hi)
        if c == 0:
            for copy in rims:
                copy.wait_recv()
        for n, first in enumerate((0, xl - 2)):
            for r in range(2):
                for z in range(PLANES):
                    at = c * 16 + r * 8 + z
                    to = z * xl + first + r
                    vort[c, to:to + 1, :] += rim_in[n, at:at + 1, :]

    spot = lax.broadcasted_iota(jnp.int32, (xl, wide), 1) >> 4
    for c in range(3):
        deposit(c)
        if c == 0:
            loads[0].wait()
        modes = times_table(vort[c], ahead_y)
        for p in range(2):
            turned = []
            for z in range(PLANES):
                tile = modes[z * xl:(z + 1) * xl, p * wide:(p + 1) * wide]
                turned.append(pltpu.roll(tile, MODES * z, 1) if z else tile)
            for q in range(8):
                picked = turned[0]
                for z in range(1, PLANES):
                    picked = jnp.where(spot == (q + z) % 8, turned[z], picked)
                if q:
                    picked = pltpu.roll(picked, wide - MODES * q, 1)
                at = (q % PENCILS) * part + p * xl
                ys[3 * (q // PENCILS) + c, at:at + xl] = picked
        send_gx(ys, xr, c, 0)
    for c in range(3):
        send_gx(ys, xr, 3 + c, 0)
    loads[2].wait()
    for k in range(CHUNKS):
        arrive(ys, xr, k, 0)
        xo[k] = table_times(ahead_x, xr[k])
        send_gz(xo, zr, k, 1)
    row = lax.broadcasted_iota(jnp.int32, (half, wide), 0)
    lane = lax.broadcasted_iota(jnp.int32, (half, wide), 1)
    slot = row & 3
    k1 = row >> 2
    kz = k1 + slabs * (lane >> 4)
    kx = 2 * me_z + (slot & 1)
    kx = jnp.where(slot >= 2, -kx, kx)
    kx = jnp.where((slot == 2) & (me_z == 0), nx // 2, kx)
    wave_z = jnp.where(kz < nz // 2, kz, kz - nz).astype(F32) * (2.0 * math.pi / nz)
    wave_x = kx.astype(F32) * (2.0 * math.pi / nx)
    flat_sq = wave_z * wave_z + wave_x * wave_x
    fixed[0] = jnp.where(kz == nz // 2, 0.0, wave_z)
    fixed[1] = jnp.where(kx == nx // 2, 0.0, wave_x)
    for h in range(2):
        ky = me_x * (2 * MODES) + h * MODES + (lane & 15)
        wave_y = ky.astype(F32) * (2.0 * math.pi / NY)
        anchor = (kz == 0) & (kx == 0) & (ky == 0)
        inverse = jnp.where(anchor, 0.0, 1.0 / jnp.where(anchor, 1.0, flat_sq + wave_y * wave_y))
        fixed[2 + 2 * h] = wave_y
        if h == 0:
            packed = ky == 0
            other = 1.0 / (flat_sq + math.pi * math.pi)
            fixed[6] = jnp.where(packed, 0.5 * (inverse - other), 0.0)
            inverse = jnp.where(packed, 0.5 * (inverse + other), inverse)
        fixed[3 + 2 * h] = inverse
    fro = lax.broadcasted_iota(jnp.int32, (half, half), 1)
    to = lax.broadcasted_iota(jnp.int32, (half, half), 0)
    to_slot = to & 3
    paired_slot = jnp.where(me_z == 0, jnp.where((to_slot & 1) == 0, to_slot, 4 - to_slot), (to_slot + 2) & 3)
    mirror_row = ((slabs - (to >> 2)) & (slabs - 1)) * KXS + paired_slot
    row_swap[...] = jnp.where(fro == mirror_row, 1.0, 0.0).astype(BF16)
    fro = lax.broadcasted_iota(jnp.int32, (2 * wide, 2 * wide), 0)
    to = lax.broadcasted_iota(jnp.int32, (2 * wide, 2 * wide), 1)
    mirror_lane = (to & wide) + (PLANES - 1 - ((to & (wide - 1)) >> 4)) * MODES
    sign = jnp.where(to < wide, 1.0, -1.0)
    lane_swap[...] = jnp.where((fro == mirror_lane) & ((to & 15) == 0), sign, 0.0).astype(BF16)
    for n in (4, 6, 8, 7, 5):
        loads[n].wait()

    def to_modes(k):
        mixed = table_times(ahead_1, zr[k])
        real, imag = mixed[:half], mixed[half:]
        cos_t, sin_t = twiddle[0], twiddle[1]
        turned = jnp.concatenate([real * cos_t + imag * sin_t, imag * cos_t - real * sin_t], axis=1)
        spec[k] = times_table(turned, ahead_2)

    def from_modes(k, real, imag):
        turned = times_table(jnp.concatenate([real, imag], axis=1), back_2)
        cos_t, sin_t = twiddle[0], twiddle[1]
        real, imag = turned[:, :wide], turned[:, wide:]
        mixed = jnp.concatenate([real * cos_t - imag * sin_t, imag * cos_t + real * sin_t], axis=0)
        zo[k] = table_times(back_1, mixed)

    def mirrored(k):
        high, low = split(spec[k])
        swapped = dot(row_swap[...], high) + dot(row_swap[...], low)
        high, low = split(swapped)
        swapped = dot(high, lane_swap[...]) + dot(low, lane_swap[...])
        parts = []
        for p in range(2):
            tile = swapped[:, p * wide:(p + 1) * wide]
            parts.append(jnp.where(k1 == 0, pltpu.roll(tile, MODES, 1), tile))
        return parts

    for h in range(2):
        for c in range(3):
            k = 3 * h + c
            arrive(xo, zr, k, 1)
            to_modes(k)
            if h == 0:
                pair = mirrored(k)
                for p in range(2):
                    at = slice(p * wide, (p + 1) * wide)
                    spec[k, :, at] = fixed[3] * spec[k, :, at] + fixed[6] * pair[p]
            else:
                for p in range(2):
                    at = slice(p * wide, (p + 1) * wide)
                    spec[k, :, at] = fixed[5] * spec[k, :, at]

        def stream(c, p):
            return spec[3 * h + c, :, p * wide:(p + 1) * wide]

        def curl(c, p):
            if c == 0:
                return fixed[1] * stream(2, p) - fixed[2 + 2 * h] * stream(1, p)
            if c == 1:
                return fixed[2 + 2 * h] * stream(0, p) - fixed[0] * stream(2, p)
            return fixed[0] * stream(1, p) - fixed[1] * stream(0, p)

        for c in range(3):
            from_modes(3 * h + c, -curl(c, 1), curl(c, 0))
            send_gz(zo, xr2, 3 * h + c, 2)
    loads[3].wait()
    loads[1].wait()
    edges = [[], [], []]
    stores = []

    def back_to_x(k):
        arrive(zo, xr2, k, 2)
        xo2[k] = table_times(back_x, xr2[k])
        send_gx(xo2, yr, k, 3)

    def back_to_y(c):
        rolled = []
        for q in range(8):
            h, b = q // PENCILS, q % PENCILS
            if b == 0:
                arrive(xo2, yr, 3 * h + c, 3)
            both = []
            for p in range(2):
                at = b * part + p * xl
                tile = yr[3 * h + c, at:at + xl]
                both.append(pltpu.roll(tile, MODES * q, 1) if q else tile)
            rolled.append(both)
        planes = []
        for z in range(PLANES):
            both = []
            for p in range(2):
                picked = rolled[0][p]
                for q in range(1, 8):
                    picked = jnp.where(spot == (q + z) % 8, rolled[q][p], picked)
                both.append(pltpu.roll(picked, wide - MODES * z, 1) if z else picked)
            planes.append(jnp.concatenate(both, axis=1))
        vel[c] = times_table(jnp.concatenate(planes, axis=0), back_y)
        for n, (far, z) in enumerate(((1, PLANES - 1), (slabs - 1, 0))):
            copy = pltpu.make_async_remote_copy(
                src_ref=vel.at[c, pl.ds(z * xl, xl)],
                dst_ref=plane_in.at[n, c],
                send_sem=plane_send.at[n, c],
                recv_sem=plane_recv.at[n, c],
                device_id={"gz": lax.rem(me_z + far, slabs)},
                device_id_type=MESH,
            )
            copy.start()
            edges[c].append(copy)
        for n, (far, x) in enumerate(((1, xl - 1), (PENCILS - 1, 0))):
            side[n, c] = jnp.concatenate([vel[c, z * xl + x:z * xl + x + 1, :] for z in range(PLANES)], axis=0)
            copy = pltpu.make_async_remote_copy(
                src_ref=side.at[n, c],
                dst_ref=side_in.at[n, c],
                send_sem=side_send.at[n, c],
                recv_sem=side_recv.at[n, c],
                device_id={"gx": lax.rem(me_x + far, PENCILS)},
                device_id_type=MESH,
            )
            copy.start()
            edges[c].append(copy)
        stores.append(pltpu.make_async_copy(vel.at[c], vel_out.at[c], store_sem.at[0, c]))
        stores[-1].start()

    at_x = lax.broadcasted_iota(jnp.int32, (xl, NY), 0)

    def stretch_inside(c):
        for z in range(PLANES):
            rows = slice(z * xl, (z + 1) * xl)
            here = vel[c, rows]
            along_z = -vel[c, (z - 1) * xl:z * xl] if z > 0 else None
            if z < PLANES - 1:
                above = vel[c, (z + 1) * xl:(z + 2) * xl]
                along_z = above + along_z if z > 0 else above
            right = jnp.where(at_x == xl - 1, 0.0, pltpu.roll(here, xl - 1, 0))
            left = jnp.where(at_x == 0, 0.0, pltpu.roll(here, 1, 0))
            along_y = pltpu.roll(here, NY - 1, 1) - pltpu.roll(here, 1, 1)
            rate = vort[0, rows] * along_z + vort[1, rows] * (right - left) + vort[2, rows] * along_y
            vorticity[c, rows] = vort[c, rows] + 0.125 * rate

    def stretch_edges(c):
        for copy in edges[c]:
            copy.wait_recv()
        for n, (first, sign) in enumerate(((0, -0.125), ((PLANES - 1) * xl, 0.125))):
            rows = slice(first, first + xl)
            vorticity[c, rows] += vort[0, rows] * (sign * plane_in[n, c])
        for n, (first, sign) in enumerate(((0, -0.125), (xl - 1, 0.125))):
            for z in range(PLANES):
                at = z * xl + first
                vorticity[c, at:at + 1, :] += vort[1, at:at + 1, :] * (sign * side_in[n, c, z:z + 1, :])
        stores.append(pltpu.make_async_copy(vorticity.at[c], vorticity_out.at[c], store_sem.at[1, c]))
        stores[-1].start()

    for k in range(CHUNKS - 1):
        back_to_x(k)
    back_to_y(0)
    back_to_x(CHUNKS - 1)
    stretch_inside(0)
    back_to_y(1)
    stretch_edges(0)
    stretch_inside(1)
    back_to_y(2)
    stretch_edges(1)
    stretch_inside(2)
    stretch_edges(2)
    for copy in hops + rims + edges[0] + edges[1] + edges[2]:
        copy.wait_send()
    for k in range(CHUNKS):
        sent(ys, k, 0)
        sent(xo, k, 1)
        sent(zo, k, 2)
        sent(xo2, k, 3)
    for copy in stores:
        copy.wait()


def on_device(strength, offsets, cell_index, migrate_count, ambient):
    slabs = lax.axis_size("gz")
    xl = ambient.shape[2]
    consts = [jnp.asarray(t) for t in tables(slabs)]
    chunk = pltpu.VMEM((CHUNKS, 8 * slabs, PLANES * MODES), F32)
    mesh = pltpu.VMEM((3, PLANES * xl, NY), F32)
    dma = pltpu.SemaphoreType.DMA
    vmem = pl.BlockSpec(memory_space=pltpu.VMEM)
    whole = pl.BlockSpec(memory_space=pl.ANY)
    flat = jax.ShapeDtypeStruct((3, PLANES * xl, NY), F32)
    velocity, vorticity = pl.pallas_call(
        functools.partial(step_kernel, slabs),
        out_shape=(pltpu.VMEM(flat.shape, F32), pltpu.VMEM(flat.shape, F32)),
        in_specs=[pl.BlockSpec(memory_space=pltpu.SMEM), vmem, vmem, vmem, whole] + [whole] * len(consts),
        out_specs=(whole, whole),
        scratch_shapes=[
            pltpu.VMEM((8, LANES), F32),
            pltpu.VMEM((xl, LANES), F32),
            pltpu.VMEM((NY, LANES), BF16),
            pltpu.VMEM((NY, LANES), BF16),
            pltpu.VMEM((24, LANES), F32),
            pltpu.VMEM((4 * xl, 1280), BF16),
            pltpu.VMEM((4 * xl, 1280), BF16),
            pltpu.VMEM((2, 48, NY), F32),
            pltpu.VMEM((2, 48, NY), F32),
            mesh, mesh, mesh,
            pltpu.VMEM((2, 3, xl, NY), F32),
            pltpu.VMEM((2, 3, PLANES, NY), F32),
            pltpu.VMEM((2, 3, PLANES, NY), F32),
            chunk, chunk, chunk, chunk,
            pltpu.VMEM((CHUNKS, 4 * slabs, 2 * PLANES * MODES), F32),
            chunk, chunk, chunk, chunk,
            pltpu.VMEM((7, 4 * slabs, PLANES * MODES), F32),
            pltpu.VMEM((4 * slabs, 4 * slabs), BF16),
            pltpu.VMEM((2 * PLANES * MODES, 2 * PLANES * MODES), BF16),
            *[pltpu.VMEM(t.shape, t.dtype) for t in consts],
            dma((4, CHUNKS)), dma((4, CHUNKS)), dma((4, CHUNKS)),
            dma((6,)), dma((6,)), dma((2,)), dma((2,)),
            dma((2, 3)), dma((2, 3)), dma((2, 3)), dma((2, 3)),
            dma((10,)), dma((2, 3)),
        ],
        compiler_params=pltpu.CompilerParams(
            collective_id=0, has_side_effects=True, vmem_limit_bytes=56 * 1024 * 1024
        ),
    )(migrate_count.reshape(2), strength, offsets, cell_index.reshape(1, PART), ambient.reshape(flat.shape), *consts)
    return velocity.reshape(ambient.shape), vorticity.reshape(ambient.shape)


def solution(mesh):
    placed = (
        P(None, ("gz", "gx")),
        P(None, ("gz", "gx")),
        P(("gz", "gx")),
        P("gz", "gx", None),
        P(None, "gz", "gx", None),
    )
    return jax.shard_map(
        on_device,
        mesh=mesh,
        in_specs=placed,
        out_specs=(P(None, "gz", "gx", None), P(None, "gz", "gx", None)),
        check_vma=False,
    )
```

```python
import functools
import math

import jax
import jax.numpy as jnp
import ml_dtypes
import numpy as np
from jax import lax
from jax.experimental import pallas as pl
from jax.experimental.pallas import tpu as pltpu
from jax.sharding import PartitionSpec as P

MESH = pl.DeviceIdType.MESH
F32 = jnp.float32
BF16 = jnp.bfloat16
PENCILS = 4
PLANES = 8
MODES = 16
KXS = 4
NY = 256
PART = 512
CHUNKS = 6
GROUP = 9
BLOCK = 32
OWN = 640
LANES = 1792
HOPS = ((1, 0, 128, 512), (1, 128, 384, 128), (-1, 0, 128, 1152), (-1, 128, 384, 1280), (2, 0, 128, 0), (-2, 0, 128, 1664))


def halves(table):
    high = table.astype(ml_dtypes.bfloat16)
    low = (table - high.astype(np.float64)).astype(ml_dtypes.bfloat16)
    return np.stack([high, low])


def real_form(angle):
    cosine, sine = np.cos(angle), np.sin(angle)
    return np.stack([np.stack([cosine, sine], -1), np.stack([-sine, cosine], -1)], -2)


def kx_of(slabs):
    base = 2 * np.arange(slabs)
    rows = np.stack([base, base + 1, -base, -base - 1], 1) % (4 * slabs)
    rows[0, 2] = 2 * slabs
    return rows


def tables(slabs):
    nx, nz = 4 * slabs, 8 * slabs
    rows = 8 * slabs
    two_pi = 2.0 * np.pi
    y = np.arange(NY)
    half, pencil, mode = np.meshgrid(np.arange(2), np.arange(PENCILS), np.arange(MODES), indexing="ij")
    ky = (pencil * 2 * MODES + half * MODES + mode).reshape(-1)
    angle = two_pi * (y[:, None] * ky[None, :] % NY) / NY
    sine = np.where(ky[None, :] == 0, (1.0 - 2.0 * (y % 2))[:, None], -np.sin(angle))
    table_y = np.concatenate([np.cos(angle), sine], 1)
    weight = np.where(ky == 0, 1.0, 2.0) / NY
    back_y = table_y.T * np.concatenate([weight, weight])[:, None]
    kx = kx_of(slabs).reshape(-1)
    x = np.arange(nx)
    form = real_form(two_pi * (kx[:, None] * x[None, :] % nx) / nx)
    form = form.reshape(nx, PENCILS, nx // PENCILS, 2, 2).transpose(0, 3, 1, 4, 2)
    table_x = form.reshape(rows, rows)
    k1 = np.arange(slabs)
    form = real_form(two_pi * (k1[:, None] * k1[None, :] % slabs) / slabs)
    table_1 = np.einsum("ksoi,ab->okasbi", form, np.eye(KXS)).reshape(rows, rows)
    k2 = np.arange(PLANES)
    form = real_form(two_pi * (k2[:, None] * k2[None, :] % PLANES) / PLANES)
    table_2 = np.einsum("kpoi,ab->ipaokb", form, np.eye(MODES)).reshape(2 * PLANES * MODES, -1)
    angle = two_pi * (k1[:, None] * k2[None, :]) / nz
    angle = np.repeat(np.repeat(angle, KXS, 0), MODES, 1)
    twiddle = np.stack([np.cos(angle), np.sin(angle)]).astype(np.float32)
    return (
        halves(table_y), halves(back_y), halves(table_x), halves(table_x.T / nx),
        halves(table_1), halves(table_1.T / nz), halves(table_2), halves(table_2.T), twiddle,
    )


def kernel_weight(distance):
    radius = jnp.abs(distance)
    near_part = 1.0 + radius * radius * (1.5 * radius - 2.5)
    beyond = 2.0 - radius
    far_part = 0.5 * beyond * beyond * (1.0 - radius)
    return jnp.where(radius < 1.0, near_part, jnp.where(radius < 2.0, far_part, 0.0))


def split(values):
    if values.shape[0] > BLOCK:
        pairs = [split(values[i:i + BLOCK]) for i in range(0, values.shape[0], BLOCK)]
        return jnp.concatenate([a for a, _ in pairs], axis=0), jnp.concatenate([b for _, b in pairs], axis=0)
    high = values.astype(BF16)
    return high, (values - high.astype(F32)).astype(BF16)


def dot(a, b):
    return jnp.dot(a, b, preferred_element_type=F32)


def table_times(table, values):
    high, low = split(values)
    width = values.shape[1]
    both = dot(table[0], jnp.concatenate([high, low], axis=1))
    return both[:, :width] + (both[:, width:] + dot(table[1], high))


def times_table(values, table):
    high, low = split(values)
    return dot(high, table[0]) + (dot(low, table[0]) + dot(high, table[1]))


def step_kernel(
    slabs, counts, strength, offsets, cells, ambient, *refs,
):
    tables_in, (vel_out, vorticity_out) = refs[:9], refs[9:11]
    (
        packet, wide_x, high_y, low_y, charge, high_l, low_l, rim, rim_in, vort, vel, vorticity,
        plane_in, side, side_in, ys, xr, xo, zr, spec, zo, xr2, xo2, yr, fixed, row_swap, lane_swap,
    ) = refs[11:38]
    tables_here = refs[38:47]
    ahead_y, back_y, ahead_x, back_x, ahead_1, back_1, ahead_2, back_2, twiddle = tables_here
    (
        send_sem, recv_sem, own_sem, packet_send, packet_recv, rim_send, rim_recv,
        plane_send, plane_recv, side_send, side_recv, load_sem, store_sem,
    ) = refs[47:]
    me_z, me_x = lax.axis_index("gz"), lax.axis_index("gx")
    nx, nz = 4 * slabs, 8 * slabs
    xl = nx // PENCILS
    half = 4 * slabs
    part = 2 * xl
    wide = PLANES * MODES

    barrier = pltpu.get_barrier_semaphore()

    def each_other_slab(act):
        group = math.gcd(slabs - 1, GROUP)

        def some(i, carry):
            for j in range(group):
                act(lax.rem(me_z + 1 + j + i * group, slabs))
            return carry

        lax.fori_loop(0, (slabs - 1) // group, some, 0)

    def greet(other):
        pl.semaphore_signal(barrier, inc=1, device_id={"gz": other}, device_id_type=MESH)

    each_other_slab(greet)
    for i in range(1, PENCILS):
        pl.semaphore_signal(barrier, inc=1, device_id={"gx": lax.rem(me_x + i, PENCILS)}, device_id_type=MESH)
    load_mesh = pltpu.make_async_copy(ambient, vort, load_sem.at[9])
    load_mesh.start()
    loads = [pltpu.make_async_copy(a, b, load_sem.at[n]) for n, (a, b) in enumerate(zip(tables_in, tables_here))]
    for copy in loads:
        copy.start()

    lane_id = lax.broadcasted_iota(jnp.int32, (1, PART), 1)
    up, down = counts[0], counts[1]
    moves = jnp.where(lane_id < up, 1, jnp.where(lane_id < up + down, -1, 0))
    cell = cells[...]
    packet[:, OWN:OWN + PART] = jnp.concatenate(
        [
            strength[...],
            offsets[...],
            (cell // (xl * NY) + PLANES * moves).astype(F32),
            (cell % (xl * NY)).astype(F32),
        ],
        axis=0,
    )

    def weigh(lo, hi):
        size = hi - lo
        fields = packet[:, lo:hi]
        lane = lax.broadcasted_iota(jnp.int32, (1, size), 1) + lo
        shift = jnp.where(lane < 128, -16.0, jnp.where(lane < OWN, -8.0, jnp.where(lane < OWN + PART, 0.0, jnp.where(lane < LANES - 128, 8.0, 16.0))))
        lateral = fields[7:8].astype(jnp.int32)
        plane = lax.broadcasted_iota(jnp.int32, (PLANES, size), 0).astype(F32)
        weight_z = kernel_weight((plane - (fields[6:7] + shift)) - fields[3:4])
        x_cell = (lateral >> 8).astype(F32)
        block = min(xl, BLOCK)
        for i in range(0, xl, block):
            row = (lax.broadcasted_iota(jnp.int32, (block, size), 0) + i).astype(F32)
            wide_x[i:i + block, lo:hi] = kernel_weight((row - x_cell) - fields[4:5])
        start = NY // 2 - (lateral & 255)
        for i in range(0, NY, 16):
            at_y = lax.broadcasted_iota(jnp.int32, (16, size), 0) + i
            away = ((at_y + start) & 255) - NY // 2
            high, low = split(kernel_weight(away.astype(F32) - fields[5:6]))
            high_y[i:i + 16, lo:hi] = high
            low_y[i:i + 16, lo:hi] = low
        for c in range(3):
            charge[8 * c:8 * c + 8, lo:hi] = fields[c:c + 1] * weight_z

    pl.semaphore_wait(barrier, slabs - 1 + PENCILS - 1)

    hops = []
    for n, (far, start, width, land) in enumerate(HOPS):
        hop = pltpu.make_async_remote_copy(
            src_ref=packet.at[:, OWN + start:OWN + start + width],
            dst_ref=packet.at[:, land:land + width],
            send_sem=packet_send.at[n],
            recv_sem=packet_recv.at[n],
            device_id={"gz": lax.rem(me_z + far + slabs, slabs)},
            device_id_type=MESH,
        )
        hop.start()
        hops.append(hop)

    def send_gx(src, dst, k, stage):
        mine = pl.ds(pl.multiple_of(me_x * part, 8), part)
        for i in (2, 1, 3):
            other = lax.rem(me_x + i, PENCILS)
            pltpu.make_async_remote_copy(
                src_ref=src.at[k, pl.ds(pl.multiple_of(other * part, 8), part)],
                dst_ref=dst.at[k, mine],
                send_sem=send_sem.at[stage, k],
                recv_sem=recv_sem.at[stage, k],
                device_id={"gx": other},
                device_id_type=MESH,
            ).start()
        own_copy(src, dst, k, stage).start()

    def send_gz(src, dst, k, stage):
        mine = pl.ds(pl.multiple_of(me_z * 8, 8), 8)

        def one(other):
            pltpu.make_async_remote_copy(
                src_ref=src.at[k, pl.ds(pl.multiple_of(other * 8, 8), 8)],
                dst_ref=dst.at[k, mine],
                send_sem=send_sem.at[stage, k],
                recv_sem=recv_sem.at[stage, k],
                device_id={"gz": other},
                device_id_type=MESH,
            ).start()

        each_other_slab(one)
        own_copy(src, dst, k, stage).start()

    def own_copy(src, dst, k, stage):
        width, index = (part, me_x) if stage in (0, 3) else (8, me_z)
        at = pl.ds(pl.multiple_of(index * width, 8), width)
        return pltpu.make_async_copy(src.at[k, at], dst.at[k, at], own_sem.at[stage, k])

    def remote_rows(stage):
        return part * (PENCILS - 1) if stage in (0, 3) else 8 * (slabs - 1)

    def arrive(src, dst, k, stage):
        window = dst.at[k, pl.ds(0, remote_rows(stage))]
        pltpu.make_async_copy(window, window, recv_sem.at[stage, k]).wait()
        own_copy(src, dst, k, stage).wait()

    def sent(src, k, stage):
        window = src.at[k, pl.ds(0, remote_rows(stage))]
        pltpu.make_async_copy(window, window, send_sem.at[stage, k]).wait()

    weigh(OWN, OWN + PART)
    for hop in hops:
        hop.wait_recv()
    weigh(0, OWN)
    weigh(OWN + PART, LANES)

    def spread_over_y(high, low, lo, hi):
        def times(a, b):
            return lax.dot_general(a, b, (((1,), (1,)), ((), ())), preferred_element_type=F32)

        top = high_y[:, lo:hi]
        return times(high, top) + (times(low, top) + times(high, low_y[:, lo:hi]))

    rims = []
    x_cell = (packet[7:8, :].astype(jnp.int32) >> 8).astype(F32)
    for n, first in enumerate((xl, -2)):
        beyond = [kernel_weight((float(first + r) - x_cell) - packet[4:5, :]) for r in range(2)]
        high, low = split(jnp.concatenate([charge[8 * c:8 * c + 8, :] * beyond[r] for c in range(3) for r in range(2)], axis=0))
        rim[n] = spread_over_y(high, low, 0, LANES)
        far = 1 if n == 0 else PENCILS - 1
        copy = pltpu.make_async_remote_copy(
            src_ref=rim.at[n],
            dst_ref=rim_in.at[n],
            send_sem=rim_send.at[n],
            recv_sem=rim_recv.at[n],
            device_id={"gx": lax.rem(me_x + far, PENCILS)},
            device_id_type=MESH,
        )
        copy.start()
        rims.append(copy)
    load_mesh.wait()

    def deposit(c):
        for planes, lo, hi in ((range(0, 2), 0, 1280), (range(2, 6), 512, 1280), (range(6, 8), 512, 1792)):
            block = min(xl, 16)
            for i in range(0, xl, block):
                columns = wide_x[i:i + block, lo:hi]
                for n, z in enumerate(planes):
                    high, low = split(columns * charge[8 * c + z:8 * c + z + 1, lo:hi])
                    at = n * xl + i
                    high_l[at:at + block, 0:hi - lo] = high
                    low_l[at:at + block, 0:hi - lo] = low
            size = len(planes) * xl
            at = planes[0] * xl
            vort[c, at:at + size] += spread_over_y(high_l[0:size, 0:hi - lo], low_l[0:size, 0:hi - lo], lo, hi)
        if c == 0:
            for copy in rims:
                copy.wait_recv()
        for n, first in enumerate((0, xl - 2)):
            for r in range(2):
                for z in range(PLANES):
                    at = c * 16 + r * 8 + z
                    to = z * xl + first + r
                    vort[c, to:to + 1, :] += rim_in[n, at:at + 1, :]

    band = min(xl, 8)
    spot = lax.broadcasted_iota(jnp.int32, (band, wide), 1) >> 4
    for c in range(3):
        deposit(c)
        if c == 0:
            loads[0].wait()
        vel[c] = times_table(vort[c], ahead_y)
        for p in range(2):
            for i in range(0, xl, band):
                turned = []
                for z in range(PLANES):
                    tile = vel[c, z * xl + i:z * xl + i + band, p * wide:(p + 1) * wide]
                    turned.append(pltpu.roll(tile, MODES * z, 1) if z else tile)
                for q in range(8):
                    picked = turned[0]
                    for z in range(1, PLANES):
                        picked = jnp.where(spot == (q + z) % 8, turned[z], picked)
                    if q:
                        picked = pltpu.roll(picked, wide - MODES * q, 1)
                    at = (q % PENCILS) * part + p * xl + i
                    ys[3 * (q // PENCILS) + c, at:at + band] = picked
        send_gx(ys, xr, c, 0)
    for c in range(3):
        send_gx(ys, xr, 3 + c, 0)
    loads[2].wait()
    for k in range(CHUNKS):
        arrive(ys, xr, k, 0)
        xo[k] = table_times(ahead_x, xr[k])
        send_gz(xo, zr, k, 1)
    row = lax.broadcasted_iota(jnp.int32, (half, wide), 0)
    lane = lax.broadcasted_iota(jnp.int32, (half, wide), 1)
    slot = row & 3
    k1 = row >> 2
    kz = k1 + slabs * (lane >> 4)
    kx = 2 * me_z + (slot & 1)
    kx = jnp.where(slot >= 2, -kx, kx)
    kx = jnp.where((slot == 2) & (me_z == 0), nx // 2, kx)
    wave_z = jnp.where(kz < nz // 2, kz, kz - nz).astype(F32) * (2.0 * math.pi / nz)
    wave_x = kx.astype(F32) * (2.0 * math.pi / nx)
    flat_sq = wave_z * wave_z + wave_x * wave_x
    fixed[0] = jnp.where(kz == nz // 2, 0.0, wave_z)
    fixed[1] = jnp.where(kx == nx // 2, 0.0, wave_x)
    for h in range(2):
        ky = me_x * (2 * MODES) + h * MODES + (lane & 15)
        wave_y = ky.astype(F32) * (2.0 * math.pi / NY)
        anchor = (kz == 0) & (kx == 0) & (ky == 0)
        inverse = jnp.where(anchor, 0.0, 1.0 / jnp.where(anchor, 1.0, flat_sq + wave_y * wave_y))
        fixed[2 + 2 * h] = wave_y
        if h == 0:
            packed = ky == 0
            other = 1.0 / (flat_sq + math.pi * math.pi)
            fixed[6] = jnp.where(packed, 0.5 * (inverse - other), 0.0)
            inverse = jnp.where(packed, 0.5 * (inverse + other), inverse)
        fixed[3 + 2 * h] = inverse
    fro = lax.broadcasted_iota(jnp.int32, (half, half), 1)
    to = lax.broadcasted_iota(jnp.int32, (half, half), 0)
    to_slot = to & 3
    paired_slot = jnp.where(me_z == 0, jnp.where((to_slot & 1) == 0, to_slot, 4 - to_slot), (to_slot + 2) & 3)
    mirror_row = ((slabs - (to >> 2)) & (slabs - 1)) * KXS + paired_slot
    row_swap[...] = jnp.where(fro == mirror_row, 1.0, 0.0).astype(BF16)
    fro = lax.broadcasted_iota(jnp.int32, (2 * wide, 2 * wide), 0)
    to = lax.broadcasted_iota(jnp.int32, (2 * wide, 2 * wide), 1)
    mirror_lane = (to & wide) + (PLANES - 1 - ((to & (wide - 1)) >> 4)) * MODES
    sign = jnp.where(to < wide, 1.0, -1.0)
    lane_swap[...] = jnp.where((fro == mirror_lane) & ((to & 15) == 0), sign, 0.0).astype(BF16)
    for n in (4, 6, 8, 7, 5):
        loads[n].wait()

    def to_modes(k):
        mixed = table_times(ahead_1, zr[k])
        real, imag = mixed[:half], mixed[half:]
        cos_t, sin_t = twiddle[0], twiddle[1]
        turned = jnp.concatenate([real * cos_t + imag * sin_t, imag * cos_t - real * sin_t], axis=1)
        spec[k] = times_table(turned, ahead_2)

    def from_modes(k, real, imag):
        turned = times_table(jnp.concatenate([real, imag], axis=1), back_2)
        cos_t, sin_t = twiddle[0], twiddle[1]
        real, imag = turned[:, :wide], turned[:, wide:]
        mixed = jnp.concatenate([real * cos_t - imag * sin_t, imag * cos_t + real * sin_t], axis=0)
        zo[k] = table_times(back_1, mixed)

    def mirrored(k):
        high, low = split(spec[k])
        swapped = dot(row_swap[...], high) + dot(row_swap[...], low)
        high, low = split(swapped)
        swapped = dot(high, lane_swap[...]) + dot(low, lane_swap[...])
        parts = []
        for p in range(2):
            tile = swapped[:, p * wide:(p + 1) * wide]
            parts.append(jnp.where(k1 == 0, pltpu.roll(tile, MODES, 1), tile))
        return parts

    for h in range(2):
        for c in range(3):
            k = 3 * h + c
            arrive(xo, zr, k, 1)
            to_modes(k)
            if h == 0:
                pair = mirrored(k)
                for p in range(2):
                    at = slice(p * wide, (p + 1) * wide)
                    spec[k, :, at] = fixed[3] * spec[k, :, at] + fixed[6] * pair[p]
            else:
                for p in range(2):
                    at = slice(p * wide, (p + 1) * wide)
                    spec[k, :, at] = fixed[5] * spec[k, :, at]

        def stream(c, p):
            return spec[3 * h + c, :, p * wide:(p + 1) * wide]

        def curl(c, p):
            if c == 0:
                return fixed[1] * stream(2, p) - fixed[2 + 2 * h] * stream(1, p)
            if c == 1:
                return fixed[2 + 2 * h] * stream(0, p) - fixed[0] * stream(2, p)
            return fixed[0] * stream(1, p) - fixed[1] * stream(0, p)

        for c in range(3):
            from_modes(3 * h + c, -curl(c, 1), curl(c, 0))
            send_gz(zo, xr2, 3 * h + c, 2)
    loads[3].wait()
    loads[1].wait()
    edges = [[], [], []]
    stores = []

    def back_to_x(k):
        arrive(zo, xr2, k, 2)
        xo2[k] = table_times(back_x, xr2[k])
        send_gx(xo2, yr, k, 3)

    def back_to_y(c):
        arrive(xo2, yr, c, 3)
        arrive(xo2, yr, 3 + c, 3)
        for p in range(2):
            for i in range(0, xl, band):
                turned = []
                for q in range(8):
                    at = (q % PENCILS) * part + p * xl + i
                    tile = yr[3 * (q // PENCILS) + c, at:at + band]
                    turned.append(pltpu.roll(tile, MODES * q, 1) if q else tile)
                for z in range(PLANES):
                    picked = turned[0]
                    for q in range(1, 8):
                        picked = jnp.where(spot == (q + z) % 8, turned[q], picked)
                    if z:
                        picked = pltpu.roll(picked, wide - MODES * z, 1)
                    vel[c, z * xl + i:z * xl + i + band, p * wide:(p + 1) * wide] = picked
        vel[c] = times_table(vel[c], back_y)
        for n, (far, z) in enumerate(((1, PLANES - 1), (slabs - 1, 0))):
            copy = pltpu.make_async_remote_copy(
                src_ref=vel.at[c, pl.ds(z * xl, xl)],
                dst_ref=plane_in.at[n, c],
                send_sem=plane_send.at[n, c],
                recv_sem=plane_recv.at[n, c],
                device_id={"gz": lax.rem(me_z + far, slabs)},
                device_id_type=MESH,
            )
            copy.start()
            edges[c].append(copy)
        for n, (far, x) in enumerate(((1, xl - 1), (PENCILS - 1, 0))):
            side[n, c] = jnp.concatenate([vel[c, z * xl + x:z * xl + x + 1, :] for z in range(PLANES)], axis=0)
            copy = pltpu.make_async_remote_copy(
                src_ref=side.at[n, c],
                dst_ref=side_in.at[n, c],
                send_sem=side_send.at[n, c],
                recv_sem=side_recv.at[n, c],
                device_id={"gx": lax.rem(me_x + far, PENCILS)},
                device_id_type=MESH,
            )
            copy.start()
            edges[c].append(copy)
        stores.append(pltpu.make_async_copy(vel.at[c], vel_out.at[c], store_sem.at[0, c]))
        stores[-1].start()

    at_x = lax.broadcasted_iota(jnp.int32, (xl, NY), 0)

    def stretch_inside(c):
        for z in range(PLANES):
            rows = slice(z * xl, (z + 1) * xl)
            here = vel[c, rows]
            along_z = -vel[c, (z - 1) * xl:z * xl] if z > 0 else None
            if z < PLANES - 1:
                above = vel[c, (z + 1) * xl:(z + 2) * xl]
                along_z = above + along_z if z > 0 else above
            right = jnp.where(at_x == xl - 1, 0.0, pltpu.roll(here, xl - 1, 0))
            left = jnp.where(at_x == 0, 0.0, pltpu.roll(here, 1, 0))
            along_y = pltpu.roll(here, NY - 1, 1) - pltpu.roll(here, 1, 1)
            rate = vort[0, rows] * along_z + vort[1, rows] * (right - left) + vort[2, rows] * along_y
            vorticity[c, rows] = vort[c, rows] + 0.125 * rate

    def stretch_edges(c):
        for copy in edges[c]:
            copy.wait_recv()
        for n, (first, sign) in enumerate(((0, -0.125), ((PLANES - 1) * xl, 0.125))):
            rows = slice(first, first + xl)
            vorticity[c, rows] += vort[0, rows] * (sign * plane_in[n, c])
        for n, (first, sign) in enumerate(((0, -0.125), (xl - 1, 0.125))):
            for z in range(PLANES):
                at = z * xl + first
                vorticity[c, at:at + 1, :] += vort[1, at:at + 1, :] * (sign * side_in[n, c, z:z + 1, :])
        stores.append(pltpu.make_async_copy(vorticity.at[c], vorticity_out.at[c], store_sem.at[1, c]))
        stores[-1].start()

    for k in range(CHUNKS - 1):
        back_to_x(k)
    back_to_y(0)
    back_to_x(CHUNKS - 1)
    stretch_inside(0)
    back_to_y(1)
    stretch_edges(0)
    stretch_inside(1)
    back_to_y(2)
    stretch_edges(1)
    stretch_inside(2)
    stretch_edges(2)
    for copy in hops + rims + edges[0] + edges[1] + edges[2]:
        copy.wait_send()
    for k in range(CHUNKS):
        sent(ys, k, 0)
        sent(xo, k, 1)
        sent(zo, k, 2)
        sent(xo2, k, 3)
    for copy in stores:
        copy.wait()


def on_device(strength, offsets, cell_index, migrate_count, ambient):
    slabs = lax.axis_size("gz")
    xl = ambient.shape[2]
    consts = [jnp.asarray(t) for t in tables(slabs)]
    chunk = pltpu.VMEM((CHUNKS, 8 * slabs, PLANES * MODES), F32)
    mesh = pltpu.VMEM((3, PLANES * xl, NY), F32)
    dma = pltpu.SemaphoreType.DMA
    vmem = pl.BlockSpec(memory_space=pltpu.VMEM)
    whole = pl.BlockSpec(memory_space=pl.ANY)
    flat = jax.ShapeDtypeStruct((3, PLANES * xl, NY), F32)
    velocity, vorticity = pl.pallas_call(
        functools.partial(step_kernel, slabs),
        out_shape=(pltpu.VMEM(flat.shape, F32), pltpu.VMEM(flat.shape, F32)),
        in_specs=[pl.BlockSpec(memory_space=pltpu.SMEM), vmem, vmem, vmem, whole] + [whole] * len(consts),
        out_specs=(whole, whole),
        scratch_shapes=[
            pltpu.VMEM((8, LANES), F32),
            pltpu.VMEM((xl, LANES), F32),
            pltpu.VMEM((NY, LANES), BF16),
            pltpu.VMEM((NY, LANES), BF16),
            pltpu.VMEM((24, LANES), F32),
            pltpu.VMEM((4 * xl, 1280), BF16),
            pltpu.VMEM((4 * xl, 1280), BF16),
            pltpu.VMEM((2, 48, NY), F32),
            pltpu.VMEM((2, 48, NY), F32),
            mesh, mesh, mesh,
            pltpu.VMEM((2, 3, xl, NY), F32),
            pltpu.VMEM((2, 3, PLANES, NY), F32),
            pltpu.VMEM((2, 3, PLANES, NY), F32),
            chunk, chunk, chunk, chunk,
            pltpu.VMEM((CHUNKS, 4 * slabs, 2 * PLANES * MODES), F32),
            chunk, chunk, chunk, chunk,
            pltpu.VMEM((7, 4 * slabs, PLANES * MODES), F32),
            pltpu.VMEM((4 * slabs, 4 * slabs), BF16),
            pltpu.VMEM((2 * PLANES * MODES, 2 * PLANES * MODES), BF16),
            *[pltpu.VMEM(t.shape, t.dtype) for t in consts],
            dma((4, CHUNKS)), dma((4, CHUNKS)), dma((4, CHUNKS)),
            dma((6,)), dma((6,)), dma((2,)), dma((2,)),
            dma((2, 3)), dma((2, 3)), dma((2, 3)), dma((2, 3)),
            dma((10,)), dma((2, 3)),
        ],
        compiler_params=pltpu.CompilerParams(
            collective_id=0, has_side_effects=True, vmem_limit_bytes=56 * 1024 * 1024
        ),
    )(migrate_count.reshape(2), strength, offsets, cell_index.reshape(1, PART), ambient.reshape(flat.shape), *consts)
    return velocity.reshape(ambient.shape), vorticity.reshape(ambient.shape)


def solution(mesh):
    placed = (
        P(None, ("gz", "gx")),
        P(None, ("gz", "gx")),
        P(("gz", "gx")),
        P("gz", "gx", None),
        P(None, "gz", "gx", None),
    )
    return jax.shard_map(
        on_device,
        mesh=mesh,
        in_specs=placed,
        out_specs=(P(None, "gz", "gx", None), P(None, "gz", "gx", None)),
        check_vma=False,
    )
```

```python
import functools
import math

import jax
import jax.numpy as jnp
import ml_dtypes
import numpy as np
from jax import lax
from jax.experimental import pallas as pl
from jax.experimental.pallas import tpu as pltpu
from jax.sharding import PartitionSpec as P

MESH = pl.DeviceIdType.MESH
F32 = jnp.float32
BF16 = jnp.bfloat16
PENCILS = 4
PLANES = 8
MODES = 16
KXS = 4
NY = 256
PART = 512
CHUNKS = 6
GROUP = 9
BLOCK = 32
OWN = 640
LANES = 1792
HOPS = ((1, 0, 128, 512), (1, 128, 384, 128), (-1, 0, 128, 1152), (-1, 128, 384, 1280), (2, 0, 128, 0), (-2, 0, 128, 1664))


def halves(table):
    high = table.astype(ml_dtypes.bfloat16)
    low = (table - high.astype(np.float64)).astype(ml_dtypes.bfloat16)
    return np.stack([high, low])


def real_form(angle):
    cosine, sine = np.cos(angle), np.sin(angle)
    return np.stack([np.stack([cosine, sine], -1), np.stack([-sine, cosine], -1)], -2)


def kx_of(slabs):
    base = 2 * np.arange(slabs)
    rows = np.stack([base, base + 1, -base, -base - 1], 1) % (4 * slabs)
    rows[0, 2] = 2 * slabs
    return rows


def tables(slabs):
    nx, nz = 4 * slabs, 8 * slabs
    rows = 8 * slabs
    two_pi = 2.0 * np.pi
    y = np.arange(NY)
    half, pencil, mode = np.meshgrid(np.arange(2), np.arange(PENCILS), np.arange(MODES), indexing="ij")
    ky = (pencil * 2 * MODES + half * MODES + mode).reshape(-1)
    angle = two_pi * (y[:, None] * ky[None, :] % NY) / NY
    sine = np.where(ky[None, :] == 0, (1.0 - 2.0 * (y % 2))[:, None], -np.sin(angle))
    table_y = np.concatenate([np.cos(angle), sine], 1)
    weight = np.where(ky == 0, 1.0, 2.0) / NY
    back_y = table_y.T * np.concatenate([weight, weight])[:, None]
    kx = kx_of(slabs).reshape(-1)
    x = np.arange(nx)
    form = real_form(two_pi * (kx[:, None] * x[None, :] % nx) / nx)
    form = form.reshape(nx, PENCILS, nx // PENCILS, 2, 2).transpose(0, 3, 1, 4, 2)
    table_x = form.reshape(rows, rows)
    k1 = np.arange(slabs)
    form = real_form(two_pi * (k1[:, None] * k1[None, :] % slabs) / slabs)
    table_1 = np.einsum("ksoi,ab->okasbi", form, np.eye(KXS)).reshape(rows, rows)
    k2 = np.arange(PLANES)
    form = real_form(two_pi * (k2[:, None] * k2[None, :] % PLANES) / PLANES)
    table_2 = np.einsum("kpoi,ab->ipaokb", form, np.eye(MODES)).reshape(2 * PLANES * MODES, -1)
    angle = two_pi * (k1[:, None] * k2[None, :]) / nz
    angle = np.repeat(np.repeat(angle, KXS, 0), MODES, 1)
    twiddle = np.stack([np.cos(angle), np.sin(angle)]).astype(np.float32)
    return (
        halves(table_y), halves(back_y), halves(table_x), halves(table_x.T / nx),
        halves(table_1), halves(table_1.T / nz), halves(table_2), halves(table_2.T), twiddle,
    )


def kernel_weight(distance):
    radius = jnp.abs(distance)
    near_part = 1.0 + radius * radius * (1.5 * radius - 2.5)
    beyond = 2.0 - radius
    far_part = 0.5 * beyond * beyond * (1.0 - radius)
    return jnp.where(radius < 1.0, near_part, jnp.where(radius < 2.0, far_part, 0.0))


def split(values):
    if values.shape[0] > BLOCK:
        pairs = [split(values[i:i + BLOCK]) for i in range(0, values.shape[0], BLOCK)]
        return jnp.concatenate([a for a, _ in pairs], axis=0), jnp.concatenate([b for _, b in pairs], axis=0)
    high = values.astype(BF16)
    return high, (values - high.astype(F32)).astype(BF16)


def dot(a, b):
    return jnp.dot(a, b, preferred_element_type=F32)


def table_times(table, values):
    high, low = split(values)
    width = values.shape[1]
    both = dot(table[0], jnp.concatenate([high, low], axis=1))
    return both[:, :width] + (both[:, width:] + dot(table[1], high))


def times_table(values, table):
    high, low = split(values)
    return dot(high, table[0]) + (dot(low, table[0]) + dot(high, table[1]))


def step_kernel(
    slabs, counts, strength, offsets, cells, ambient, *refs,
):
    tables_in, (vel_out, vorticity_out) = refs[:9], refs[9:11]
    (
        packet, wide_x, high_y, low_y, charge, high_l, low_l, rim, rim_in, vort, vel, vorticity,
        plane_in, side, side_in, ys, xr, xo, zr, spec, zo, xr2, xo2, yr, fixed, row_swap, lane_swap,
    ) = refs[11:38]
    tables_here = refs[38:47]
    ahead_y, back_y, ahead_x, back_x, ahead_1, back_1, ahead_2, back_2, twiddle = tables_here
    (
        send_sem, recv_sem, own_sem, packet_send, packet_recv, rim_send, rim_recv,
        plane_send, plane_recv, side_send, side_recv, load_sem, store_sem,
    ) = refs[47:]
    me_z, me_x = lax.axis_index("gz"), lax.axis_index("gx")
    nx, nz = 4 * slabs, 8 * slabs
    xl = nx // PENCILS
    half = 4 * slabs
    part = 2 * xl
    wide = PLANES * MODES

    barrier = pltpu.get_barrier_semaphore()

    def each_other_slab(act):
        group = math.gcd(slabs - 1, GROUP)

        def some(i, carry):
            for j in range(group):
                act(lax.rem(me_z + 1 + j + i * group, slabs))
            return carry

        lax.fori_loop(0, (slabs - 1) // group, some, 0)

    def greet(other):
        pl.semaphore_signal(barrier, inc=1, device_id={"gz": other}, device_id_type=MESH)

    each_other_slab(greet)
    for i in range(1, PENCILS):
        pl.semaphore_signal(barrier, inc=1, device_id={"gx": lax.rem(me_x + i, PENCILS)}, device_id_type=MESH)
    load_mesh = pltpu.make_async_copy(ambient, vort, load_sem.at[9])
    loads = [pltpu.make_async_copy(a, b, load_sem.at[n]) for n, (a, b) in enumerate(zip(tables_in, tables_here))]

    lane_id = lax.broadcasted_iota(jnp.int32, (1, PART), 1)
    up, down = counts[0], counts[1]
    moves = jnp.where(lane_id < up, 1, jnp.where(lane_id < up + down, -1, 0))
    cell = cells[...]
    packet[:, OWN:OWN + PART] = jnp.concatenate(
        [
            strength[...],
            offsets[...],
            (cell // (xl * NY) + PLANES * moves).astype(F32),
            (cell % (xl * NY)).astype(F32),
        ],
        axis=0,
    )

    def weigh(lo, hi):
        size = hi - lo
        fields = packet[:, lo:hi]
        lane = lax.broadcasted_iota(jnp.int32, (1, size), 1) + lo
        shift = jnp.where(lane < 128, -16.0, jnp.where(lane < OWN, -8.0, jnp.where(lane < OWN + PART, 0.0, jnp.where(lane < LANES - 128, 8.0, 16.0))))
        lateral = fields[7:8].astype(jnp.int32)
        plane = lax.broadcasted_iota(jnp.int32, (PLANES, size), 0).astype(F32)
        weight_z = kernel_weight((plane - (fields[6:7] + shift)) - fields[3:4])
        x_cell = (lateral >> 8).astype(F32)
        block = min(xl, BLOCK)
        for i in range(0, xl, block):
            row = (lax.broadcasted_iota(jnp.int32, (block, size), 0) + i).astype(F32)
            wide_x[i:i + block, lo:hi] = kernel_weight((row - x_cell) - fields[4:5])
        start = NY // 2 - (lateral & 255)
        for i in range(0, NY, 16):
            at_y = lax.broadcasted_iota(jnp.int32, (16, size), 0) + i
            away = ((at_y + start) & 255) - NY // 2
            high, low = split(kernel_weight(away.astype(F32) - fields[5:6]))
            high_y[i:i + 16, lo:hi] = high
            low_y[i:i + 16, lo:hi] = low
        for c in range(3):
            charge[8 * c:8 * c + 8, lo:hi] = fields[c:c + 1] * weight_z

    pl.semaphore_wait(barrier, slabs - 1 + PENCILS - 1)

    hops = []
    for n, (far, start, width, land) in enumerate(HOPS):
        hop = pltpu.make_async_remote_copy(
            src_ref=packet.at[:, OWN + start:OWN + start + width],
            dst_ref=packet.at[:, land:land + width],
            send_sem=packet_send.at[n],
            recv_sem=packet_recv.at[n],
            device_id={"gz": lax.rem(me_z + far + slabs, slabs)},
            device_id_type=MESH,
        )
        hop.start()
        hops.append(hop)

    def send_gx(src, dst, k, stage):
        mine = pl.ds(pl.multiple_of(me_x * part, 8), part)
        for i in (2, 1, 3):
            other = lax.rem(me_x + i, PENCILS)
            pltpu.make_async_remote_copy(
                src_ref=src.at[k, pl.ds(pl.multiple_of(other * part, 8), part)],
                dst_ref=dst.at[k, mine],
                send_sem=send_sem.at[stage, k],
                recv_sem=recv_sem.at[stage, k],
                device_id={"gx": other},
                device_id_type=MESH,
            ).start()
        own_copy(src, dst, k, stage).start()

    def send_gz(src, dst, k, stage):
        mine = pl.ds(pl.multiple_of(me_z * 8, 8), 8)

        def one(other):
            pltpu.make_async_remote_copy(
                src_ref=src.at[k, pl.ds(pl.multiple_of(other * 8, 8), 8)],
                dst_ref=dst.at[k, mine],
                send_sem=send_sem.at[stage, k],
                recv_sem=recv_sem.at[stage, k],
                device_id={"gz": other},
                device_id_type=MESH,
            ).start()

        each_other_slab(one)
        own_copy(src, dst, k, stage).start()

    def own_copy(src, dst, k, stage):
        width, index = (part, me_x) if stage in (0, 3) else (8, me_z)
        at = pl.ds(pl.multiple_of(index * width, 8), width)
        return pltpu.make_async_copy(src.at[k, at], dst.at[k, at], own_sem.at[stage, k])

    def remote_rows(stage):
        return part * (PENCILS - 1) if stage in (0, 3) else 8 * (slabs - 1)

    def arrive(src, dst, k, stage):
        window = dst.at[k, pl.ds(0, remote_rows(stage))]
        pltpu.make_async_copy(window, window, recv_sem.at[stage, k]).wait()
        own_copy(src, dst, k, stage).wait()

    def sent(src, k, stage):
        window = src.at[k, pl.ds(0, remote_rows(stage))]
        pltpu.make_async_copy(window, window, send_sem.at[stage, k]).wait()

    load_mesh.start()
    loads[0].start()
    weigh(OWN, OWN + PART)
    for hop in hops:
        hop.wait_recv()
    weigh(0, OWN)
    weigh(OWN + PART, LANES)

    def spread_over_y(high, low, lo, hi):
        def times(a, b):
            return lax.dot_general(a, b, (((1,), (1,)), ((), ())), preferred_element_type=F32)

        top = high_y[:, lo:hi]
        return times(high, top) + (times(low, top) + times(high, low_y[:, lo:hi]))

    rims = []
    x_cell = (packet[7:8, :].astype(jnp.int32) >> 8).astype(F32)
    for n, first in enumerate((xl, -2)):
        beyond = [kernel_weight((float(first + r) - x_cell) - packet[4:5, :]) for r in range(2)]
        high, low = split(jnp.concatenate([charge[8 * c:8 * c + 8, :] * beyond[r] for c in range(3) for r in range(2)], axis=0))
        rim[n] = spread_over_y(high, low, 0, LANES)
        far = 1 if n == 0 else PENCILS - 1
        copy = pltpu.make_async_remote_copy(
            src_ref=rim.at[n],
            dst_ref=rim_in.at[n],
            send_sem=rim_send.at[n],
            recv_sem=rim_recv.at[n],
            device_id={"gx": lax.rem(me_x + far, PENCILS)},
            device_id_type=MESH,
        )
        copy.start()
        rims.append(copy)
    load_mesh.wait()
    for n in (2, 4, 6, 8, 7, 5, 3, 1):
        loads[n].start()

    def deposit(c):
        for planes, lo, hi in ((range(0, 2), 0, 1280), (range(2, 6), 512, 1280), (range(6, 8), 512, 1792)):
            block = min(xl, 16)
            for i in range(0, xl, block):
                columns = wide_x[i:i + block, lo:hi]
                for n, z in enumerate(planes):
                    high, low = split(columns * charge[8 * c + z:8 * c + z + 1, lo:hi])
                    at = n * xl + i
                    high_l[at:at + block, 0:hi - lo] = high
                    low_l[at:at + block, 0:hi - lo] = low
            size = len(planes) * xl
            at = planes[0] * xl
            vort[c, at:at + size] += spread_over_y(high_l[0:size, 0:hi - lo], low_l[0:size, 0:hi - lo], lo, hi)
        if c == 0:
            for copy in rims:
                copy.wait_recv()
        for n, first in enumerate((0, xl - 2)):
            for r in range(2):
                for z in range(PLANES):
                    at = c * 16 + r * 8 + z
                    to = z * xl + first + r
                    vort[c, to:to + 1, :] += rim_in[n, at:at + 1, :]

    def to_x(k):
        if k == 0:
            loads[2].wait()
        arrive(ys, xr, k, 0)
        xo[k] = table_times(ahead_x, xr[k])
        send_gz(xo, zr, k, 1)

    band = min(xl, 8)
    spot = lax.broadcasted_iota(jnp.int32, (band, wide), 1) >> 4
    for c in range(3):
        deposit(c)
        if c == 0:
            loads[0].wait()
        vel[c] = times_table(vort[c], ahead_y)
        for p in range(2):
            for i in range(0, xl, band):
                turned = []
                for z in range(PLANES):
                    tile = vel[c, z * xl + i:z * xl + i + band, p * wide:(p + 1) * wide]
                    turned.append(pltpu.roll(tile, MODES * z, 1) if z else tile)
                for q in range(8):
                    picked = turned[0]
                    for z in range(1, PLANES):
                        picked = jnp.where(spot == (q + z) % 8, turned[z], picked)
                    if q:
                        picked = pltpu.roll(picked, wide - MODES * q, 1)
                    at = (q % PENCILS) * part + p * xl + i
                    ys[3 * (q // PENCILS) + c, at:at + band] = picked
        send_gx(ys, xr, c, 0)
        if c == 1:
            to_x(0)
    for c in range(3):
        send_gx(ys, xr, 3 + c, 0)
    for k in range(1, CHUNKS):
        to_x(k)
    row = lax.broadcasted_iota(jnp.int32, (half, wide), 0)
    lane = lax.broadcasted_iota(jnp.int32, (half, wide), 1)
    slot = row & 3
    k1 = row >> 2
    kz = k1 + slabs * (lane >> 4)
    kx = 2 * me_z + (slot & 1)
    kx = jnp.where(slot >= 2, -kx, kx)
    kx = jnp.where((slot == 2) & (me_z == 0), nx // 2, kx)
    wave_z = jnp.where(kz < nz // 2, kz, kz - nz).astype(F32) * (2.0 * math.pi / nz)
    wave_x = kx.astype(F32) * (2.0 * math.pi / nx)
    flat_sq = wave_z * wave_z + wave_x * wave_x
    fixed[0] = jnp.where(kz == nz // 2, 0.0, wave_z)
    fixed[1] = jnp.where(kx == nx // 2, 0.0, wave_x)
    for h in range(2):
        ky = me_x * (2 * MODES) + h * MODES + (lane & 15)
        wave_y = ky.astype(F32) * (2.0 * math.pi / NY)
        anchor = (kz == 0) & (kx == 0) & (ky == 0)
        inverse = jnp.where(anchor, 0.0, 1.0 / jnp.where(anchor, 1.0, flat_sq + wave_y * wave_y))
        fixed[2 + 2 * h] = wave_y
        if h == 0:
            packed = ky == 0
            other = 1.0 / (flat_sq + math.pi * math.pi)
            fixed[6] = jnp.where(packed, 0.5 * (inverse - other), 0.0)
            inverse = jnp.where(packed, 0.5 * (inverse + other), inverse)
        fixed[3 + 2 * h] = inverse
    fro = lax.broadcasted_iota(jnp.int32, (half, half), 1)
    to = lax.broadcasted_iota(jnp.int32, (half, half), 0)
    to_slot = to & 3
    paired_slot = jnp.where(me_z == 0, jnp.where((to_slot & 1) == 0, to_slot, 4 - to_slot), (to_slot + 2) & 3)
    mirror_row = ((slabs - (to >> 2)) & (slabs - 1)) * KXS + paired_slot
    row_swap[...] = jnp.where(fro == mirror_row, 1.0, 0.0).astype(BF16)
    fro = lax.broadcasted_iota(jnp.int32, (2 * wide, 2 * wide), 0)
    to = lax.broadcasted_iota(jnp.int32, (2 * wide, 2 * wide), 1)
    mirror_lane = (to & wide) + (PLANES - 1 - ((to & (wide - 1)) >> 4)) * MODES
    sign = jnp.where(to < wide, 1.0, -1.0)
    lane_swap[...] = jnp.where((fro == mirror_lane) & ((to & 15) == 0), sign, 0.0).astype(BF16)
    for n in (4, 6, 8, 7, 5):
        loads[n].wait()

    def to_modes(k):
        mixed = table_times(ahead_1, zr[k])
        real, imag = mixed[:half], mixed[half:]
        cos_t, sin_t = twiddle[0], twiddle[1]
        turned = jnp.concatenate([real * cos_t + imag * sin_t, imag * cos_t - real * sin_t], axis=1)
        spec[k] = times_table(turned, ahead_2)

    def from_modes(k, real, imag):
        turned = times_table(jnp.concatenate([real, imag], axis=1), back_2)
        cos_t, sin_t = twiddle[0], twiddle[1]
        real, imag = turned[:, :wide], turned[:, wide:]
        mixed = jnp.concatenate([real * cos_t - imag * sin_t, imag * cos_t + real * sin_t], axis=0)
        zo[k] = table_times(back_1, mixed)

    def mirrored(k):
        high, low = split(spec[k])
        swapped = dot(row_swap[...], high) + dot(row_swap[...], low)
        high, low = split(swapped)
        swapped = dot(high, lane_swap[...]) + dot(low, lane_swap[...])
        parts = []
        for p in range(2):
            tile = swapped[:, p * wide:(p + 1) * wide]
            parts.append(jnp.where(k1 == 0, pltpu.roll(tile, MODES, 1), tile))
        return parts

    for h in range(2):
        for c in range(3):
            k = 3 * h + c
            arrive(xo, zr, k, 1)
            to_modes(k)
            if h == 0:
                pair = mirrored(k)
                for p in range(2):
                    at = slice(p * wide, (p + 1) * wide)
                    spec[k, :, at] = fixed[3] * spec[k, :, at] + fixed[6] * pair[p]
            else:
                for p in range(2):
                    at = slice(p * wide, (p + 1) * wide)
                    spec[k, :, at] = fixed[5] * spec[k, :, at]

        def stream(c, p):
            return spec[3 * h + c, :, p * wide:(p + 1) * wide]

        def curl(c, p):
            if c == 0:
                return fixed[1] * stream(2, p) - fixed[2 + 2 * h] * stream(1, p)
            if c == 1:
                return fixed[2 + 2 * h] * stream(0, p) - fixed[0] * stream(2, p)
            return fixed[0] * stream(1, p) - fixed[1] * stream(0, p)

        for c in range(3):
            from_modes(3 * h + c, -curl(c, 1), curl(c, 0))
            send_gz(zo, xr2, 3 * h + c, 2)
    loads[3].wait()
    loads[1].wait()
    edges = [[], [], []]
    stores = []

    def back_to_x(k):
        arrive(zo, xr2, k, 2)
        xo2[k] = table_times(back_x, xr2[k])
        send_gx(xo2, yr, k, 3)

    def back_to_y(c):
        arrive(xo2, yr, c, 3)
        arrive(xo2, yr, 3 + c, 3)
        for p in range(2):
            for i in range(0, xl, band):
                turned = []
                for q in range(8):
                    at = (q % PENCILS) * part + p * xl + i
                    tile = yr[3 * (q // PENCILS) + c, at:at + band]
                    turned.append(pltpu.roll(tile, MODES * q, 1) if q else tile)
                for z in range(PLANES):
                    picked = turned[0]
                    for q in range(1, 8):
                        picked = jnp.where(spot == (q + z) % 8, turned[q], picked)
                    if z:
                        picked = pltpu.roll(picked, wide - MODES * z, 1)
                    vel[c, z * xl + i:z * xl + i + band, p * wide:(p + 1) * wide] = picked
        vel[c] = times_table(vel[c], back_y)
        for n, (far, z) in enumerate(((1, PLANES - 1), (slabs - 1, 0))):
            copy = pltpu.make_async_remote_copy(
                src_ref=vel.at[c, pl.ds(z * xl, xl)],
                dst_ref=plane_in.at[n, c],
                send_sem=plane_send.at[n, c],
                recv_sem=plane_recv.at[n, c],
                device_id={"gz": lax.rem(me_z + far, slabs)},
                device_id_type=MESH,
            )
            copy.start()
            edges[c].append(copy)
        for n, (far, x) in enumerate(((1, xl - 1), (PENCILS - 1, 0))):
            side[n, c] = jnp.concatenate([vel[c, z * xl + x:z * xl + x + 1, :] for z in range(PLANES)], axis=0)
            copy = pltpu.make_async_remote_copy(
                src_ref=side.at[n, c],
                dst_ref=side_in.at[n, c],
                send_sem=side_send.at[n, c],
                recv_sem=side_recv.at[n, c],
                device_id={"gx": lax.rem(me_x + far, PENCILS)},
                device_id_type=MESH,
            )
            copy.start()
            edges[c].append(copy)
        stores.append(pltpu.make_async_copy(vel.at[c], vel_out.at[c], store_sem.at[0, c]))
        stores[-1].start()

    at_x = lax.broadcasted_iota(jnp.int32, (xl, NY), 0)

    def stretch_inside(c):
        for z in range(PLANES):
            rows = slice(z * xl, (z + 1) * xl)
            here = vel[c, rows]
            along_z = -vel[c, (z - 1) * xl:z * xl] if z > 0 else None
            if z < PLANES - 1:
                above = vel[c, (z + 1) * xl:(z + 2) * xl]
                along_z = above + along_z if z > 0 else above
            right = jnp.where(at_x == xl - 1, 0.0, pltpu.roll(here, xl - 1, 0))
            left = jnp.where(at_x == 0, 0.0, pltpu.roll(here, 1, 0))
            along_y = pltpu.roll(here, NY - 1, 1) - pltpu.roll(here, 1, 1)
            rate = vort[0, rows] * along_z + vort[1, rows] * (right - left) + vort[2, rows] * along_y
            vorticity[c, rows] = vort[c, rows] + 0.125 * rate

    def stretch_edges(c):
        for copy in edges[c]:
            copy.wait_recv()
        for n, (first, sign) in enumerate(((0, -0.125), ((PLANES - 1) * xl, 0.125))):
            rows = slice(first, first + xl)
            vorticity[c, rows] += vort[0, rows] * (sign * plane_in[n, c])
        for n, (first, sign) in enumerate(((0, -0.125), (xl - 1, 0.125))):
            for z in range(PLANES):
                at = z * xl + first
                vorticity[c, at:at + 1, :] += vort[1, at:at + 1, :] * (sign * side_in[n, c, z:z + 1, :])
        stores.append(pltpu.make_async_copy(vorticity.at[c], vorticity_out.at[c], store_sem.at[1, c]))
        stores[-1].start()

    for k in range(CHUNKS - 1):
        back_to_x(k)
    back_to_y(0)
    back_to_x(CHUNKS - 1)
    stretch_inside(0)
    back_to_y(1)
    stretch_edges(0)
    stretch_inside(1)
    back_to_y(2)
    stretch_edges(1)
    stretch_inside(2)
    stretch_edges(2)
    for copy in hops + rims + edges[0] + edges[1] + edges[2]:
        copy.wait_send()
    for k in range(CHUNKS):
        sent(ys, k, 0)
        sent(xo, k, 1)
        sent(zo, k, 2)
        sent(xo2, k, 3)
    for copy in stores:
        copy.wait()


def on_device(strength, offsets, cell_index, migrate_count, ambient):
    slabs = lax.axis_size("gz")
    xl = ambient.shape[2]
    consts = [jnp.asarray(t) for t in tables(slabs)]
    chunk = pltpu.VMEM((CHUNKS, 8 * slabs, PLANES * MODES), F32)
    mesh = pltpu.VMEM((3, PLANES * xl, NY), F32)
    dma = pltpu.SemaphoreType.DMA
    vmem = pl.BlockSpec(memory_space=pltpu.VMEM)
    whole = pl.BlockSpec(memory_space=pl.ANY)
    flat = jax.ShapeDtypeStruct((3, PLANES * xl, NY), F32)
    velocity, vorticity = pl.pallas_call(
        functools.partial(step_kernel, slabs),
        out_shape=(pltpu.VMEM(flat.shape, F32), pltpu.VMEM(flat.shape, F32)),
        in_specs=[pl.BlockSpec(memory_space=pltpu.SMEM), vmem, vmem, vmem, whole] + [whole] * len(consts),
        out_specs=(whole, whole),
        scratch_shapes=[
            pltpu.VMEM((8, LANES), F32),
            pltpu.VMEM((xl, LANES), F32),
            pltpu.VMEM((NY, LANES), BF16),
            pltpu.VMEM((NY, LANES), BF16),
            pltpu.VMEM((24, LANES), F32),
            pltpu.VMEM((4 * xl, 1280), BF16),
            pltpu.VMEM((4 * xl, 1280), BF16),
            pltpu.VMEM((2, 48, NY), F32),
            pltpu.VMEM((2, 48, NY), F32),
            mesh, mesh, mesh,
            pltpu.VMEM((2, 3, xl, NY), F32),
            pltpu.VMEM((2, 3, PLANES, NY), F32),
            pltpu.VMEM((2, 3, PLANES, NY), F32),
            chunk, chunk, chunk, chunk,
            pltpu.VMEM((CHUNKS, 4 * slabs, 2 * PLANES * MODES), F32),
            chunk, chunk, chunk, chunk,
            pltpu.VMEM((7, 4 * slabs, PLANES * MODES), F32),
            pltpu.VMEM((4 * slabs, 4 * slabs), BF16),
            pltpu.VMEM((2 * PLANES * MODES, 2 * PLANES * MODES), BF16),
            *[pltpu.VMEM(t.shape, t.dtype) for t in consts],
            dma((4, CHUNKS)), dma((4, CHUNKS)), dma((4, CHUNKS)),
            dma((6,)), dma((6,)), dma((2,)), dma((2,)),
            dma((2, 3)), dma((2, 3)), dma((2, 3)), dma((2, 3)),
            dma((10,)), dma((2, 3)),
        ],
        compiler_params=pltpu.CompilerParams(
            collective_id=0, has_side_effects=True, vmem_limit_bytes=56 * 1024 * 1024
        ),
    )(migrate_count.reshape(2), strength, offsets, cell_index.reshape(1, PART), ambient.reshape(flat.shape), *consts)
    return velocity.reshape(ambient.shape), vorticity.reshape(ambient.shape)


def solution(mesh):
    placed = (
        P(None, ("gz", "gx")),
        P(None, ("gz", "gx")),
        P(("gz", "gx")),
        P("gz", "gx", None),
        P(None, "gz", "gx", None),
    )
    return jax.shard_map(
        on_device,
        mesh=mesh,
        in_specs=placed,
        out_specs=(P(None, "gz", "gx", None), P(None, "gz", "gx", None)),
        check_vma=False,
    )
```

```python
import functools
import math

import jax
import jax.numpy as jnp
import ml_dtypes
import numpy as np
from jax import lax
from jax.experimental import pallas as pl
from jax.experimental.pallas import tpu as pltpu
from jax.sharding import PartitionSpec as P

MESH = pl.DeviceIdType.MESH
F32 = jnp.float32
BF16 = jnp.bfloat16
PENCILS = 4
PLANES = 8
MODES = 16
KXS = 4
NY = 256
PART = 512
CHUNKS = 6
GROUP = 9
BLOCK = 32
OWN = 640
LANES = 1792
HOPS = ((1, 0, 128, 512), (1, 128, 384, 128), (-1, 0, 128, 1152), (-1, 128, 384, 1280), (2, 0, 128, 0), (-2, 0, 128, 1664))


def halves(table):
    high = table.astype(ml_dtypes.bfloat16)
    low = (table - high.astype(np.float64)).astype(ml_dtypes.bfloat16)
    return np.stack([high, low])


def real_form(angle):
    cosine, sine = np.cos(angle), np.sin(angle)
    return np.stack([np.stack([cosine, sine], -1), np.stack([-sine, cosine], -1)], -2)


def kx_of(slabs):
    base = 2 * np.arange(slabs)
    rows = np.stack([base, base + 1, -base, -base - 1], 1) % (4 * slabs)
    rows[0, 2] = 2 * slabs
    return rows


def tables(slabs):
    nx, nz = 4 * slabs, 8 * slabs
    rows = 8 * slabs
    two_pi = 2.0 * np.pi
    y = np.arange(NY)
    half, pencil, mode = np.meshgrid(np.arange(2), np.arange(PENCILS), np.arange(MODES), indexing="ij")
    ky = (pencil * 2 * MODES + half * MODES + mode).reshape(-1)
    angle = two_pi * (y[:, None] * ky[None, :] % NY) / NY
    sine = np.where(ky[None, :] == 0, (1.0 - 2.0 * (y % 2))[:, None], -np.sin(angle))
    table_y = np.concatenate([np.cos(angle), sine], 1)
    weight = np.where(ky == 0, 1.0, 2.0) / NY
    back_y = table_y.T * np.concatenate([weight, weight])[:, None]
    kx = kx_of(slabs).reshape(-1)
    x = np.arange(nx)
    form = real_form(two_pi * (kx[:, None] * x[None, :] % nx) / nx)
    form = form.reshape(nx, PENCILS, nx // PENCILS, 2, 2).transpose(0, 3, 1, 4, 2)
    table_x = form.reshape(rows, rows)
    k1 = np.arange(slabs)
    form = real_form(two_pi * (k1[:, None] * k1[None, :] % slabs) / slabs)
    table_1 = np.einsum("ksoi,ab->okasbi", form, np.eye(KXS)).reshape(rows, rows)
    k2 = np.arange(PLANES)
    form = real_form(two_pi * (k2[:, None] * k2[None, :] % PLANES) / PLANES)
    table_2 = np.einsum("kpoi,ab->ipaokb", form, np.eye(MODES)).reshape(2 * PLANES * MODES, -1)
    angle = two_pi * (k1[:, None] * k2[None, :]) / nz
    angle = np.repeat(np.repeat(angle, KXS, 0), MODES, 1)
    twiddle = np.stack([np.cos(angle), np.sin(angle)]).astype(np.float32)
    return (
        halves(table_y), halves(back_y), halves(table_x), halves(table_x.T / nx),
        halves(table_1), halves(table_1.T / nz), halves(table_2), halves(table_2.T), twiddle,
    )


def kernel_weight(distance):
    radius = jnp.abs(distance)
    near_part = 1.0 + radius * radius * (1.5 * radius - 2.5)
    beyond = 2.0 - radius
    far_part = 0.5 * beyond * beyond * (1.0 - radius)
    return jnp.where(radius < 1.0, near_part, jnp.where(radius < 2.0, far_part, 0.0))


def split(values):
    if values.shape[0] > BLOCK:
        pairs = [split(values[i:i + BLOCK]) for i in range(0, values.shape[0], BLOCK)]
        return jnp.concatenate([a for a, _ in pairs], axis=0), jnp.concatenate([b for _, b in pairs], axis=0)
    high = values.astype(BF16)
    return high, (values - high.astype(F32)).astype(BF16)


def dot(a, b):
    return jnp.dot(a, b, preferred_element_type=F32)


def table_times(table, values):
    high, low = split(values)
    width = values.shape[1]
    both = dot(table[0], jnp.concatenate([high, low], axis=1))
    return both[:, :width] + (both[:, width:] + dot(table[1], high))


def times_table(values, table):
    high, low = split(values)
    return dot(high, table[0]) + (dot(low, table[0]) + dot(high, table[1]))


def step_kernel(
    slabs, counts, strength_in, offsets_in, cells_in, ambient, *refs,
):
    tables_in, (vel_out, vorticity_out) = refs[:9], refs[9:11]
    (
        packet, wide_x, high_y, low_y, charge, high_l, low_l, rim, rim_in, vort, vel, vorticity,
        plane_in, side, side_in, ys, xr, xo, zr, spec, zo, xr2, xo2, yr, fixed, row_swap, lane_swap,
    ) = refs[11:38]
    tables_here = refs[38:47]
    ahead_y, back_y, ahead_x, back_x, ahead_1, back_1, ahead_2, back_2, twiddle = tables_here
    (
        send_sem, recv_sem, own_sem, packet_send, packet_recv, rim_send, rim_recv,
        plane_send, plane_recv, side_send, side_recv, load_sem, store_sem, strength, offsets, cells,
    ) = refs[47:]
    me_z, me_x = lax.axis_index("gz"), lax.axis_index("gx")
    nx, nz = 4 * slabs, 8 * slabs
    xl = nx // PENCILS
    half = 4 * slabs
    part = 2 * xl
    wide = PLANES * MODES

    barrier = pltpu.get_barrier_semaphore()

    def each_other_slab(act):
        group = math.gcd(slabs - 1, GROUP)

        def some(i, carry):
            for j in range(group):
                act(lax.rem(me_z + 1 + j + i * group, slabs))
            return carry

        lax.fori_loop(0, (slabs - 1) // group, some, 0)

    def greet(other):
        pl.semaphore_signal(barrier, inc=1, device_id={"gz": other}, device_id_type=MESH)

    small = [
        pltpu.make_async_copy(a, b, load_sem.at[10 + n])
        for n, (a, b) in enumerate(((strength_in, strength), (offsets_in, offsets), (cells_in, cells)))
    ]
    for copy in small:
        copy.start()
    each_other_slab(greet)
    for i in range(1, PENCILS):
        pl.semaphore_signal(barrier, inc=1, device_id={"gx": lax.rem(me_x + i, PENCILS)}, device_id_type=MESH)
    load_mesh = pltpu.make_async_copy(ambient, vort, load_sem.at[9])
    loads = [pltpu.make_async_copy(a, b, load_sem.at[n]) for n, (a, b) in enumerate(zip(tables_in, tables_here))]

    lane_id = lax.broadcasted_iota(jnp.int32, (1, PART), 1)
    up, down = counts[0], counts[1]
    moves = jnp.where(lane_id < up, 1, jnp.where(lane_id < up + down, -1, 0))
    for copy in small:
        copy.wait()
    cell = cells[...]
    packet[:, OWN:OWN + PART] = jnp.concatenate(
        [
            strength[...],
            offsets[...],
            (cell // (xl * NY) + PLANES * moves).astype(F32),
            (cell % (xl * NY)).astype(F32),
        ],
        axis=0,
    )

    def weigh(lo, hi):
        size = hi - lo
        fields = packet[:, lo:hi]
        lane = lax.broadcasted_iota(jnp.int32, (1, size), 1) + lo
        shift = jnp.where(lane < 128, -16.0, jnp.where(lane < OWN, -8.0, jnp.where(lane < OWN + PART, 0.0, jnp.where(lane < LANES - 128, 8.0, 16.0))))
        lateral = fields[7:8].astype(jnp.int32)
        plane = lax.broadcasted_iota(jnp.int32, (PLANES, size), 0).astype(F32)
        weight_z = kernel_weight((plane - (fields[6:7] + shift)) - fields[3:4])
        x_cell = (lateral >> 8).astype(F32)
        block = min(xl, BLOCK)
        for i in range(0, xl, block):
            row = (lax.broadcasted_iota(jnp.int32, (block, size), 0) + i).astype(F32)
            wide_x[i:i + block, lo:hi] = kernel_weight((row - x_cell) - fields[4:5])
        start = NY // 2 - (lateral & 255)
        for i in range(0, NY, 16):
            at_y = lax.broadcasted_iota(jnp.int32, (16, size), 0) + i
            away = ((at_y + start) & 255) - NY // 2
            high, low = split(kernel_weight(away.astype(F32) - fields[5:6]))
            high_y[i:i + 16, lo:hi] = high
            low_y[i:i + 16, lo:hi] = low
        for c in range(3):
            charge[8 * c:8 * c + 8, lo:hi] = fields[c:c + 1] * weight_z

    pl.semaphore_wait(barrier, slabs - 1 + PENCILS - 1)

    hops = []
    for n, (far, start, width, land) in enumerate(HOPS):
        hop = pltpu.make_async_remote_copy(
            src_ref=packet.at[:, OWN + start:OWN + start + width],
            dst_ref=packet.at[:, land:land + width],
            send_sem=packet_send.at[n],
            recv_sem=packet_recv.at[n],
            device_id={"gz": lax.rem(me_z + far + slabs, slabs)},
            device_id_type=MESH,
        )
        hop.start()
        hops.append(hop)

    def send_gx(src, dst, k, stage):
        mine = pl.ds(pl.multiple_of(me_x * part, 8), part)
        for i in (2, 1, 3):
            other = lax.rem(me_x + i, PENCILS)
            pltpu.make_async_remote_copy(
                src_ref=src.at[k, pl.ds(pl.multiple_of(other * part, 8), part)],
                dst_ref=dst.at[k, mine],
                send_sem=send_sem.at[stage, k],
                recv_sem=recv_sem.at[stage, k],
                device_id={"gx": other},
                device_id_type=MESH,
            ).start()
        own_copy(src, dst, k, stage).start()

    def send_gz(src, dst, k, stage):
        mine = pl.ds(pl.multiple_of(me_z * 8, 8), 8)

        def one(other):
            pltpu.make_async_remote_copy(
                src_ref=src.at[k, pl.ds(pl.multiple_of(other * 8, 8), 8)],
                dst_ref=dst.at[k, mine],
                send_sem=send_sem.at[stage, k],
                recv_sem=recv_sem.at[stage, k],
                device_id={"gz": other},
                device_id_type=MESH,
            ).start()

        each_other_slab(one)
        own_copy(src, dst, k, stage).start()

    def own_copy(src, dst, k, stage):
        width, index = (part, me_x) if stage in (0, 3) else (8, me_z)
        at = pl.ds(pl.multiple_of(index * width, 8), width)
        return pltpu.make_async_copy(src.at[k, at], dst.at[k, at], own_sem.at[stage, k])

    def remote_rows(stage):
        return part * (PENCILS - 1) if stage in (0, 3) else 8 * (slabs - 1)

    def arrive(src, dst, k, stage):
        window = dst.at[k, pl.ds(0, remote_rows(stage))]
        pltpu.make_async_copy(window, window, recv_sem.at[stage, k]).wait()
        own_copy(src, dst, k, stage).wait()

    def sent(src, k, stage):
        window = src.at[k, pl.ds(0, remote_rows(stage))]
        pltpu.make_async_copy(window, window, send_sem.at[stage, k]).wait()

    load_mesh.start()
    loads[0].start()
    weigh(OWN, OWN + PART)
    for hop in hops:
        hop.wait_recv()
    weigh(0, OWN)
    weigh(OWN + PART, LANES)

    def spread_over_y(high, low, lo, hi):
        def times(a, b):
            return lax.dot_general(a, b, (((1,), (1,)), ((), ())), preferred_element_type=F32)

        top = high_y[:, lo:hi]
        return times(high, top) + (times(low, top) + times(high, low_y[:, lo:hi]))

    rims = []
    x_cell = (packet[7:8, :].astype(jnp.int32) >> 8).astype(F32)
    for n, first in enumerate((xl, -2)):
        beyond = [kernel_weight((float(first + r) - x_cell) - packet[4:5, :]) for r in range(2)]
        high, low = split(jnp.concatenate([charge[8 * c:8 * c + 8, :] * beyond[r] for c in range(3) for r in range(2)], axis=0))
        rim[n] = spread_over_y(high, low, 0, LANES)
        far = 1 if n == 0 else PENCILS - 1
        copy = pltpu.make_async_remote_copy(
            src_ref=rim.at[n],
            dst_ref=rim_in.at[n],
            send_sem=rim_send.at[n],
            recv_sem=rim_recv.at[n],
            device_id={"gx": lax.rem(me_x + far, PENCILS)},
            device_id_type=MESH,
        )
        copy.start()
        rims.append(copy)
    load_mesh.wait()
    for n in (2, 4, 6, 8, 7, 5, 3, 1):
        loads[n].start()

    def deposit(c):
        for planes, lo, hi in ((range(0, 2), 0, 1280), (range(2, 6), 512, 1280), (range(6, 8), 512, 1792)):
            block = min(xl, 16)
            for i in range(0, xl, block):
                columns = wide_x[i:i + block, lo:hi]
                for n, z in enumerate(planes):
                    high, low = split(columns * charge[8 * c + z:8 * c + z + 1, lo:hi])
                    at = n * xl + i
                    high_l[at:at + block, 0:hi - lo] = high
                    low_l[at:at + block, 0:hi - lo] = low
            size = len(planes) * xl
            at = planes[0] * xl
            vort[c, at:at + size] += spread_over_y(high_l[0:size, 0:hi - lo], low_l[0:size, 0:hi - lo], lo, hi)
        if c == 0:
            for copy in rims:
                copy.wait_recv()
        for n, first in enumerate((0, xl - 2)):
            for r in range(2):
                for z in range(PLANES):
                    at = c * 16 + r * 8 + z
                    to = z * xl + first + r
                    vort[c, to:to + 1, :] += rim_in[n, at:at + 1, :]

    def to_x(k):
        if k == 0:
            loads[2].wait()
        arrive(ys, xr, k, 0)
        xo[k] = table_times(ahead_x, xr[k])
        send_gz(xo, zr, k, 1)

    band = min(xl, 8)
    spot = lax.broadcasted_iota(jnp.int32, (band, wide), 1) >> 4
    for c in range(3):
        deposit(c)
        if c == 0:
            loads[0].wait()
        vel[c] = times_table(vort[c], ahead_y)
        for p in range(2):
            for i in range(0, xl, band):
                turned = []
                for z in range(PLANES):
                    tile = vel[c, z * xl + i:z * xl + i + band, p * wide:(p + 1) * wide]
                    turned.append(pltpu.roll(tile, MODES * z, 1) if z else tile)
                for q in range(8):
                    picked = turned[0]
                    for z in range(1, PLANES):
                        picked = jnp.where(spot == (q + z) % 8, turned[z], picked)
                    if q:
                        picked = pltpu.roll(picked, wide - MODES * q, 1)
                    at = (q % PENCILS) * part + p * xl + i
                    ys[3 * (q // PENCILS) + c, at:at + band] = picked
        send_gx(ys, xr, c, 0)
        if c == 1:
            to_x(0)
    for c in range(3):
        send_gx(ys, xr, 3 + c, 0)
    for k in range(1, CHUNKS):
        to_x(k)
    row = lax.broadcasted_iota(jnp.int32, (half, wide), 0)
    lane = lax.broadcasted_iota(jnp.int32, (half, wide), 1)
    slot = row & 3
    k1 = row >> 2
    kz = k1 + slabs * (lane >> 4)
    kx = 2 * me_z + (slot & 1)
    kx = jnp.where(slot >= 2, -kx, kx)
    kx = jnp.where((slot == 2) & (me_z == 0), nx // 2, kx)
    wave_z = jnp.where(kz < nz // 2, kz, kz - nz).astype(F32) * (2.0 * math.pi / nz)
    wave_x = kx.astype(F32) * (2.0 * math.pi / nx)
    flat_sq = wave_z * wave_z + wave_x * wave_x
    fixed[0] = jnp.where(kz == nz // 2, 0.0, wave_z)
    fixed[1] = jnp.where(kx == nx // 2, 0.0, wave_x)
    for h in range(2):
        ky = me_x * (2 * MODES) + h * MODES + (lane & 15)
        wave_y = ky.astype(F32) * (2.0 * math.pi / NY)
        anchor = (kz == 0) & (kx == 0) & (ky == 0)
        inverse = jnp.where(anchor, 0.0, 1.0 / jnp.where(anchor, 1.0, flat_sq + wave_y * wave_y))
        fixed[2 + 2 * h] = wave_y
        if h == 0:
            packed = ky == 0
            other = 1.0 / (flat_sq + math.pi * math.pi)
            fixed[6] = jnp.where(packed, 0.5 * (inverse - other), 0.0)
            inverse = jnp.where(packed, 0.5 * (inverse + other), inverse)
        fixed[3 + 2 * h] = inverse
    fro = lax.broadcasted_iota(jnp.int32, (half, half), 1)
    to = lax.broadcasted_iota(jnp.int32, (half, half), 0)
    to_slot = to & 3
    paired_slot = jnp.where(me_z == 0, jnp.where((to_slot & 1) == 0, to_slot, 4 - to_slot), (to_slot + 2) & 3)
    mirror_row = ((slabs - (to >> 2)) & (slabs - 1)) * KXS + paired_slot
    row_swap[...] = jnp.where(fro == mirror_row, 1.0, 0.0).astype(BF16)
    fro = lax.broadcasted_iota(jnp.int32, (2 * wide, 2 * wide), 0)
    to = lax.broadcasted_iota(jnp.int32, (2 * wide, 2 * wide), 1)
    mirror_lane = (to & wide) + (PLANES - 1 - ((to & (wide - 1)) >> 4)) * MODES
    sign = jnp.where(to < wide, 1.0, -1.0)
    lane_swap[...] = jnp.where((fro == mirror_lane) & ((to & 15) == 0), sign, 0.0).astype(BF16)
    for n in (4, 6, 8, 7, 5):
        loads[n].wait()

    def to_modes(k):
        mixed = table_times(ahead_1, zr[k])
        real, imag = mixed[:half], mixed[half:]
        cos_t, sin_t = twiddle[0], twiddle[1]
        turned = jnp.concatenate([real * cos_t + imag * sin_t, imag * cos_t - real * sin_t], axis=1)
        spec[k] = times_table(turned, ahead_2)

    def from_modes(k, real, imag):
        turned = times_table(jnp.concatenate([real, imag], axis=1), back_2)
        cos_t, sin_t = twiddle[0], twiddle[1]
        real, imag = turned[:, :wide], turned[:, wide:]
        mixed = jnp.concatenate([real * cos_t - imag * sin_t, imag * cos_t + real * sin_t], axis=0)
        zo[k] = table_times(back_1, mixed)

    def mirrored(k):
        high, low = split(spec[k])
        swapped = dot(row_swap[...], high) + dot(row_swap[...], low)
        high, low = split(swapped)
        swapped = dot(high, lane_swap[...]) + dot(low, lane_swap[...])
        parts = []
        for p in range(2):
            tile = swapped[:, p * wide:(p + 1) * wide]
            parts.append(jnp.where(k1 == 0, pltpu.roll(tile, MODES, 1), tile))
        return parts

    for h in range(2):
        for c in range(3):
            k = 3 * h + c
            arrive(xo, zr, k, 1)
            to_modes(k)
            if h == 0:
                pair = mirrored(k)
                for p in range(2):
                    at = slice(p * wide, (p + 1) * wide)
                    spec[k, :, at] = fixed[3] * spec[k, :, at] + fixed[6] * pair[p]
            else:
                for p in range(2):
                    at = slice(p * wide, (p + 1) * wide)
                    spec[k, :, at] = fixed[5] * spec[k, :, at]

        def stream(c, p):
            return spec[3 * h + c, :, p * wide:(p + 1) * wide]

        def curl(c, p):
            if c == 0:
                return fixed[1] * stream(2, p) - fixed[2 + 2 * h] * stream(1, p)
            if c == 1:
                return fixed[2 + 2 * h] * stream(0, p) - fixed[0] * stream(2, p)
            return fixed[0] * stream(1, p) - fixed[1] * stream(0, p)

        for c in range(3):
            from_modes(3 * h + c, -curl(c, 1), curl(c, 0))
            send_gz(zo, xr2, 3 * h + c, 2)
    loads[3].wait()
    loads[1].wait()
    edges = [[], [], []]
    stores = []

    def back_to_x(k):
        arrive(zo, xr2, k, 2)
        xo2[k] = table_times(back_x, xr2[k])
        send_gx(xo2, yr, k, 3)

    def back_to_y(c):
        arrive(xo2, yr, c, 3)
        arrive(xo2, yr, 3 + c, 3)
        for p in range(2):
            for i in range(0, xl, band):
                turned = []
                for q in range(8):
                    at = (q % PENCILS) * part + p * xl + i
                    tile = yr[3 * (q // PENCILS) + c, at:at + band]
                    turned.append(pltpu.roll(tile, MODES * q, 1) if q else tile)
                for z in range(PLANES):
                    picked = turned[0]
                    for q in range(1, 8):
                        picked = jnp.where(spot == (q + z) % 8, turned[q], picked)
                    if z:
                        picked = pltpu.roll(picked, wide - MODES * z, 1)
                    vel[c, z * xl + i:z * xl + i + band, p * wide:(p + 1) * wide] = picked
        vel[c] = times_table(vel[c], back_y)
        for n, (far, z) in enumerate(((1, PLANES - 1), (slabs - 1, 0))):
            copy = pltpu.make_async_remote_copy(
                src_ref=vel.at[c, pl.ds(z * xl, xl)],
                dst_ref=plane_in.at[n, c],
                send_sem=plane_send.at[n, c],
                recv_sem=plane_recv.at[n, c],
                device_id={"gz": lax.rem(me_z + far, slabs)},
                device_id_type=MESH,
            )
            copy.start()
            edges[c].append(copy)
        for n, (far, x) in enumerate(((1, xl - 1), (PENCILS - 1, 0))):
            side[n, c] = jnp.concatenate([vel[c, z * xl + x:z * xl + x + 1, :] for z in range(PLANES)], axis=0)
            copy = pltpu.make_async_remote_copy(
                src_ref=side.at[n, c],
                dst_ref=side_in.at[n, c],
                send_sem=side_send.at[n, c],
                recv_sem=side_recv.at[n, c],
                device_id={"gx": lax.rem(me_x + far, PENCILS)},
                device_id_type=MESH,
            )
            copy.start()
            edges[c].append(copy)
        stores.append(pltpu.make_async_copy(vel.at[c], vel_out.at[c], store_sem.at[0, c]))
        stores[-1].start()

    at_x = lax.broadcasted_iota(jnp.int32, (xl, NY), 0)

    def stretch_inside(c):
        for z in range(PLANES):
            rows = slice(z * xl, (z + 1) * xl)
            here = vel[c, rows]
            along_z = -vel[c, (z - 1) * xl:z * xl] if z > 0 else None
            if z < PLANES - 1:
                above = vel[c, (z + 1) * xl:(z + 2) * xl]
                along_z = above + along_z if z > 0 else above
            right = jnp.where(at_x == xl - 1, 0.0, pltpu.roll(here, xl - 1, 0))
            left = jnp.where(at_x == 0, 0.0, pltpu.roll(here, 1, 0))
            along_y = pltpu.roll(here, NY - 1, 1) - pltpu.roll(here, 1, 1)
            rate = vort[0, rows] * along_z + vort[1, rows] * (right - left) + vort[2, rows] * along_y
            vorticity[c, rows] = vort[c, rows] + 0.125 * rate

    def stretch_edges(c):
        for copy in edges[c]:
            copy.wait_recv()
        for n, (first, sign) in enumerate(((0, -0.125), ((PLANES - 1) * xl, 0.125))):
            rows = slice(first, first + xl)
            vorticity[c, rows] += vort[0, rows] * (sign * plane_in[n, c])
        for n, (first, sign) in enumerate(((0, -0.125), (xl - 1, 0.125))):
            for z in range(PLANES):
                at = z * xl + first
                vorticity[c, at:at + 1, :] += vort[1, at:at + 1, :] * (sign * side_in[n, c, z:z + 1, :])
        stores.append(pltpu.make_async_copy(vorticity.at[c], vorticity_out.at[c], store_sem.at[1, c]))
        stores[-1].start()

    for k in range(CHUNKS - 1):
        back_to_x(k)
    back_to_y(0)
    back_to_x(CHUNKS - 1)
    stretch_inside(0)
    back_to_y(1)
    stretch_edges(0)
    stretch_inside(1)
    back_to_y(2)
    stretch_edges(1)
    stretch_inside(2)
    stretch_edges(2)
    for copy in hops + rims + edges[0] + edges[1] + edges[2]:
        copy.wait_send()
    for k in range(CHUNKS):
        sent(ys, k, 0)
        sent(xo, k, 1)
        sent(zo, k, 2)
        sent(xo2, k, 3)
    for copy in stores:
        copy.wait()


def on_device(strength, offsets, cell_index, migrate_count, ambient):
    slabs = lax.axis_size("gz")
    xl = ambient.shape[2]
    consts = [jnp.asarray(t) for t in tables(slabs)]
    chunk = pltpu.VMEM((CHUNKS, 8 * slabs, PLANES * MODES), F32)
    mesh = pltpu.VMEM((3, PLANES * xl, NY), F32)
    dma = pltpu.SemaphoreType.DMA
    whole = pl.BlockSpec(memory_space=pl.ANY)
    flat = jax.ShapeDtypeStruct((3, PLANES * xl, NY), F32)
    velocity, vorticity = pl.pallas_call(
        functools.partial(step_kernel, slabs),
        out_shape=(pltpu.VMEM(flat.shape, F32), pltpu.VMEM(flat.shape, F32)),
        in_specs=[pl.BlockSpec(memory_space=pltpu.SMEM), whole, whole, whole, whole] + [whole] * len(consts),
        out_specs=(whole, whole),
        scratch_shapes=[
            pltpu.VMEM((8, LANES), F32),
            pltpu.VMEM((xl, LANES), F32),
            pltpu.VMEM((NY, LANES), BF16),
            pltpu.VMEM((NY, LANES), BF16),
            pltpu.VMEM((24, LANES), F32),
            pltpu.VMEM((4 * xl, 1280), BF16),
            pltpu.VMEM((4 * xl, 1280), BF16),
            pltpu.VMEM((2, 48, NY), F32),
            pltpu.VMEM((2, 48, NY), F32),
            mesh, mesh, mesh,
            pltpu.VMEM((2, 3, xl, NY), F32),
            pltpu.VMEM((2, 3, PLANES, NY), F32),
            pltpu.VMEM((2, 3, PLANES, NY), F32),
            chunk, chunk, chunk, chunk,
            pltpu.VMEM((CHUNKS, 4 * slabs, 2 * PLANES * MODES), F32),
            chunk, chunk, chunk, chunk,
            pltpu.VMEM((7, 4 * slabs, PLANES * MODES), F32),
            pltpu.VMEM((4 * slabs, 4 * slabs), BF16),
            pltpu.VMEM((2 * PLANES * MODES, 2 * PLANES * MODES), BF16),
            *[pltpu.VMEM(t.shape, t.dtype) for t in consts],
            dma((4, CHUNKS)), dma((4, CHUNKS)), dma((4, CHUNKS)),
            dma((6,)), dma((6,)), dma((2,)), dma((2,)),
            dma((2, 3)), dma((2, 3)), dma((2, 3)), dma((2, 3)),
            dma((13,)), dma((2, 3)),
            pltpu.VMEM((3, PART), F32), pltpu.VMEM((3, PART), F32), pltpu.VMEM((1, PART), jnp.int32),
        ],
        compiler_params=pltpu.CompilerParams(
            collective_id=0, has_side_effects=True, vmem_limit_bytes=56 * 1024 * 1024
        ),
    )(migrate_count.reshape(2), strength, offsets, cell_index.reshape(1, PART), ambient.reshape(flat.shape), *consts)
    return velocity.reshape(ambient.shape), vorticity.reshape(ambient.shape)


def solution(mesh):
    placed = (
        P(None, ("gz", "gx")),
        P(None, ("gz", "gx")),
        P(("gz", "gx")),
        P("gz", "gx", None),
        P(None, "gz", "gx", None),
    )
    return jax.shard_map(
        on_device,
        mesh=mesh,
        in_specs=placed,
        out_specs=(P(None, "gz", "gx", None), P(None, "gz", "gx", None)),
        check_vma=False,
    )
```
